32 devices in a mesh: dp: 2 (over x), ctx: 4 (over y, core), tensor: 4 (over z).
Axes of the slice: x: 2, y: 2, z: 4, core: 2. Of those that a mesh axis runs over, the one named last changes fastest.
Arguments:
- hidden_in: bfloat16 [2, 2048, 768], P('dp', 'ctx'), may hold values from -6 to 6
- encoder_out: bfloat16 [2, 2048, 768], P('dp', 'ctx'), may hold values from -6 to 6
- dec_segments: int32 [2, 2048], P('dp'), may hold values from 0 to 7, as said below
- enc_segments: int32 [2, 2048], P('dp'), may hold values from 0 to 7, as said below
- gain_self: bfloat16 [768], replicated, may hold values from 0.5 to 1.5
- gain_cross: bfloat16 [768], replicated, may hold values from 0.5 to 1.5
- gain_feed: bfloat16 [768], replicated, may hold values from 0.5 to 1.5
- self_query: bfloat16 [768, 768], P(None, 'tensor'), may hold values from -0.02734375 to 0.02734375
- self_key: bfloat16 [768, 768], P(None, 'tensor'), may hold values from -0.21875 to 0.21875
- self_value: bfloat16 [768, 768], P(None, 'tensor'), may hold values from -0.21875 to 0.21875
- self_output: bfloat16 [768, 768], P('tensor'), may hold values from -0.75 to 0.75
- bias_table: bfloat16 [32, 12], P(None, 'tensor'), may hold values from -4 to 4
- cross_query: bfloat16 [768, 768], P(None, 'tensor'), may hold values from -0.02734375 to 0.02734375
- cross_key: bfloat16 [768, 768], P(None, 'tensor'), may hold values from -0.21875 to 0.21875
- cross_value: bfloat16 [768, 768], P(None, 'tensor'), may hold values from -0.21875 to 0.21875
- cross_output: bfloat16 [768, 768], P('tensor'), may hold values from -0.75 to 0.75
- hidden_up: bfloat16 [768, 3072], P(None, 'tensor'), may hold values from -0.21875 to 0.21875
- hidden_down: bfloat16 [3072, 768], P('tensor'), may hold values from -0.109375 to 0.109375
- out_grad: bfloat16 [2, 2048, 768], P('dp', 'ctx'), may hold values from -6 to 6
Outputs:
- layer_out: bfloat16 [2, 2048, 768], P('dp', 'ctx')
- grad_hidden: bfloat16 [2, 2048, 768], P('dp', 'ctx')
- grad_encoder: bfloat16 [2, 2048, 768], P('dp', 'ctx')
- grad_gain_self: float32 [768], replicated
- grad_gain_cross: float32 [768], replicated
- grad_gain_feed: float32 [768], replicated
- grad_self_query: float32 [768, 768], P(None, 'tensor')
- grad_self_key: float32 [768, 768], P(None, 'tensor')
- grad_self_value: float32 [768, 768], P(None, 'tensor')
- grad_self_output: float32 [768, 768], P('tensor')
- grad_bias_table: float32 [32, 12], P(None, 'tensor')
- grad_cross_query: float32 [768, 768], P(None, 'tensor')
- grad_cross_key: float32 [768, 768], P(None, 'tensor')
- grad_cross_value: float32 [768, 768], P(None, 'tensor')
- grad_cross_output: float32 [768, 768], P('tensor')
- grad_hidden_up: float32 [768, 3072], P(None, 'tensor')
- grad_hidden_down: float32 [3072, 768], P('tensor')
The draws below stay inside these ranges and needn't reach their ends.
Inputs may be any that keep to these rules, and one draw needn't show every extreme that they name: `dec_segments`: in each row the document numbers never fall and each of 0 to 7 appears. `enc_segments`: in each row the document numbers never fall and each of 0 to 7 appears; decoder document d of a row reads encoder document d of the same row.
All inputs are finite; a program needn't handle non-finite values.
Results may differ from the reference program's by a relative error of at most 0.023.
Values may be sent and summed in bfloat16 or wider, within the bound.
No kernel may reach another device: no remote copies, remote signals or barrier semaphores. Data moves between devices by JAX's collectives and lax.ppermute only.
A program may use at most 192 MiB of HBM per device.

```python
import math
import jax
import jax.numpy as jnp
from jax import lax

D = 768
H = 12
DH = 64
FF = 3072
BUCKETS = 32
MAXDIST = 128
TOK_DEV = 512
DOCS = 8
SEQS = 2
SEQ_LEN = 2048


def segment_row(row_key, variant):
    long_index = jax.random.randint(jax.random.fold_in(row_key, 7), (), 0, DOCS)
    others = jax.random.randint(jax.random.fold_in(row_key, variant), (DOCS,), 1, (TOK_DEV - 1) // (DOCS - 1) + 1)
    is_long = jnp.arange(DOCS) == long_index
    others = jnp.where(is_long, 0, others)
    lengths = jnp.where(is_long, SEQ_LEN - jnp.sum(others), others)
    starts = jnp.cumsum(lengths) - lengths
    places = jnp.arange(SEQ_LEN, dtype=jnp.int32)
    return jnp.sum((places[:, None] >= starts[None, 1:]).astype(jnp.int32), axis=1).astype(jnp.int32)


def segment_rows(key, variant):
    row_keys = jax.vmap(lambda row_number: jax.random.fold_in(key, row_number))(jnp.arange(SEQS))
    return jax.vmap(lambda row_key: segment_row(row_key, variant))(row_keys)


def draw_dec_segments(key, part):
    return segment_rows(key, 1)


def draw_enc_segments(key, part):
    return segment_rows(key, 2)


def levels(key, shape, cuts, smallest, top_value):
    factor_of = 1.0
    for dim, parts in cuts:
        draws = jax.random.uniform(jax.random.fold_in(jax.random.fold_in(key, 6), dim), (parts,), jnp.float32, smallest / len(cuts), top_value / len(cuts))
        factor_of = factor_of * jnp.repeat(jnp.exp(draws), shape[dim] // parts).reshape((-1,) + (1,) * (len(shape) - 1 - dim))
    return factor_of


def normal_values(own_key, extent, scale, bound, cuts=(), kind=jnp.bfloat16):
    values = scale * jax.random.normal(own_key, extent, jnp.float32)
    if cuts:
        values = values * levels(own_key, extent, cuts, -0.22, 0.18)
    return jnp.clip(values, -bound, bound).astype(kind)


def setup_inputs(seed: int = 0) -> dict:
    streams_of = jax.random.split(jax.random.key(seed), 20)
    return {
        "hidden_in": normal_values(streams_of[0], (SEQS, SEQ_LEN, D), 1.0, 6.0, ((0, 2), (1, 4))),
        "encoder_out": normal_values(streams_of[1], (SEQS, SEQ_LEN, D), 1.0, 6.0, ((0, 2), (1, 4))),
        "dec_segments": draw_dec_segments(jax.random.fold_in(streams_of[19], 71), 0),
        "enc_segments": draw_enc_segments(jax.random.fold_in(streams_of[19], 71), 0),
        "gain_self": jnp.clip(1.0 + 0.1 * jax.random.normal(streams_of[4], (D,), jnp.float32), 0.5, 1.5).astype(jnp.bfloat16),
        "gain_cross": jnp.clip(1.0 + 0.1 * jax.random.normal(streams_of[5], (D,), jnp.float32), 0.5, 1.5).astype(jnp.bfloat16),
        "gain_feed": jnp.clip(1.0 + 0.1 * jax.random.normal(streams_of[6], (D,), jnp.float32), 0.5, 1.5).astype(jnp.bfloat16),
        "self_query": normal_values(streams_of[7], (D, H * DH), (D * DH) ** -0.5, 0.02734375, ((1, 4),)),
        "self_key": normal_values(streams_of[8], (D, H * DH), D ** -0.5, 0.21875, ((1, 4),)),
        "self_value": normal_values(streams_of[9], (D, H * DH), D ** -0.5, 0.21875, ((1, 4),)),
        "self_output": normal_values(streams_of[10], (H * DH, D), DH ** -0.5, 0.75, ((0, 4),)),
        "bias_table": normal_values(streams_of[11], (BUCKETS, H), 1.0, 4.0, ((1, 4),)),
        "cross_query": normal_values(streams_of[12], (D, H * DH), (D * DH) ** -0.5, 0.02734375, ((1, 4),)),
        "cross_key": normal_values(streams_of[13], (D, H * DH), D ** -0.5, 0.21875, ((1, 4),)),
        "cross_value": normal_values(streams_of[14], (D, H * DH), D ** -0.5, 0.21875, ((1, 4),)),
        "cross_output": normal_values(streams_of[15], (H * DH, D), DH ** -0.5, 0.75, ((0, 4),)),
        "hidden_up": normal_values(streams_of[16], (D, FF), D ** -0.5, 0.21875, ((1, 4),)),
        "hidden_down": normal_values(streams_of[17], (FF, D), FF ** -0.5, 0.109375, ((0, 4),)),
        "out_grad": normal_values(streams_of[18], (SEQS, SEQ_LEN, D), 1.0, 6.0, ((0, 2), (1, 4))),
    }


@jax.custom_vjp
def low(v):
    return lax.optimization_barrier(v.astype(jnp.bfloat16)).astype(jnp.float32)

@jax.custom_vjp
def low_back(v):
    return v

def low_keep(v):
    return (low(v), None)

def low_pass(kept, grad):
    return (grad,)

def back_keep(v):
    return (v, None)

def back_low(kept, grad):
    return (low(grad),)
low.defvjp(low_keep, low_pass)
low_back.defvjp(back_keep, back_low)
EPSILON = 1e-06
MASKED = -1000000000.0
HIGHEST = lax.Precision.HIGHEST
CURVE_SCALE = math.sqrt(2.0 / math.pi)
CUBIC_TERM = 0.044715

def smooth_gate(values):
    return 0.5 * values * (1.0 + jnp.tanh(CURVE_SCALE * (values + CUBIC_TERM * values * values * values)))

def position_bucket(distance):
    exact_cut = BUCKETS // 2
    if distance < exact_cut:
        return distance
    scaled = math.log(distance / exact_cut) / math.log(MAXDIST / exact_cut) * (BUCKETS - exact_cut)
    return min(exact_cut + int(scaled), BUCKETS - 1)

def bucket_bounds():
    thresholds = []
    for target in range(1, BUCKETS):
        distance = 0
        while position_bucket(distance) < target:
            distance = distance + 1
        thresholds.append(distance)
    return thresholds

def bucket_of(distance):
    buckets = jnp.zeros(distance.shape, jnp.int32)
    for threshold in bucket_bounds():
        buckets = buckets + (distance >= threshold).astype(jnp.int32)
    return buckets

def rms_scale(values, gain):
    return values * lax.rsqrt(lax.optimization_barrier(jnp.mean(values * values, axis=-1, keepdims=True)) + EPSILON) * gain

def matmul(left, right):
    return jnp.dot(left, right, precision=HIGHEST)

def both_ways(v):
    return low_back(low(v))

def attend(queries, key_rows, values, allowed, position_bias):
    query_heads = queries.reshape(queries.shape[0], H, DH)
    key_heads = key_rows.reshape(key_rows.shape[0], H, DH)
    value_heads = values.reshape(values.shape[0], H, DH)
    scores = low_back(jnp.einsum('qhd,khd->hqk', query_heads, key_heads, precision=HIGHEST) + position_bias)
    scores = jnp.where(allowed[None], scores, MASKED)
    weights = jax.nn.softmax(scores, axis=-1)
    mixed_rows = jnp.einsum('hqk,khd->qhd', low(weights), value_heads, precision=HIGHEST)
    return both_ways(mixed_rows.reshape(queries.shape[0], H * DH))

def forward(tokens, encoded, weights, buckets, self_allowed, cross_allowed):
    gain_self, gain_cross, gain_feed, self_query, self_key, self_value, self_output, bias_table, cross_query, cross_key, cross_value, cross_output, hidden_up, hidden_down = weights
    normed_self = low(rms_scale(tokens, gain_self))
    queries = both_ways(matmul(normed_self, self_query))
    key_rows = both_ways(matmul(normed_self, self_key))
    values = both_ways(matmul(normed_self, self_value))
    position_bias = jnp.transpose(jnp.take(bias_table, buckets, axis=0), (2, 0, 1))
    mixed_self = attend(queries, key_rows, values, self_allowed, position_bias)
    after_self = tokens + low_back(matmul(mixed_self, self_output))
    normed_cross = low(rms_scale(after_self, gain_cross))
    cross_queries = both_ways(matmul(normed_cross, cross_query))
    cross_keys = both_ways(matmul(encoded, cross_key))
    cross_values = both_ways(matmul(encoded, cross_value))
    mixed_cross = attend(cross_queries, cross_keys, cross_values, cross_allowed, 0.0)
    after_cross = after_self + low_back(matmul(mixed_cross, cross_output))
    normed_feed = low(rms_scale(after_cross, gain_feed))
    pre_act = low_back(matmul(normed_feed, hidden_up))
    active = low(smooth_gate(pre_act))
    return after_cross + low_back(matmul(active, hidden_down))

def reference(hidden_in, encoder_out, dec_segments, enc_segments, gain_self, gain_cross, gain_feed, self_query, self_key, self_value, self_output, bias_table, cross_query, cross_key, cross_value, cross_output, hidden_up, hidden_down, out_grad):
    params = tuple((weight.astype(jnp.float32) for weight in (gain_self, gain_cross, gain_feed, self_query, self_key, self_value, self_output, bias_table, cross_query, cross_key, cross_value, cross_output, hidden_up, hidden_down)))
    places = jnp.arange(SEQ_LEN, dtype=jnp.int32)
    distance = places[:, None] - places[None, :]
    buckets = bucket_of(jnp.maximum(distance, 0))
    causal = distance >= 0

    def one_sequence(running, slices):
        tokens, encoded, dec_ids, enc_ids, cotangent = slices
        self_allowed = causal & (dec_ids[:, None] == dec_ids[None, :])
        cross_allowed = dec_ids[:, None] == enc_ids[None, :]

        def apply(token_rows, encoded_rows, *weights):
            return forward(token_rows, encoded_rows, weights, buckets, self_allowed, cross_allowed)
        result, pullback = jax.vjp(apply, tokens.astype(jnp.float32), encoded.astype(jnp.float32), *params)
        gradients = pullback(cotangent.astype(jnp.float32))
        running = tuple((total + update for total, update in zip(running, gradients[2:])))
        return (running, (result.astype(jnp.bfloat16), gradients[0].astype(jnp.bfloat16), gradients[1].astype(jnp.bfloat16)))
    initial = tuple((jnp.zeros_like(weight) for weight in params))
    totals, outputs = lax.scan(one_sequence, initial, (hidden_in, encoder_out, dec_segments, enc_segments, out_grad))
    return (outputs[0], outputs[1], outputs[2], totals[0], totals[1], totals[2], totals[3], totals[4], totals[5], totals[6], totals[7], totals[8], totals[9], totals[10], totals[11], totals[12], totals[13])
```

```python
import math
import functools
import numpy as np
import jax
import jax.numpy as jnp
from jax import lax
from jax.sharding import PartitionSpec as P
from jax.experimental import pallas as pl
from jax.experimental.pallas import tpu as pltpu

BUCKETS = 32
MAXDIST = 128
DOCS = 8
EPSILON = 1e-06
MASKED = -1000000000.0
MASK_WEIGHT = -float(2**30)
CURVE_SCALE = math.sqrt(2.0 / math.pi)
CUBIC_TERM = 0.044715
HIGHEST = lax.Precision.HIGHEST

HEAD = 64
KEYS = 256
WIDE = 256
SPAN = 1280
VMEM_BYTES = 60 * 1024 * 1024


def position_bucket(distance):
    exact_cut = BUCKETS // 2
    if distance < exact_cut:
        return distance
    scaled = math.log(distance / exact_cut) / math.log(MAXDIST / exact_cut) * (BUCKETS - exact_cut)
    return min(exact_cut + int(scaled), BUCKETS - 1)


def span_onehot():
    table = np.zeros((SPAN, BUCKETS), np.float32)
    for place in range(KEYS, KEYS + 3 * KEYS):
        table[place, position_bucket(place - KEYS)] = 1.0
    return table


def dot_nt(left, right):
    return lax.dot_general(left, right, (((1,), (1,)), ((), ())), preferred_element_type=jnp.float32)


def dot_nn(left, right):
    return lax.dot_general(left, right, (((1,), (0,)), ((), ())), preferred_element_type=jnp.float32)


def onehot_rows(count, first, meta, base):
    lane = lax.broadcasted_iota(jnp.int32, (1, HEAD), 1)
    low = jnp.zeros((1, HEAD), jnp.int32)
    high = jnp.zeros((1, HEAD), jnp.int32)
    for d in range(DOCS):
        low = jnp.where(lane == d, meta[base + d], low)
        high = jnp.where(lane == d, meta[base + d + 1], high)
    place = lax.broadcasted_iota(jnp.int32, (count, HEAD), 0) + first
    return (place >= low) & (place < high)


def head_mask(width, first, head, feature_from):
    lane = lax.broadcasted_iota(jnp.int32, (1, width), 1)
    start = first + head * HEAD
    keep = (lane >= start) & (lane < start + HEAD)
    if feature_from is not None:
        keep = keep | (lane >= feature_from)
    return keep.astype(jnp.float32).astype(jnp.bfloat16)


def gather_blocks(meta, parts, kvs, kext, key_base):
    rows = parts[0].shape[0]
    me = meta[1]
    inner = kext.shape[1] - HEAD
    for r, part in enumerate(parts):
        at = pl.multiple_of(jnp.bitwise_xor(me, r) * rows, rows)
        kvs[pl.ds(at, rows), :] = part[...]
        kext[pl.ds(at, rows), 0:inner] = part[:, 0:inner]
        kext[pl.ds(at, rows), inner:] = onehot_rows(rows, at, meta, key_base).astype(jnp.float32).astype(jnp.bfloat16)


def query_heads(meta, q_ref, qx, qm, heads, query_base):
    rows, inner = q_ref.shape
    own = onehot_rows(rows, meta[0], meta, query_base)
    qx[:, 0:inner] = q_ref[...]
    qx[:, inner:] = jnp.where(own, 0.0, MASK_WEIGHT).astype(jnp.bfloat16)
    for h in range(heads):
        qm[h] = qx[...] * head_mask(qx.shape[1], 0, h, inner)


def bias_tiles(u_ref, tile, heads):
    for h in range(heads):
        row = jnp.broadcast_to(u_ref[h : h + 1, :], (KEYS, SPAN))
        tile[h] = pltpu.roll(row, 0, 1, stride=1, stride_axis=0)[:, 0 : 4 * KEYS]


def key_range(meta, rows, query_base, key_base):
    first = meta[0]
    last = first + rows - 1
    low = meta[key_base]
    high = meta[key_base + 1]
    for d in range(1, DOCS):
        low = jnp.where(meta[query_base + d] <= first, meta[key_base + d], low)
        high = jnp.where(meta[query_base + d] <= last, meta[key_base + d + 1], high)
    return lax.div(low, KEYS), lax.div(high + KEYS - 1, KEYS)


def for_blocks(meta, rows, causal, query_base, key_base, step):
    low, high = key_range(meta, rows, query_base, key_base)
    if not causal:
        lax.fori_loop(low, high, lambda kb, c: (step(kb, None), c)[1], 0)
        return
    near = lax.div(meta[0], KEYS)
    lax.fori_loop(low, near - 1, lambda kb, c: (step(kb, None), c)[1], 0)

    @pl.when(near > 0)
    def _():
        step(near - 1, 2 * KEYS)

    step(near, KEYS)
    step(near + 1, 0)


def forward_kernel(causal, heads, count, meta, *refs):
    if causal:
        u_ref, q_ref = refs[0], refs[1]
        refs = refs[2:]
    else:
        q_ref = refs[0]
        refs = refs[1:]
    parts, refs = refs[:count], refs[count:]
    out_ref, lse_ref, kvs, kext, vt, qx, qm, ot, top, total = refs[:10]
    query_base = 2
    key_base = 2 if causal else 2 + DOCS + 1
    rows = q_ref.shape[0]
    gather_blocks(meta, parts, kvs, kext, key_base)
    query_heads(meta, q_ref, qx, qm, heads, query_base)
    lanes = kvs.shape[1]
    for kb in range(kvs.shape[0] // KEYS):
        vt[kb] = kvs[kb * KEYS : (kb + 1) * KEYS, lanes - WIDE :].T
    if causal:
        tile = refs[10]
        bias_tiles(u_ref, tile, heads)
    top[...] = jnp.full_like(top, -3e38)
    total[...] = jnp.zeros_like(total)
    ot[...] = jnp.zeros_like(ot)
    shift = WIDE - heads * HEAD

    def step(kb, place):
        kx = kext[pl.ds(pl.multiple_of(kb * KEYS, KEYS), KEYS), :]
        for h in range(heads):
            scores = dot_nt(kx, qm[h])
            far = 0.0
            if place is not None:
                scores = scores + tile[h, :, place : place + rows]
            elif causal:
                far = u_ref[h : h + 1, 4 * KEYS - 1 : 4 * KEYS]
            before = top[h : h + 1, :]
            after = jnp.maximum(before, jnp.max(scores, axis=0, keepdims=True) + far)
            scale = jnp.exp(before - after)
            weights = jnp.exp(scores - (after - far))
            top[h : h + 1, :] = after
            total[h : h + 1, :] = total[h : h + 1, :] * scale + jnp.sum(weights, axis=0, keepdims=True)
            own = vt[kb, shift + h * HEAD : shift + (h + 1) * HEAD, :]
            at = slice(h * HEAD, (h + 1) * HEAD)
            ot[at, :] = ot[at, :] * scale + dot_nn(own, weights.astype(jnp.bfloat16))

    for_blocks(meta, rows, causal, query_base, key_base, step)
    for h in range(heads):
        at = slice(h * HEAD, (h + 1) * HEAD)
        out_ref[at, :] = (ot[at, :] / total[h : h + 1, :]).astype(jnp.bfloat16)
    lse_ref[...] = top[...] + jnp.log(total[...])


def attend(causal, heads, meta, u, queries, parts):
    rows, inner = queries.shape
    part_rows, lanes = parts[0].shape
    count = len(parts)
    length = part_rows * count
    smem = pl.BlockSpec(memory_space=pltpu.SMEM)
    vmem = pl.BlockSpec(memory_space=pltpu.VMEM)
    given = ([u] if causal else []) + [queries] + list(parts)
    scratch = [
        pltpu.VMEM((length, lanes), jnp.bfloat16),
        pltpu.VMEM((length, inner + HEAD), jnp.bfloat16),
        pltpu.VMEM((length // KEYS, WIDE, KEYS), jnp.bfloat16),
        pltpu.VMEM((rows, inner + HEAD), jnp.bfloat16),
        pltpu.VMEM((heads, rows, inner + HEAD), jnp.bfloat16),
        pltpu.VMEM((inner, rows), jnp.float32),
        pltpu.VMEM((8, rows), jnp.float32),
        pltpu.VMEM((8, rows), jnp.float32),
    ]
    if causal:
        scratch.append(pltpu.VMEM((heads, KEYS, 4 * KEYS), jnp.float32))
    return pl.pallas_call(
        functools.partial(forward_kernel, causal, heads, count),
        out_shape=(
            jax.ShapeDtypeStruct((inner, rows), jnp.bfloat16),
            jax.ShapeDtypeStruct((8, rows), jnp.float32),
        ),
        in_specs=[smem] + [vmem] * len(given),
        out_specs=(vmem, vmem),
        scratch_shapes=scratch,
        compiler_params=pltpu.CompilerParams(vmem_limit_bytes=VMEM_BYTES),
        name="self_forward" if causal else "cross_forward",
    )(meta, *given)


def fold_diagonals(values):
    half = values.shape[0] // 2
    while half >= 1:
        values = values[:half] + pltpu.roll(values[half : 2 * half], SPAN - half, 1)
        half = half // 2
    return values


def backward_kernel(causal, heads, count, meta, *refs):
    if causal:
        u_ref = refs[0]
        refs = refs[1:]
    q_ref, do_ref, mixed_ref, lse_ref = refs[:4]
    parts, refs = refs[4 : 4 + count], refs[4 + count :]
    dq_ref = refs[0]
    d_refs, refs = refs[1 : 1 + count], refs[1 + count :]
    if causal:
        dbias_ref = refs[0]
        refs = refs[1:]
    kvs, kext, kt, qx, qm, dom, ra, rb, dqt, row, dkv = refs[:11]
    query_base = 2
    key_base = 2 if causal else 2 + DOCS + 1
    rows, inner = q_ref.shape
    lanes = kvs.shape[1]
    gather_blocks(meta, parts, kvs, kext, key_base)
    query_heads(meta, q_ref, qx, qm, heads, query_base)
    for kb in range(kvs.shape[0] // KEYS):
        kt[kb] = kvs[kb * KEYS : (kb + 1) * KEYS, 0:WIDE].T
    shift = WIDE - inner
    for h in range(heads):
        dom[h] = do_ref[:, lanes - WIDE :] * head_mask(WIDE, shift, h, None)
        ra[h * rows : (h + 1) * rows, :] = q_ext_only(qx, h, inner)
    ra[heads * rows :, :] = do_ref[:, 0:WIDE] * head_mask(WIDE, inner, 0, None)
    for h in range(1, heads):
        rb[(h - 1) * rows : h * rows, :] = do_ref[:, WIDE:] * head_mask(lanes - WIDE, inner - WIDE, h, None)
    turned = do_ref[:, lanes - WIDE :].astype(jnp.float32).T
    inner_sum = turned[shift:, :] * mixed_ref[...].astype(jnp.float32)
    for h in range(heads):
        row[h : h + 1, :] = jnp.sum(inner_sum[h * HEAD : (h + 1) * HEAD, :], axis=0, keepdims=True)
    dqt[...] = jnp.zeros_like(dqt)
    dkv[...] = jnp.zeros_like(dkv)
    if causal:
        tile, dtile, dfar = refs[11:14]
        bias_tiles(u_ref, tile, heads)
        dtile[...] = jnp.zeros_like(dtile)
        dfar[...] = jnp.zeros_like(dfar)

    def step(kb, place):
        at_keys = pl.ds(pl.multiple_of(kb * KEYS, KEYS), KEYS)
        kx = kext[at_keys, :]
        vx = kvs[at_keys, lanes - WIDE :]
        weights_low = []
        grads_low = []
        for h in range(heads):
            scores = dot_nt(kx, qm[h])
            lse = lse_ref[h : h + 1, :]
            if place is not None:
                scores = scores + tile[h, :, place : place + rows]
            elif causal:
                lse = lse - u_ref[h : h + 1, 4 * KEYS - 1 : 4 * KEYS]
            weights = jnp.exp(scores - lse)
            grad_weights = dot_nt(vx, dom[h])
            grads = weights * (grad_weights - row[h : h + 1, :])
            low = grads.astype(jnp.bfloat16)
            weights_low.append(weights.astype(jnp.bfloat16))
            grads_low.append(low)
            if causal:
                if place is not None:
                    dtile[h, :, place : place + rows] += low.astype(jnp.float32)
                else:
                    dfar[h : h + 1, :] += jnp.sum(low.astype(jnp.float32), axis=0, keepdims=True)
            at = slice(h * HEAD, (h + 1) * HEAD)
            dqt[at, :] += dot_nn(kt[kb, at, :], low)
        dkv[at_keys, 0:WIDE] = dot_nn(jnp.concatenate(grads_low + weights_low[:1], axis=1), ra[...]).astype(jnp.bfloat16)
        dkv[at_keys, WIDE:] = dot_nn(jnp.concatenate(weights_low[1:], axis=1), rb[...]).astype(jnp.bfloat16)

    for_blocks(meta, rows, causal, query_base, key_base, step)
    dq_ref[...] = dqt[...].astype(jnp.bfloat16)
    me = meta[1]
    part_rows = parts[0].shape[0]
    for r in range(count):
        at = pl.multiple_of(jnp.bitwise_xor(me, r) * part_rows, part_rows)
        d_refs[r][...] = dkv[pl.ds(at, part_rows), :]
    if causal:
        lane = lax.broadcasted_iota(jnp.int32, (1, SPAN), 1)
        dbias_ref[...] = jnp.zeros_like(dbias_ref)
        for h in range(heads):
            padded = jnp.concatenate([dtile[h], jnp.zeros((KEYS, SPAN - 4 * KEYS), jnp.float32)], axis=1)
            far = jnp.sum(dfar[h : h + 1, :], axis=1, keepdims=True)
            dbias_ref[h : h + 1, :] = fold_diagonals(padded) + jnp.where(lane == 4 * KEYS - 1, far, 0.0)


def q_ext_only(qx, head, inner):
    return qx[...] * head_mask(qx.shape[1], 0, head, None)


def attend_back(causal, heads, meta, u, queries, do_pad, mixed, lse, parts):
    rows, inner = queries.shape
    part_rows, lanes = parts[0].shape
    count = len(parts)
    length = part_rows * count
    smem = pl.BlockSpec(memory_space=pltpu.SMEM)
    vmem = pl.BlockSpec(memory_space=pltpu.VMEM)
    given = ([u] if causal else []) + [queries, do_pad, mixed, lse] + list(parts)
    out_shape = [jax.ShapeDtypeStruct((inner, rows), jnp.bfloat16)]
    out_shape += [jax.ShapeDtypeStruct((part_rows, lanes), jnp.bfloat16)] * count
    if causal:
        out_shape.append(jax.ShapeDtypeStruct((8, SPAN), jnp.float32))
    scratch = [
        pltpu.VMEM((length, lanes), jnp.bfloat16),
        pltpu.VMEM((length, inner + HEAD), jnp.bfloat16),
        pltpu.VMEM((length // KEYS, WIDE, KEYS), jnp.bfloat16),
        pltpu.VMEM((rows, inner + HEAD), jnp.bfloat16),
        pltpu.VMEM((heads, rows, inner + HEAD), jnp.bfloat16),
        pltpu.VMEM((heads, rows, WIDE), jnp.bfloat16),
        pltpu.VMEM(((heads + 1) * rows, WIDE), jnp.bfloat16),
        pltpu.VMEM(((heads - 1) * rows, lanes - WIDE), jnp.bfloat16),
        pltpu.VMEM((inner, rows), jnp.float32),
        pltpu.VMEM((8, rows), jnp.float32),
        pltpu.VMEM((length, lanes), jnp.bfloat16),
    ]
    if causal:
        scratch += [
            pltpu.VMEM((heads, KEYS, 4 * KEYS), jnp.float32),
            pltpu.VMEM((heads, KEYS, 4 * KEYS), jnp.float32),
            pltpu.VMEM((8, rows), jnp.float32),
        ]
    return pl.pallas_call(
        functools.partial(backward_kernel, causal, heads, count),
        out_shape=tuple(out_shape),
        in_specs=[smem] + [vmem] * len(given),
        out_specs=tuple([vmem] * len(out_shape)),
        scratch_shapes=scratch,
        compiler_params=pltpu.CompilerParams(vmem_limit_bytes=VMEM_BYTES),
        name="self_backward" if causal else "cross_backward",
    )(meta, *given)


def position_rows(bias_table, heads):
    table = span_onehot()
    rows = jnp.dot(bias_table.astype(jnp.bfloat16).T, jnp.asarray(table.T, jnp.bfloat16), preferred_element_type=jnp.float32)
    rows = rows + jnp.asarray(np.where(table.sum(1) > 0, 0.0, MASKED)[None, :], jnp.float32)
    return jnp.concatenate([rows, jnp.zeros((8 - heads, SPAN), jnp.float32)], axis=0)


def make_meta(dec_row, enc_row, offset, place):
    docs = jnp.arange(DOCS + 1, dtype=jnp.int32)
    dec = jnp.sum((dec_row[None, :] < docs[:, None]).astype(jnp.int32), axis=1)
    enc = jnp.sum((enc_row[None, :] < docs[:, None]).astype(jnp.int32), axis=1)
    return jnp.concatenate([jnp.stack([offset, place]).astype(jnp.int32), dec, enc])


def smooth_gate(values):
    return (
        0.5
        * values
        * (1.0 + jnp.tanh(CURVE_SCALE * (values + CUBIC_TERM * values * values * values)))
    )


def smooth_slope(values):
    bent = jnp.tanh(CURVE_SCALE * (values + CUBIC_TERM * values * values * values))
    return 0.5 * (1.0 + bent) + 0.5 * values * (1.0 - bent * bent) * CURVE_SCALE * (
        1.0 + 3.0 * CUBIC_TERM * values * values
    )


def norm_forward(values, gain):
    scale = lax.rsqrt(jnp.mean(values * values, axis=-1, keepdims=True) + EPSILON)
    plain = values * scale
    return (plain, scale, (plain * gain).astype(jnp.bfloat16))


def norm_backward(grad_normed, plain, scale, gain):
    grad_plain = grad_normed * gain
    inner = jnp.mean(grad_plain * plain, axis=-1, keepdims=True)
    return scale * (grad_plain - plain * inner)


def product(left, right, left_dim, right_dim):
    return lax.dot_general(
        left, right, (((left_dim,), (right_dim,)), ((), ())), preferred_element_type=jnp.float32
    )


def swap(values, axis, flip):
    count = lax.axis_size(axis)
    return lax.ppermute(values, axis, [(i, i ^ flip) for i in range(count)])


def gather_xor(values, axis):
    count = lax.axis_size(axis)
    held = {0: values}
    bit = count // 2
    while bit >= 1:
        for r in list(held):
            held[r ^ bit] = swap(held[r], axis, bit)
        bit //= 2
    return [held[r] for r in range(count)]


def scatter_xor(blocks, axis):
    count = lax.axis_size(axis)
    held = dict(enumerate(blocks))
    bit = 1
    while bit < count:
        kept = {}
        for r in held:
            if not r & bit:
                kept[r] = held[r].astype(jnp.float32) + swap(
                    held[r ^ bit].astype(jnp.bfloat16), axis, bit
                ).astype(jnp.float32)
        held = kept
        bit *= 2
    return held[0]


def scatter_rows(values, axis):
    count = lax.axis_size(axis)
    me = lax.axis_index(axis)
    rows = values.shape[0] // count
    total = lax.dynamic_slice_in_dim(values, me * rows, rows, 0)
    for flip in range(1, count):
        block = lax.dynamic_slice_in_dim(values, (me ^ flip) * rows, rows, 0)
        total = total + swap(block.astype(jnp.bfloat16), axis, flip).astype(jnp.float32)
    return total


def gather_rows(values, axis):
    return lax.all_gather(values, axis, axis=0, tiled=True)


def body(
    hidden_in,
    encoder_out,
    dec_segments,
    enc_segments,
    gain_self,
    gain_cross,
    gain_feed,
    self_query,
    self_key,
    self_value,
    self_output,
    bias_table,
    cross_query,
    cross_key,
    cross_value,
    cross_output,
    hidden_up,
    hidden_down,
    out_grad,
):
    tok_len, width = hidden_in.shape[1:]
    heads = bias_table.shape[1]
    inner = self_query.shape[1]
    low = jnp.bfloat16
    place = lax.axis_index("ctx")
    slot = lax.axis_index("tensor")
    slots = lax.axis_size("tensor")
    share = tok_len // slots
    meta = make_meta(dec_segments[0], enc_segments[0], place * tok_len, place)
    bias_rows = position_rows(bias_table, heads)
    tokens = hidden_in[0].astype(jnp.float32)
    encoded = encoder_out[0]
    cotangent = out_grad[0]
    gain_one = gain_self.astype(jnp.float32)
    gain_two = gain_cross.astype(jnp.float32)
    gain_three = gain_feed.astype(jnp.float32)

    self_output_all = gather_rows(self_output, "tensor")
    cross_query_all = gather_rows(cross_query.T, "tensor")
    cross_output_all = gather_rows(cross_output, "tensor")
    self_sides = jnp.concatenate([self_key, self_value], axis=1)
    cross_sides = jnp.concatenate([cross_key, cross_value], axis=1)
    pad = jnp.zeros((inner, width), low)

    plain_self, scale_self, normed_self = norm_forward(tokens, gain_one)
    sides = gather_xor(product(normed_self, self_sides, 1, 0).astype(low), "ctx")
    queries = product(normed_self, self_query, 1, 0).astype(low)
    cross_parts = gather_xor(product(encoded, cross_sides, 1, 0).astype(low), "ctx")
    mixed_self, lse_self = attend(True, heads, meta, bias_rows, queries, sides)
    after_self = tokens + product(gather_rows(mixed_self, "tensor"), self_output_all, 0, 0)

    plain_cross, scale_cross, normed_cross = norm_forward(after_self, gain_two)
    cross_queries = product(normed_cross, cross_query, 1, 0).astype(low)
    mixed_cross, lse_cross = attend(False, heads, meta, None, cross_queries, cross_parts)
    after_cross = after_self + product(gather_rows(mixed_cross, "tensor"), cross_output_all, 0, 0)

    plain_feed, scale_feed, normed_feed = norm_forward(after_cross, gain_three)
    pre_act = product(normed_feed, hidden_up, 1, 0)
    grad_pre = (product(cotangent, hidden_down, 1, 1) * smooth_slope(pre_act)).astype(low)
    active = smooth_gate(pre_act).astype(low)
    feed_part = product(grad_pre, hidden_up, 1, 1)
    grad_gain_feed = jnp.sum(feed_part * plain_feed, axis=0)
    feed_rows = scatter_rows(feed_part, "tensor")
    final = after_cross + lax.psum(product(active, hidden_down, 1, 0).astype(low), "tensor").astype(
        jnp.float32
    )
    layer_out = final.astype(low)
    grad_hidden_down = product(active, cotangent, 0, 0)
    grad_hidden_up = product(normed_feed, grad_pre, 0, 0)

    def own(values):
        return lax.dynamic_slice_in_dim(values, slot * share, share, 0)

    grad_rows = own(cotangent).astype(jnp.float32) + norm_backward(
        feed_rows, own(plain_feed), own(scale_feed), gain_three
    )
    branch_cross = gather_rows(grad_rows.astype(low), "tensor")
    grad_after_cross = branch_cross.astype(jnp.float32)
    grad_cross_output = product(mixed_cross, branch_cross, 1, 0)
    grad_mixed_cross = product(
        branch_cross, jnp.concatenate([pad, cross_output], axis=0), 1, 1
    ).astype(low)
    back = attend_back(
        False, heads, meta, None, cross_queries, grad_mixed_cross, mixed_cross, lse_cross, cross_parts
    )
    grad_cross_q = back[0]
    grad_cross_sides = scatter_xor(back[1:], "ctx").astype(low)
    cross_part = product(gather_rows(grad_cross_q, "tensor"), cross_query_all, 0, 0)
    grad_gain_cross = jnp.sum(cross_part * plain_cross, axis=0) * (1.0 / slots)
    grad_after_self = grad_after_cross + norm_backward(
        cross_part, plain_cross, scale_cross, gain_two
    )
    branch_self = grad_after_self.astype(low)
    grad_encoder = lax.psum(product(grad_cross_sides, cross_sides, 1, 1).astype(low), "tensor")
    grad_cross_query = product(normed_cross, grad_cross_q, 0, 1)
    grad_cross_both = product(encoded, grad_cross_sides, 0, 0)

    grad_self_output = product(mixed_self, branch_self, 1, 0)
    grad_mixed_self = product(
        branch_self, jnp.concatenate([pad, self_output], axis=0), 1, 1
    ).astype(low)
    back = attend_back(
        True, heads, meta, bias_rows, queries, grad_mixed_self, mixed_self, lse_self, sides
    )
    grad_queries = back[0]
    grad_sides = scatter_xor(back[1:-1], "ctx").astype(low)
    grad_bias = jnp.dot(
        jnp.asarray(span_onehot().T), back[-1].T, precision=HIGHEST
    )[:, :heads]
    self_part = product(grad_queries, self_query, 0, 1) + product(grad_sides, self_sides, 1, 1)
    grad_gain_self = jnp.sum(self_part * plain_self, axis=0)
    self_rows = scatter_rows(self_part, "tensor")
    hidden_rows = own(grad_after_self) + norm_backward(
        self_rows, own(plain_self), own(scale_self), gain_one
    )
    grad_hidden = gather_rows(hidden_rows.astype(low), "tensor")
    grad_self_query = product(normed_self, grad_queries, 0, 1)
    grad_self_both = product(normed_self, grad_sides, 0, 0)

    def total(values):
        return lax.psum(values.astype(low), ("dp", "ctx")).astype(jnp.float32)

    gains = lax.psum(
        jnp.stack([grad_gain_self, grad_gain_cross, grad_gain_feed]), ("dp", "ctx", "tensor")
    )
    grad_self_both = total(grad_self_both)
    grad_cross_both = total(grad_cross_both)
    return (
        layer_out[None],
        grad_hidden[None],
        grad_encoder[None],
        gains[0],
        gains[1],
        gains[2],
        total(grad_self_query),
        grad_self_both[:, :inner],
        grad_self_both[:, inner:],
        total(grad_self_output),
        lax.psum(grad_bias, ("dp", "ctx")),
        total(grad_cross_query),
        grad_cross_both[:, :inner],
        grad_cross_both[:, inner:],
        total(grad_cross_output),
        total(grad_hidden_up),
        total(grad_hidden_down),
    )


def solution(mesh):
    rows = P("dp", "ctx", None)
    ids = P("dp", None)
    columns = P(None, "tensor")
    shards = P("tensor", None)
    placed = (
        (rows, rows, ids, ids, P(), P(), P())
        + (columns, columns, columns, shards, columns, columns, columns, columns, shards)
        + (columns, shards, rows)
    )
    given = (
        (rows, rows, rows, P(), P(), P())
        + (columns, columns, columns, shards, columns, columns, columns, columns, shards)
        + (columns, shards)
    )
    return jax.shard_map(body, mesh=mesh, in_specs=placed, out_specs=given, check_vma=False)
```

```python
import math
import functools
import numpy as np
import jax
import jax.numpy as jnp
from jax import lax
from jax.sharding import PartitionSpec as P
from jax.experimental import pallas as pl
from jax.experimental.pallas import tpu as pltpu

BUCKETS = 32
MAXDIST = 128
DOCS = 8
EPSILON = 1e-06
MASKED = -1000000000.0
MASK_WEIGHT = -float(2**30)
CURVE_SCALE = math.sqrt(2.0 / math.pi)
CUBIC_TERM = 0.044715
HIGHEST = lax.Precision.HIGHEST

HEAD = 64
KEYS = 256
WIDE = 256
SPAN = 1280
VMEM_BYTES = 60 * 1024 * 1024


def position_bucket(distance):
    exact_cut = BUCKETS // 2
    if distance < exact_cut:
        return distance
    scaled = math.log(distance / exact_cut) / math.log(MAXDIST / exact_cut) * (BUCKETS - exact_cut)
    return min(exact_cut + int(scaled), BUCKETS - 1)


def span_onehot():
    table = np.zeros((SPAN, BUCKETS), np.float32)
    for place in range(KEYS, KEYS + 3 * KEYS):
        table[place, position_bucket(place - KEYS)] = 1.0
    return table


def taking(microseconds):
    return pl.CostEstimate(flops=int(microseconds * 1e9), transcendentals=0, bytes_accessed=int(microseconds * 3.5e6))


def dot_nt(left, right):
    return lax.dot_general(left, right, (((1,), (1,)), ((), ())), preferred_element_type=jnp.float32)


def dot_nn(left, right):
    return lax.dot_general(left, right, (((1,), (0,)), ((), ())), preferred_element_type=jnp.float32)


def onehot_rows(count, first, meta, base):
    lane = lax.broadcasted_iota(jnp.int32, (1, HEAD), 1)
    low = jnp.zeros((1, HEAD), jnp.int32)
    high = jnp.zeros((1, HEAD), jnp.int32)
    for d in range(DOCS):
        low = jnp.where(lane == d, meta[base + d], low)
        high = jnp.where(lane == d, meta[base + d + 1], high)
    place = lax.broadcasted_iota(jnp.int32, (count, HEAD), 0) + first
    return (place >= low) & (place < high)


def head_mask(width, first, head, feature_from):
    lane = lax.broadcasted_iota(jnp.int32, (1, width), 1)
    start = first + head * HEAD
    keep = (lane >= start) & (lane < start + HEAD)
    if feature_from is not None:
        keep = keep | (lane >= feature_from)
    return keep.astype(jnp.float32).astype(jnp.bfloat16)


def gather_blocks(meta, parts, kvs, kext, key_base):
    rows = parts[0].shape[0]
    me = meta[1]
    inner = kext.shape[1] - HEAD
    for r, part in enumerate(parts):
        at = pl.multiple_of(jnp.bitwise_xor(me, r) * rows, rows)
        kvs[pl.ds(at, rows), :] = part[...]
        kext[pl.ds(at, rows), 0:inner] = part[:, 0:inner]
        kext[pl.ds(at, rows), inner:] = onehot_rows(rows, at, meta, key_base).astype(jnp.float32).astype(jnp.bfloat16)


def query_heads(meta, q_ref, qx, qm, heads, query_base):
    rows, inner = q_ref.shape
    own = onehot_rows(rows, meta[0], meta, query_base)
    qx[:, 0:inner] = q_ref[...]
    qx[:, inner:] = jnp.where(own, 0.0, MASK_WEIGHT).astype(jnp.bfloat16)
    for h in range(heads):
        qm[h] = qx[...] * head_mask(qx.shape[1], 0, h, inner)


def bias_tiles(u_ref, tile, heads):
    for h in range(heads):
        row = jnp.broadcast_to(u_ref[h : h + 1, :], (KEYS, SPAN))
        tile[h] = pltpu.roll(row, 0, 1, stride=1, stride_axis=0)[:, 0 : 4 * KEYS]


def key_range(meta, rows, query_base, key_base):
    first = meta[0]
    last = first + rows - 1
    low = meta[key_base]
    high = meta[key_base + 1]
    for d in range(1, DOCS):
        low = jnp.where(meta[query_base + d] <= first, meta[key_base + d], low)
        high = jnp.where(meta[query_base + d] <= last, meta[key_base + d + 1], high)
    return lax.div(low, KEYS), lax.div(high + KEYS - 1, KEYS)


def for_blocks(meta, rows, causal, query_base, key_base, step):
    low, high = key_range(meta, rows, query_base, key_base)
    if not causal:
        lax.fori_loop(low, high, lambda kb, c: (step(kb, None), c)[1], 0)
        return
    near = lax.div(meta[0], KEYS)
    lax.fori_loop(low, near - 1, lambda kb, c: (step(kb, None), c)[1], 0)

    @pl.when(near > 0)
    def _():
        step(near - 1, 2 * KEYS)

    step(near, KEYS)
    step(near + 1, 0)


def forward_kernel(causal, heads, count, meta, *refs):
    if causal:
        u_ref, q_ref = refs[0], refs[1]
        refs = refs[2:]
    else:
        q_ref = refs[0]
        refs = refs[1:]
    parts, refs = refs[:count], refs[count:]
    out_ref, lse_ref, kvs, kext, vt, qx, qm, ot, top, total = refs[:10]
    query_base = 2
    key_base = 2 if causal else 2 + DOCS + 1
    rows = q_ref.shape[0]
    gather_blocks(meta, parts, kvs, kext, key_base)
    query_heads(meta, q_ref, qx, qm, heads, query_base)
    lanes = kvs.shape[1]
    for kb in range(kvs.shape[0] // KEYS):
        vt[kb] = kvs[kb * KEYS : (kb + 1) * KEYS, lanes - WIDE :].T
    if causal:
        tile = refs[10]
        bias_tiles(u_ref, tile, heads)
    top[...] = jnp.full_like(top, -3e38)
    total[...] = jnp.zeros_like(total)
    ot[...] = jnp.zeros_like(ot)
    shift = WIDE - heads * HEAD

    def step(kb, place):
        kx = kext[pl.ds(pl.multiple_of(kb * KEYS, KEYS), KEYS), :]
        for h in range(heads):
            scores = dot_nt(kx, qm[h])
            far = 0.0
            if place is not None:
                scores = scores + tile[h, :, place : place + rows]
            elif causal:
                far = u_ref[h : h + 1, 4 * KEYS - 1 : 4 * KEYS]
            before = top[h : h + 1, :]
            after = jnp.maximum(before, jnp.max(scores, axis=0, keepdims=True) + far)
            scale = jnp.exp(before - after)
            weights = jnp.exp(scores - (after - far))
            top[h : h + 1, :] = after
            total[h : h + 1, :] = total[h : h + 1, :] * scale + jnp.sum(weights, axis=0, keepdims=True)
            own = vt[kb, shift + h * HEAD : shift + (h + 1) * HEAD, :]
            at = slice(h * HEAD, (h + 1) * HEAD)
            ot[at, :] = ot[at, :] * scale + dot_nn(own, weights.astype(jnp.bfloat16))

    for_blocks(meta, rows, causal, query_base, key_base, step)
    for h in range(heads):
        at = slice(h * HEAD, (h + 1) * HEAD)
        out_ref[at, :] = (ot[at, :] / total[h : h + 1, :]).astype(jnp.bfloat16)
    lse_ref[...] = top[...] + jnp.log(total[...])


def attend(causal, heads, meta, u, queries, parts):
    rows, inner = queries.shape
    part_rows, lanes = parts[0].shape
    count = len(parts)
    length = part_rows * count
    smem = pl.BlockSpec(memory_space=pltpu.SMEM)
    vmem = pl.BlockSpec(memory_space=pltpu.VMEM)
    given = ([u] if causal else []) + [queries] + list(parts)
    scratch = [
        pltpu.VMEM((length, lanes), jnp.bfloat16),
        pltpu.VMEM((length, inner + HEAD), jnp.bfloat16),
        pltpu.VMEM((length // KEYS, WIDE, KEYS), jnp.bfloat16),
        pltpu.VMEM((rows, inner + HEAD), jnp.bfloat16),
        pltpu.VMEM((heads, rows, inner + HEAD), jnp.bfloat16),
        pltpu.VMEM((inner, rows), jnp.float32),
        pltpu.VMEM((8, rows), jnp.float32),
        pltpu.VMEM((8, rows), jnp.float32),
    ]
    if causal:
        scratch.append(pltpu.VMEM((heads, KEYS, 4 * KEYS), jnp.float32))
    return pl.pallas_call(
        functools.partial(forward_kernel, causal, heads, count),
        out_shape=(
            jax.ShapeDtypeStruct((inner, rows), jnp.bfloat16),
            jax.ShapeDtypeStruct((8, rows), jnp.float32),
        ),
        in_specs=[smem] + [vmem] * len(given),
        out_specs=(vmem, vmem),
        scratch_shapes=scratch,
        compiler_params=pltpu.CompilerParams(vmem_limit_bytes=30 * 1024 * 1024),
        cost_estimate=taking(13),
        name="self_forward" if causal else "cross_forward",
    )(meta, *given)


def fold_diagonals(values):
    half = values.shape[0] // 2
    while half >= 1:
        values = values[:half] + pltpu.roll(values[half : 2 * half], SPAN - half, 1)
        half = half // 2
    return values


def backward_kernel(causal, heads, count, branch_count, meta, *refs):
    if causal:
        u_ref = refs[0]
        refs = refs[1:]
    q_ref, out_weight, mixed_ref, lse_ref = refs[:4]
    parts, refs = refs[4 : 4 + count], refs[4 + count :]
    branches, refs = refs[:branch_count], refs[branch_count:]
    dq_ref = refs[0]
    d_refs, refs = refs[1 : 1 + count], refs[1 + count :]
    if causal:
        dbias_ref = refs[0]
        refs = refs[1:]
    if branch_count > 1:
        branch_ref = refs[0]
        refs = refs[1:]
        lay_blocks(meta, branches, branch_ref)
    else:
        branch_ref = branches[0]
    kvs, kext, kt, qx, qm, dom, ra, rb, dqt, row, dkv, do_ref = refs[:12]
    query_base = 2
    key_base = 2 if causal else 2 + DOCS + 1
    rows, inner = q_ref.shape
    lanes = kvs.shape[1]
    do_ref[:, 0:inner] = jnp.zeros((rows, inner), jnp.bfloat16)
    do_ref[:, inner:] = dot_nt(branch_ref[...], out_weight[...]).astype(jnp.bfloat16)
    gather_blocks(meta, parts, kvs, kext, key_base)
    query_heads(meta, q_ref, qx, qm, heads, query_base)
    for kb in range(kvs.shape[0] // KEYS):
        kt[kb] = kvs[kb * KEYS : (kb + 1) * KEYS, 0:WIDE].T
    shift = WIDE - inner
    for h in range(heads):
        dom[h] = do_ref[:, lanes - WIDE :] * head_mask(WIDE, shift, h, None)
        ra[h * rows : (h + 1) * rows, :] = q_ext_only(qx, h, inner)
    ra[heads * rows :, :] = do_ref[:, 0:WIDE] * head_mask(WIDE, inner, 0, None)
    for h in range(1, heads):
        rb[(h - 1) * rows : h * rows, :] = do_ref[:, WIDE:] * head_mask(lanes - WIDE, inner - WIDE, h, None)
    turned = do_ref[:, lanes - WIDE :].astype(jnp.float32).T
    inner_sum = turned[shift:, :] * mixed_ref[...].astype(jnp.float32)
    for h in range(heads):
        row[h : h + 1, :] = jnp.sum(inner_sum[h * HEAD : (h + 1) * HEAD, :], axis=0, keepdims=True)
    dqt[...] = jnp.zeros_like(dqt)
    dkv[...] = jnp.zeros_like(dkv)
    if causal:
        tile, dtile, dfar = refs[12:15]
        bias_tiles(u_ref, tile, heads)
        dtile[...] = jnp.zeros_like(dtile)
        dfar[...] = jnp.zeros_like(dfar)

    def step(kb, place):
        at_keys = pl.ds(pl.multiple_of(kb * KEYS, KEYS), KEYS)
        kx = kext[at_keys, :]
        vx = kvs[at_keys, lanes - WIDE :]
        weights_low = []
        grads_low = []
        for h in range(heads):
            scores = dot_nt(kx, qm[h])
            lse = lse_ref[h : h + 1, :]
            if place is not None:
                scores = scores + tile[h, :, place : place + rows]
            elif causal:
                lse = lse - u_ref[h : h + 1, 4 * KEYS - 1 : 4 * KEYS]
            weights = jnp.exp(scores - lse)
            grad_weights = dot_nt(vx, dom[h])
            grads = weights * (grad_weights - row[h : h + 1, :])
            low = grads.astype(jnp.bfloat16)
            weights_low.append(weights.astype(jnp.bfloat16))
            grads_low.append(low)
            if causal:
                if place is not None:
                    dtile[h, :, place : place + rows] += low.astype(jnp.float32)
                else:
                    dfar[h : h + 1, :] += jnp.sum(low.astype(jnp.float32), axis=0, keepdims=True)
            at = slice(h * HEAD, (h + 1) * HEAD)
            dqt[at, :] += dot_nn(kt[kb, at, :], low)
        dkv[at_keys, 0:WIDE] = dot_nn(jnp.concatenate(grads_low + weights_low[:1], axis=1), ra[...]).astype(jnp.bfloat16)
        dkv[at_keys, WIDE:] = dot_nn(jnp.concatenate(weights_low[1:], axis=1), rb[...]).astype(jnp.bfloat16)

    for_blocks(meta, rows, causal, query_base, key_base, step)
    dq_ref[...] = dqt[...].astype(jnp.bfloat16)
    me = meta[1]
    part_rows = parts[0].shape[0]
    for r in range(count):
        at = pl.multiple_of(jnp.bitwise_xor(me, r) * part_rows, part_rows)
        d_refs[r][...] = dkv[pl.ds(at, part_rows), :]
    if causal:
        lane = lax.broadcasted_iota(jnp.int32, (1, SPAN), 1)
        dbias_ref[...] = jnp.zeros_like(dbias_ref)
        for h in range(heads):
            padded = jnp.concatenate([dtile[h], jnp.zeros((KEYS, SPAN - 4 * KEYS), jnp.float32)], axis=1)
            far = jnp.sum(dfar[h : h + 1, :], axis=1, keepdims=True)
            dbias_ref[h : h + 1, :] = fold_diagonals(padded) + jnp.where(lane == 4 * KEYS - 1, far, 0.0)


def q_ext_only(qx, head, inner):
    return qx[...] * head_mask(qx.shape[1], 0, head, None)


def attend_back(causal, heads, meta, u, queries, out_weight, mixed, lse, parts, branches):
    rows, inner = queries.shape
    part_rows, lanes = parts[0].shape
    count = len(parts)
    length = part_rows * count
    smem = pl.BlockSpec(memory_space=pltpu.SMEM)
    vmem = pl.BlockSpec(memory_space=pltpu.VMEM)
    given = ([u] if causal else []) + [queries, out_weight, mixed, lse] + list(parts) + list(branches)
    out_shape = [jax.ShapeDtypeStruct((inner, rows), jnp.bfloat16)]
    out_shape += [jax.ShapeDtypeStruct((part_rows, lanes), jnp.bfloat16)] * count
    if causal:
        out_shape.append(jax.ShapeDtypeStruct((8, SPAN), jnp.float32))
    if len(branches) > 1:
        out_shape.append(jax.ShapeDtypeStruct((rows, out_weight.shape[1]), jnp.bfloat16))
    scratch = [
        pltpu.VMEM((length, lanes), jnp.bfloat16),
        pltpu.VMEM((length, inner + HEAD), jnp.bfloat16),
        pltpu.VMEM((length // KEYS, WIDE, KEYS), jnp.bfloat16),
        pltpu.VMEM((rows, inner + HEAD), jnp.bfloat16),
        pltpu.VMEM((heads, rows, inner + HEAD), jnp.bfloat16),
        pltpu.VMEM((heads, rows, WIDE), jnp.bfloat16),
        pltpu.VMEM(((heads + 1) * rows, WIDE), jnp.bfloat16),
        pltpu.VMEM(((heads - 1) * rows, lanes - WIDE), jnp.bfloat16),
        pltpu.VMEM((inner, rows), jnp.float32),
        pltpu.VMEM((8, rows), jnp.float32),
        pltpu.VMEM((length, lanes), jnp.bfloat16),
        pltpu.VMEM((rows, lanes), jnp.bfloat16),
    ]
    if causal:
        scratch += [
            pltpu.VMEM((heads, KEYS, 4 * KEYS), jnp.float32),
            pltpu.VMEM((heads, KEYS, 4 * KEYS), jnp.float32),
            pltpu.VMEM((8, rows), jnp.float32),
        ]
    return pl.pallas_call(
        functools.partial(backward_kernel, causal, heads, count, len(branches)),
        out_shape=tuple(out_shape),
        in_specs=[smem] + [vmem] * len(given),
        out_specs=tuple([vmem] * len(out_shape)),
        scratch_shapes=scratch,
        compiler_params=pltpu.CompilerParams(vmem_limit_bytes=30 * 1024 * 1024),
        cost_estimate=taking(19),
        name="self_backward" if causal else "cross_backward",
    )(meta, *given)


def position_rows(bias_table, heads):
    table = span_onehot()
    rows = jnp.dot(bias_table.astype(jnp.bfloat16).T, jnp.asarray(table.T, jnp.bfloat16), preferred_element_type=jnp.float32)
    rows = rows + jnp.asarray(np.where(table.sum(1) > 0, 0.0, MASKED)[None, :], jnp.float32)
    return jnp.concatenate([rows, jnp.zeros((8 - heads, SPAN), jnp.float32)], axis=0)


def make_meta(dec_row, enc_row, offset, place, rest):
    docs = jnp.arange(DOCS + 1, dtype=jnp.int32)
    dec = jnp.sum((dec_row[None, :] < docs[:, None]).astype(jnp.int32), axis=1)
    enc = jnp.sum((enc_row[None, :] < docs[:, None]).astype(jnp.int32), axis=1)
    first = jnp.stack([offset, place]).astype(jnp.int32)
    return jnp.concatenate([first, dec, enc, jnp.stack(rest).astype(jnp.int32)])


def room(*groups):
    total = 0
    for group in groups:
        for x in group:
            rows = int(np.prod(x.shape[:-1])) if x.shape else 1
            lanes = -(-x.shape[-1] // 128) * 128 if x.shape else 128
            total += max(rows, 8) * lanes * jnp.dtype(x.dtype).itemsize
    return 2 * total + 4 * 1024 * 1024


def onchip(kernel, name, out_shape, given, scratch=(), specs=None, cost=2):
    vmem = pl.BlockSpec(memory_space=pltpu.VMEM)
    in_specs = [pl.BlockSpec(memory_space=pltpu.SMEM)] + [vmem] * (len(given) - 1)
    for at, spec in (specs or {}).items():
        in_specs[at] = spec
    return pl.pallas_call(
        kernel,
        grid=(1,) if specs else (),
        out_shape=tuple(out_shape),
        in_specs=in_specs,
        out_specs=tuple([vmem] * len(out_shape)),
        scratch_shapes=list(scratch),
        compiler_params=pltpu.CompilerParams(vmem_limit_bytes=room(out_shape, given, scratch)),
        cost_estimate=taking(cost),
        name=name,
    )(*given)


def shape_of(rows, columns, kind):
    return jax.ShapeDtypeStruct((rows, columns), kind)


F32 = jnp.float32
LOW = jnp.bfloat16
AT_SLOT = 2 + 2 * (DOCS + 1)
AT_ODD = AT_SLOT + 1
AT_HALF = AT_SLOT + 2
AT_QUARTER = AT_SLOT + 3


def plain_of(values):
    scale = lax.rsqrt(jnp.mean(values * values, axis=-1, keepdims=True) + EPSILON)
    return values * scale, scale


def input_gradient(grad_normed, plain, scale, gain):
    grad_plain = grad_normed * gain
    inner = jnp.mean(grad_plain * plain, axis=-1, keepdims=True)
    return scale * (grad_plain - plain * inner)


def sides_kernel(meta, x_ref, gain_ref, k_ref, v_ref, normed_ref, out_ref):
    plain, _ = plain_of(x_ref[...].astype(F32))
    normed = (plain * gain_ref[...].astype(F32)).astype(LOW)
    normed_ref[...] = normed
    out_ref[...] = dot_nt(normed, jnp.concatenate([k_ref[...], v_ref[...]], axis=0)).astype(LOW)


def others_kernel(meta, normed_ref, q_ref, enc_ref, k_ref, v_ref, out_ref, sides_ref):
    out_ref[...] = dot_nt(normed_ref[...], q_ref[...]).astype(LOW)
    sides_ref[...] = dot_nt(enc_ref[...], jnp.concatenate([k_ref[...], v_ref[...]], axis=0)).astype(LOW)


def lay_weight(meta, halves, whole):
    count = len(halves) // 2
    rows = halves[0].shape[0]
    for i, half in enumerate(halves):
        shard = jnp.bitwise_xor(meta[AT_SLOT], i % count)
        odd = meta[AT_ODD] if i < count else 1 - meta[AT_ODD]
        at = pl.multiple_of((2 * shard + odd) * rows, rows)
        whole[pl.ds(at, rows), :] = half[...]


def lay_blocks(meta, blocks, whole):
    rows = blocks[0].shape[0]
    for r, block in enumerate(blocks):
        at = pl.multiple_of(jnp.bitwise_xor(meta[AT_SLOT], r) * rows, rows)
        whole[pl.ds(at, rows), :] = block[...]


def deal_blocks(meta, whole, blocks):
    rows = blocks[0].shape[0]
    for r, block in enumerate(blocks):
        at = pl.multiple_of(jnp.bitwise_xor(meta[AT_SLOT], r) * rows, rows)
        block[...] = whole[pl.ds(at, rows), :].astype(block.dtype)


def cross_entry_kernel(count, meta, x_ref, *refs):
    blocks, halves = refs[:count], refs[count : 3 * count]
    gain_ref, q_ref, after_ref, normed_ref, out_ref, weight, mixed = refs[3 * count :]
    lay_weight(meta, halves, weight)
    lay_blocks(meta, blocks, mixed)
    after = x_ref[...].astype(F32) + dot_nn(mixed[...].T, weight[...])
    after_ref[...] = after
    plain, _ = plain_of(after)
    normed = (plain * gain_ref[...].astype(F32)).astype(LOW)
    normed_ref[...] = normed
    out_ref[...] = dot_nt(normed, q_ref[...]).astype(LOW)


def feed_kernel(count, meta, after_ref, *refs):
    blocks, halves, refs = refs[:count], refs[count : 3 * count], refs[3 * count :]
    gain_ref, up_ref, down_ref, grad_ref = refs[:4]
    rows_ref, normed_ref, active_ref, pre_ref, gain_grad_ref = refs[4:9]
    dealt = refs[9 : 9 + count]
    weight, mixed, part, total = refs[9 + count :]
    lay_weight(meta, halves, weight)
    lay_blocks(meta, blocks, mixed)
    total[...] = after_ref[...] + dot_nn(mixed[...].T, weight[...])
    deal_blocks(meta, total, [rows_ref])
    plain, _ = plain_of(total[...])
    normed = (plain * gain_ref[...].astype(F32)).astype(LOW)
    normed_ref[...] = normed
    pre = dot_nn(normed, up_ref[...])
    squared = pre * pre
    bent = jnp.tanh(CURVE_SCALE * pre * (1.0 + CUBIC_TERM * squared))
    active_ref[...] = (0.5 * pre * (1.0 + bent)).astype(LOW)
    slope = 0.5 * (1.0 + bent) + 0.5 * pre * (1.0 - bent * bent) * CURVE_SCALE * (
        1.0 + 3.0 * CUBIC_TERM * squared
    )
    grad_pre = (dot_nt(grad_ref[...], down_ref[...]) * slope).astype(LOW)
    pre_ref[...] = grad_pre
    part[...] = dot_nt(grad_pre, up_ref[...])
    deal_blocks(meta, part, dealt)
    gain_grad_ref[...] = jnp.broadcast_to(
        jnp.sum(part[...] * plain, axis=0, keepdims=True), gain_grad_ref.shape
    )


def feed_back_kernel(count, meta, rows_ref, grad_ref, gain_ref, *refs):
    blocks, out_ref = refs[:count], refs[count]
    grad = blocks[0][...].astype(F32)
    for block in blocks[1:]:
        grad = grad + block[...].astype(F32)
    plain, scale = plain_of(rows_ref[...])
    rows = rows_ref.shape[0]
    own = grad_ref[pl.ds(pl.multiple_of(meta[AT_SLOT] * rows, rows), rows), :].astype(F32)
    out_ref[...] = (own + input_gradient(grad, plain, scale, gain_ref[...].astype(F32))).astype(LOW)


def layer_kernel(count, meta, active_ref, down_ref, *refs):
    dealt, part = refs[:count], refs[count]
    part[...] = dot_nn(active_ref[...], down_ref[...])
    deal_blocks(meta, part, dealt)


def three(a_ref, b_ref, c_ref):
    return a_ref[...].astype(F32) + b_ref[...].astype(F32) + c_ref[...].astype(F32)


def encoder_kernel(count, meta, keep_ref, add_ref, recv_ref, k_ref, v_ref, rows_ref, *refs):
    blocks, sides_ref, layer_ref = refs[:count], refs[count], refs[count + 1]
    dealt, part = refs[count + 2 : 2 * count + 2], refs[2 * count + 2]
    sides = three(keep_ref, add_ref, recv_ref).astype(LOW)
    sides_ref[...] = sides
    part[...] = dot_nn(sides, jnp.concatenate([k_ref[...], v_ref[...]], axis=0))
    deal_blocks(meta, part, dealt)
    rows = rows_ref[...]
    for block in blocks:
        rows = rows + block[...].astype(F32)
    layer_ref[...] = rows.astype(LOW)


def self_entry_kernel(count, meta, after_ref, *refs):
    blocks, halves, refs = refs[:count], refs[count : 3 * count], refs[3 * count :]
    gain_ref, branch_ref, rows_ref, out_ref, gain_grad_ref, weight, turned, total = refs
    lay_weight(meta, halves, weight)
    lay_blocks(meta, blocks, turned)
    part = dot_nn(turned[...].T, weight[...])
    plain, scale = plain_of(after_ref[...])
    grad = branch_ref[...].astype(F32) + input_gradient(part, plain, scale, gain_ref[...].astype(F32))
    total[...] = grad
    out_ref[...] = grad.astype(LOW)
    deal_blocks(meta, total, [rows_ref])
    share = 1.0 / count
    gain_grad_ref[...] = jnp.broadcast_to(
        share * jnp.sum(part * plain, axis=0, keepdims=True), gain_grad_ref.shape
    )


def exit_kernel(count, meta, keep_ref, add_ref, recv_ref, dq_ref, q_ref, k_ref, v_ref, x_ref, *refs):
    sides_ref, gain_grad_ref = refs[:2]
    dealt, part = refs[2 : 2 + count], refs[2 + count]
    sides = three(keep_ref, add_ref, recv_ref).astype(LOW)
    sides_ref[...] = sides
    part[...] = dot_nn(dq_ref[...].T, q_ref[...]) + dot_nn(
        sides, jnp.concatenate([k_ref[...], v_ref[...]], axis=0)
    )
    deal_blocks(meta, part, dealt)
    plain, _ = plain_of(x_ref[...].astype(F32))
    gain_grad_ref[...] = jnp.broadcast_to(
        jnp.sum(part[...] * plain, axis=0, keepdims=True), gain_grad_ref.shape
    )


def last_rows_kernel(count, meta, rows_ref, x_ref, gain_ref, *refs):
    blocks, pairs, out_ref = refs[:count], refs[count : 2 * count], refs[2 * count]
    grad = blocks[0][...].astype(F32)
    for block in blocks[1:]:
        grad = grad + block[...].astype(F32)
    rows = rows_ref.shape[0]
    own = x_ref[pl.ds(pl.multiple_of(meta[AT_SLOT] * rows, rows), rows), :].astype(F32)
    plain, scale = plain_of(own)
    out_ref[0:rows, :] = (
        rows_ref[...] + input_gradient(grad, plain, scale, gain_ref[...].astype(F32))
    ).astype(LOW)
    total = pairs[0][...].astype(F32)
    for pair in pairs[1:]:
        total = total + pair[...].astype(F32)
    out_ref[rows:, :] = total.astype(LOW)


def layer_rows_kernel(count, meta, *refs):
    lay_blocks(meta, refs[:count], refs[count])


def pair_rows_kernel(count, meta, *refs):
    blocks, first_ref, second_ref = refs[:count], refs[count], refs[count + 1]
    rows = blocks[0].shape[0] // 2
    for r, block in enumerate(blocks):
        at = pl.multiple_of(jnp.bitwise_xor(meta[AT_SLOT], r) * rows, rows)
        first_ref[pl.ds(at, rows), :] = block[0:rows, :]
        second_ref[pl.ds(at, rows), :] = block[rows:, :]


def feed_weights_kernel(split, meta, normed_ref, pre_ref, active_ref, grad_ref, first_ref, second_ref):
    up = dot_nn(normed_ref[...].T, pre_ref[...]).astype(LOW)
    down = dot_nn(active_ref[...].T, grad_ref[...]).astype(LOW)
    if not split:
        first_ref[...] = up
        second_ref[...] = down
        return
    half = meta[AT_HALF]

    @pl.when(half == 0)
    def _():
        first_ref[...] = up
        second_ref[...] = down

    @pl.when(half == 1)
    def _():
        first_ref[...] = down
        second_ref[...] = up


def cross_weights_kernel(meta, dq_ref, normed_ref, sides_ref, enc_ref, mixed_cross_ref, branch_cross_ref, mixed_self_ref, branch_self_ref, out_ref):
    inner = dq_ref.shape[0]
    out_ref[0:inner, :] = dot_nn(dq_ref[...], normed_ref[...]).astype(LOW)
    out_ref[inner : 3 * inner, :] = dot_nn(sides_ref[...].T, enc_ref[...]).astype(LOW)
    out_ref[3 * inner : 4 * inner, :] = dot_nn(mixed_cross_ref[...], branch_cross_ref[...]).astype(LOW)
    out_ref[4 * inner :, :] = dot_nn(mixed_self_ref[...], branch_self_ref[...]).astype(LOW)


def payload_kernel(split, meta, cross_ref, normed_ref, dq_ref, sides_ref, g1_ref, g2_ref, g3_ref, bias_ref, hot_ref, *refs):
    outs, whole = refs[:-1], refs[-1]
    inner = dq_ref.shape[0]
    width = normed_ref.shape[1]
    at = 5 * inner
    whole[0:at, :] = cross_ref[...]
    whole[at : at + inner, :] = dot_nn(dq_ref[...], normed_ref[...]).astype(LOW)
    whole[at + inner : at + 3 * inner, :] = dot_nn(sides_ref[...].T, normed_ref[...]).astype(LOW)
    row = lax.broadcasted_iota(jnp.int32, (8, width), 0)
    gains = jnp.where(row == 0, g1_ref[...], jnp.where(row == 1, g2_ref[...], g3_ref[...]))
    gains = jnp.where(row < 3, gains, 0.0)
    diagonal = bias_ref[...]
    high = diagonal.astype(LOW)
    rest = (diagonal - high.astype(F32)).astype(LOW)
    bias = dot_nn(high, hot_ref[...]) + dot_nn(rest, hot_ref[...])
    bias = jnp.concatenate([bias, jnp.zeros((8, width - bias.shape[1]), F32)], axis=1)
    at = at + 3 * inner
    whole[at : at + 16, :] = jnp.concatenate([gains, bias], axis=0).astype(LOW)
    whole[at + 16 :, :] = jnp.zeros((whole.shape[0] - at - 16, width), LOW)
    if not split:
        outs[0][...] = whole[...]
        return
    rows = whole.shape[0] // 2
    half = meta[AT_HALF]
    outs[0][...] = whole[pl.ds(pl.multiple_of(half * rows, rows), rows), :]
    outs[1][...] = whole[pl.ds(pl.multiple_of((1 - half) * rows, rows), rows), :]


def quarter_kernel(meta, keep_ref, recv_ref, *refs):
    blocks, total = refs[:4], refs[4]
    total[...] = keep_ref[...].astype(F32) + recv_ref[...].astype(F32)
    rows = blocks[0].shape[0]
    for f in range(4):
        at = pl.multiple_of(jnp.bitwise_xor(meta[AT_QUARTER], f) * rows, rows)
        blocks[f][...] = total[pl.ds(at, rows), :].astype(LOW)


def finish_kernel(split, meta, *refs):
    count = 8 if split else 1
    parts, outs, whole = refs[:count], refs[count:-1], refs[-1]
    if split:
        rows = parts[0].shape[0]
        half = meta[AT_HALF]
        for i, part in enumerate(parts):
            side = half if i < 4 else 1 - half
            at = side * 4 * rows + jnp.bitwise_xor(meta[AT_QUARTER], i % 4) * rows
            whole[pl.ds(pl.multiple_of(at, rows), rows), :] = part[...].astype(F32)
    else:
        whole[...] = parts[0][...].astype(F32)
    at = 0
    for out in outs:
        out[...] = whole[at : at + out.shape[0], :]
        at += out.shape[0]


def swap(values, axis, flip):
    count = lax.axis_size(axis)
    return lax.ppermute(values, axis, [(i, i ^ flip) for i in range(count)])


def swaps(values, axis):
    return [values] + [swap(values, axis, flip) for flip in range(1, lax.axis_size(axis))]


def trades(blocks, axis):
    return [blocks[0]] + [swap(block, axis, flip) for flip, block in enumerate(blocks) if flip]


def after(values, *others):
    return lax.optimization_barrier((values,) + others)[0]


def body(
    hidden_in,
    encoder_out,
    dec_segments,
    enc_segments,
    gain_self,
    gain_cross,
    gain_feed,
    self_query,
    self_key,
    self_value,
    self_output,
    bias_table,
    cross_query,
    cross_key,
    cross_value,
    cross_output,
    hidden_up,
    hidden_down,
    out_grad,
):
    tok_len, width = hidden_in.shape[1:]
    heads = bias_table.shape[1]
    inner = self_query.shape[1]
    place = lax.axis_index("ctx")
    slot = lax.axis_index("tensor")
    slots = lax.axis_size("tensor")
    split = lax.axis_size("dp") == 2 and lax.axis_size("ctx") == 4
    both = ("dp", "ctx")
    share = tok_len // slots
    lanes = 2 * inner
    odd = place & 1
    combined = lax.axis_index("dp") * 4 + place
    meta = make_meta(
        dec_segments[0],
        enc_segments[0],
        place * tok_len,
        place,
        [slot, odd, combined & 1, (combined >> 1) & 3],
    )
    bias_rows = position_rows(bias_table, heads)
    tokens = hidden_in[0]
    encoded = encoder_out[0]
    cotangent = out_grad[0]
    gain_one = gain_self[None]
    gain_two = gain_cross[None]
    gain_three = gain_feed[None]
    rows_low = shape_of(tok_len, width, LOW)
    rows_full = shape_of(tok_len, width, F32)
    part_low = shape_of(share, width, LOW)
    part_full = shape_of(share, width, F32)
    sum_row = shape_of(8, width, F32)
    weight_room = pltpu.VMEM((slots * inner, width), LOW)
    mixed_room = pltpu.VMEM((slots * inner, tok_len), LOW)
    total_room = pltpu.VMEM((tok_len, width), F32)

    def send(block, flip):
        return lax.ppermute(block, both, [(i, i ^ flip) for i in range(8)])

    def share_terms(halves):
        if not split:
            return list(halves)
        rows, columns = halves[0].shape
        return onchip(
            quarter_kernel,
            "quarters",
            [shape_of(rows // 4, columns, LOW)] * 4,
            [meta, halves[0], send(halves[1], 1)],
            [pltpu.VMEM((rows, columns), F32)],
            cost=3,
        )

    def sum_shares(blocks):
        if not split:
            return [lax.psum(block, both) for block in blocks]
        own = blocks[0].astype(F32)
        for flip in (3, 1, 2):
            own = own + send(blocks[flip], 2 * flip).astype(F32)
        return [own.astype(LOW)]

    def spread_shares(own):
        if not split:
            return [jnp.concatenate(own, axis=0)]
        held = [own[0]] + [send(own[0], 2 * flip) for flip in (1, 2, 3)]
        return held + [send(block, 1) for block in held]

    self_query, self_key, self_value = self_query.T, self_key.T, self_value.T
    cross_query, cross_key, cross_value = cross_query.T, cross_key.T, cross_value.T

    def half_shards(weight):
        return swaps(lax.dynamic_slice_in_dim(weight, odd * (inner // 2), inner // 2, 0), "tensor")

    def both_halves(halves):
        return halves + [swap(half, "ctx", 1) for half in halves]

    self_output_halves = half_shards(self_output)

    normed_self, own_sides = onchip(
        sides_kernel,
        "self_sides",
        [rows_low, shape_of(tok_len, lanes, LOW)],
        [meta, tokens, gain_one, self_key, self_value],
    )
    far_sides = swap(own_sides, "ctx", 2)
    queries, own_cross = onchip(
        others_kernel,
        "query_and_cross_sides",
        [shape_of(tok_len, inner, LOW), shape_of(tok_len, lanes, LOW)],
        [meta, normed_self, self_query, encoded, cross_key, cross_value],
    )
    sides = [own_sides, swap(own_sides, "ctx", 1), far_sides, swap(far_sides, "ctx", 1)]
    own_cross = after(own_cross, far_sides)
    far_cross = swap(own_cross, "ctx", 2)
    cross_sides = [own_cross, swap(own_cross, "ctx", 1), far_cross, swap(far_cross, "ctx", 1)]
    mixed_self, lse_self = attend(True, heads, meta, bias_rows, queries, sides)
    self_output_parts = both_halves(self_output_halves)
    later = after((cross_output, cross_query), *self_output_halves)
    cross_output_halves = half_shards(later[0])
    cross_query_halves = half_shards(after(later[1], *cross_output_halves))
    cross_output_parts = both_halves(cross_output_halves)
    cross_query_parts = both_halves(cross_query_halves)
    after_self, normed_cross, cross_queries = onchip(
        functools.partial(cross_entry_kernel, slots),
        "cross_entry",
        [rows_full, rows_low, shape_of(tok_len, inner, LOW)],
        [meta, tokens] + swaps(mixed_self, "tensor") + self_output_parts + [gain_two, cross_query],
        [weight_room, mixed_room],
        cost=5,
    )
    mixed_cross, lse_cross = attend(False, heads, meta, None, cross_queries, cross_sides)
    fed = onchip(
        functools.partial(feed_kernel, slots),
        "feed",
        [part_full, rows_low, rows_low, rows_low, sum_row] + [part_low] * slots,
        [meta, after_self]
        + swaps(mixed_cross, "tensor")
        + cross_output_parts
        + [gain_three, hidden_up, hidden_down, cotangent],
        [weight_room, mixed_room, total_room, total_room],
        cost=8,
    )
    after_rows, normed_feed, active, grad_pre, gain_grad_feed = fed[:5]
    (branch_rows,) = onchip(
        functools.partial(feed_back_kernel, slots),
        "feed_back",
        [part_low],
        [meta, after_rows, cotangent, gain_three] + trades(fed[5:], "tensor"),
    )
    feed_weights = onchip(
        functools.partial(feed_weights_kernel, split),
        "feed_weights",
        [shape_of(width, hidden_up.shape[1], LOW)] * 2,
        [meta, normed_feed, grad_pre, active, cotangent],
        cost=5,
    )
    layer_parts = onchip(
        functools.partial(layer_kernel, slots),
        "layer_parts",
        [part_low] * slots,
        [meta, active, hidden_down],
        [total_room],
        cost=3,
    )
    feed_blocks = share_terms(feed_weights)
    branches = list(after(tuple(swaps(branch_rows, "tensor")), layer_parts, feed_blocks))
    feed_own = sum_shares(feed_blocks)
    layer_blocks = trades(after(tuple(layer_parts), *branches), "tensor")

    back = attend_back(
        False, heads, meta, None, cross_queries, cross_output, mixed_cross, lse_cross, cross_sides, branches
    )
    grad_cross_q, terms, branch_cross = back[0], back[1:5], back[5]
    near_terms = [swap(terms[1], "ctx", 1), swap(terms[3], "ctx", 1)]
    far_terms = swap((terms[2].astype(F32) + near_terms[1].astype(F32)).astype(LOW), "ctx", 2)
    after_self_rows, branch_self, gain_grad_cross = onchip(
        functools.partial(self_entry_kernel, slots),
        "self_entry",
        [part_full, rows_low, sum_row],
        [meta, after_self]
        + swaps(after(grad_cross_q, feed_own, *layer_blocks), "tensor")
        + cross_query_parts
        + [gain_two, branch_cross],
        [weight_room, mixed_room, total_room],
        cost=5,
    )
    encoded_out = onchip(
        functools.partial(encoder_kernel, slots),
        "encoder_parts",
        [shape_of(tok_len, lanes, LOW), part_low] + [part_low] * slots,
        [meta, terms[0], near_terms[0], far_terms, cross_key, cross_value, after_rows] + layer_blocks,
        [total_room],
        cost=4,
    )
    grad_cross_sides = encoded_out[0]
    feed_summed = spread_shares(feed_own)
    branch_self = after(branch_self, encoded_out)
    encoder_blocks = trades(after(tuple(encoded_out[2:]), branch_self), "tensor")

    back = attend_back(
        True, heads, meta, bias_rows, queries, self_output, mixed_self, lse_self, sides, [branch_self]
    )
    grad_queries, terms, diagonals = back[0], back[1:5], back[5]
    terms = after(tuple(terms), *encoder_blocks)
    near_terms = [swap(terms[1], "ctx", 1), swap(terms[3], "ctx", 1)]
    far_terms = swap((terms[2].astype(F32) + near_terms[1].astype(F32)).astype(LOW), "ctx", 2)
    layer_pieces = swaps(after(encoded_out[1], *encoder_blocks), "tensor")
    (cross_weights,) = onchip(
        cross_weights_kernel,
        "cross_weights",
        [shape_of(5 * inner, width, LOW)],
        [meta, grad_cross_q, normed_cross, grad_cross_sides, encoded, mixed_cross, branch_cross]
        + [mixed_self, branch_self],
        cost=4,
    )
    left = onchip(
        functools.partial(exit_kernel, slots),
        "self_exit",
        [shape_of(tok_len, lanes, LOW), sum_row] + [part_low] * slots,
        [meta, terms[0], near_terms[0], far_terms, grad_queries, self_query, self_key, self_value, tokens],
        [total_room],
    )
    grad_sides, gain_grad_self = left[:2]
    left = left[:2] + after(tuple(left[2:]), *layer_pieces)
    (last_rows,) = onchip(
        functools.partial(last_rows_kernel, slots),
        "last_rows",
        [shape_of(2 * share, width, LOW)],
        [meta, after_self_rows, tokens, gain_one] + trades(left[2:], "tensor") + encoder_blocks,
        cost=3,
    )
    (layer_out,) = onchip(
        functools.partial(layer_rows_kernel, slots), "layer_rows", [rows_low], [meta] + layer_pieces
    )
    weight_rows = -(-(8 * inner + 16) // 128) * 128
    hot = jnp.asarray(np.pad(span_onehot(), ((0, 0), (0, 128 - BUCKETS))), LOW)
    payload = onchip(
        functools.partial(payload_kernel, split),
        "last_weights",
        [shape_of(weight_rows // 2, width, LOW)] * 2 if split else [shape_of(weight_rows, width, LOW)],
        [meta, cross_weights, normed_self, grad_queries, grad_sides]
        + [gain_grad_self, gain_grad_cross, gain_grad_feed, diagonals, hot],
        [pltpu.VMEM((weight_rows, width), LOW)],
        cost=5,
    )
    summed = spread_shares(sum_shares(share_terms(payload)))
    weights = onchip(
        functools.partial(finish_kernel, split),
        "finish",
        [shape_of(inner, width, F32)] * 8 + [shape_of(16, width, F32)],
        [meta] + summed,
        [pltpu.VMEM((weight_rows, width), F32)],
        cost=4,
    )
    tail = weights[8]
    grad_up, grad_down = onchip(
        functools.partial(finish_kernel, split),
        "feed_finish",
        [shape_of(width, hidden_up.shape[1], F32)] * 2,
        [meta] + feed_summed,
        [pltpu.VMEM((2 * width, width), F32)],
        cost=4,
    )
    grad_hidden, grad_encoder = onchip(
        functools.partial(pair_rows_kernel, slots),
        "gathered_rows",
        [rows_low, rows_low],
        [meta] + swaps(last_rows, "tensor"),
        cost=3,
    )
    gains = tail[:8]
    for flip in range(1, slots):
        gains = gains + swap(tail[:8], "tensor", flip)
    return (
        layer_out[None],
        grad_hidden[None],
        grad_encoder[None],
        gains[0],
        gains[1],
        gains[2],
        weights[5].T,
        weights[6].T,
        weights[7].T,
        weights[4],
        tail[8 : 8 + heads, :BUCKETS].T,
        weights[0].T,
        weights[1].T,
        weights[2].T,
        weights[3],
        grad_up,
        grad_down,
    )


def solution(mesh):
    rows = P("dp", "ctx", None)
    ids = P("dp", None)
    columns = P(None, "tensor")
    shards = P("tensor", None)
    placed = (
        (rows, rows, ids, ids, P(), P(), P())
        + (columns, columns, columns, shards, columns, columns, columns, columns, shards)
        + (columns, shards, rows)
    )
    given = (
        (rows, rows, rows, P(), P(), P())
        + (columns, columns, columns, shards, columns, columns, columns, columns, shards)
        + (columns, shards)
    )
    return jax.shard_map(body, mesh=mesh, in_specs=placed, out_specs=given, check_vma=False)
```

```python
import math
import functools
import numpy as np
import jax
import jax.numpy as jnp
from jax import lax
from jax.sharding import PartitionSpec as P
from jax.experimental import pallas as pl
from jax.experimental.pallas import tpu as pltpu

BUCKETS = 32
MAXDIST = 128
DOCS = 8
EPSILON = 1e-06
MASKED = -1000000000.0
MASK_WEIGHT = -float(2**30)
CURVE_SCALE = math.sqrt(2.0 / math.pi)
CUBIC_TERM = 0.044715
HIGHEST = lax.Precision.HIGHEST

HEAD = 64
KEYS = 256
WIDE = 256
SPAN = 1280
VMEM_BYTES = 60 * 1024 * 1024


def position_bucket(distance):
    exact_cut = BUCKETS // 2
    if distance < exact_cut:
        return distance
    scaled = math.log(distance / exact_cut) / math.log(MAXDIST / exact_cut) * (BUCKETS - exact_cut)
    return min(exact_cut + int(scaled), BUCKETS - 1)


def span_onehot():
    table = np.zeros((SPAN, BUCKETS), np.float32)
    for place in range(KEYS, KEYS + 3 * KEYS):
        table[place, position_bucket(place - KEYS)] = 1.0
    return table


def taking(microseconds):
    return pl.CostEstimate(flops=int(microseconds * 1e9), transcendentals=0, bytes_accessed=int(microseconds * 3.5e6))


def dot_nt(left, right):
    return lax.dot_general(left, right, (((1,), (1,)), ((), ())), preferred_element_type=jnp.float32)


def dot_nn(left, right):
    return lax.dot_general(left, right, (((1,), (0,)), ((), ())), preferred_element_type=jnp.float32)


def onehot_rows(count, first, meta, base):
    lane = lax.broadcasted_iota(jnp.int32, (1, HEAD), 1)
    low = jnp.zeros((1, HEAD), jnp.int32)
    high = jnp.zeros((1, HEAD), jnp.int32)
    for d in range(DOCS):
        low = jnp.where(lane == d, meta[base + d], low)
        high = jnp.where(lane == d, meta[base + d + 1], high)
    place = lax.broadcasted_iota(jnp.int32, (count, HEAD), 0) + first
    return (place >= low) & (place < high)


def head_mask(width, first, head, feature_from):
    lane = lax.broadcasted_iota(jnp.int32, (1, width), 1)
    start = first + head * HEAD
    keep = (lane >= start) & (lane < start + HEAD)
    if feature_from is not None:
        keep = keep | (lane >= feature_from)
    return keep.astype(jnp.float32).astype(jnp.bfloat16)


def gather_blocks(meta, parts, kvs, kext, key_base):
    rows = parts[0].shape[0]
    me = meta[1]
    inner = kext.shape[1] - HEAD
    for r, part in enumerate(parts):
        at = pl.multiple_of(jnp.bitwise_xor(me, r) * rows, rows)
        kvs[pl.ds(at, rows), :] = part[...]
        kext[pl.ds(at, rows), 0:inner] = part[:, 0:inner]
        kext[pl.ds(at, rows), inner:] = onehot_rows(rows, at, meta, key_base).astype(jnp.float32).astype(jnp.bfloat16)


def query_heads(meta, q_ref, qx, qm, heads, query_base):
    rows, inner = q_ref.shape
    own = onehot_rows(rows, meta[0], meta, query_base)
    qx[:, 0:inner] = q_ref[...]
    qx[:, inner:] = jnp.where(own, 0.0, MASK_WEIGHT).astype(jnp.bfloat16)
    for h in range(heads):
        qm[h] = qx[...] * head_mask(qx.shape[1], 0, h, inner)


def bias_tiles(u_ref, tile, heads):
    for h in range(heads):
        row = jnp.broadcast_to(u_ref[h : h + 1, :], (KEYS, SPAN))
        tile[h] = pltpu.roll(row, 0, 1, stride=1, stride_axis=0)[:, 0 : 4 * KEYS]


def key_range(meta, rows, query_base, key_base):
    first = meta[0]
    last = first + rows - 1
    low = meta[key_base]
    high = meta[key_base + 1]
    for d in range(1, DOCS):
        low = jnp.where(meta[query_base + d] <= first, meta[key_base + d], low)
        high = jnp.where(meta[query_base + d] <= last, meta[key_base + d + 1], high)
    return lax.div(low, KEYS), lax.div(high + KEYS - 1, KEYS)


def for_blocks(meta, rows, causal, query_base, key_base, step):
    low, high = key_range(meta, rows, query_base, key_base)
    if not causal:
        lax.fori_loop(low, high, lambda kb, c: (step(kb, None), c)[1], 0)
        return
    near = lax.div(meta[0], KEYS)
    lax.fori_loop(low, near - 1, lambda kb, c: (step(kb, None), c)[1], 0)

    @pl.when(near > 0)
    def _():
        step(near - 1, 2 * KEYS)

    step(near, KEYS)
    step(near + 1, 0)


def forward_kernel(causal, heads, count, meta, *refs):
    if causal:
        u_ref, q_ref = refs[0], refs[1]
        refs = refs[2:]
    else:
        q_ref = refs[0]
        refs = refs[1:]
    parts, refs = refs[:count], refs[count:]
    out_ref, lse_ref, kvs, kext, vt, qx, qm, ot, top, total = refs[:10]
    query_base = 2
    key_base = 2 if causal else 2 + DOCS + 1
    rows = q_ref.shape[0]
    gather_blocks(meta, parts, kvs, kext, key_base)
    query_heads(meta, q_ref, qx, qm, heads, query_base)
    lanes = kvs.shape[1]
    for kb in range(kvs.shape[0] // KEYS):
        vt[kb] = kvs[kb * KEYS : (kb + 1) * KEYS, lanes - WIDE :].T
    if causal:
        tile = refs[10]
        bias_tiles(u_ref, tile, heads)
    top[...] = jnp.full_like(top, -3e38)
    total[...] = jnp.zeros_like(total)
    ot[...] = jnp.zeros_like(ot)
    shift = WIDE - heads * HEAD

    def step(kb, place):
        kx = kext[pl.ds(pl.multiple_of(kb * KEYS, KEYS), KEYS), :]
        for h in range(heads):
            scores = dot_nt(kx, qm[h])
            far = 0.0
            if place is not None:
                scores = scores + tile[h, :, place : place + rows]
            elif causal:
                far = u_ref[h : h + 1, 4 * KEYS - 1 : 4 * KEYS]
            before = top[h : h + 1, :]
            after = jnp.maximum(before, jnp.max(scores, axis=0, keepdims=True) + far)
            scale = jnp.exp(before - after)
            weights = jnp.exp(scores - (after - far))
            top[h : h + 1, :] = after
            total[h : h + 1, :] = total[h : h + 1, :] * scale + jnp.sum(weights, axis=0, keepdims=True)
            own = vt[kb, shift + h * HEAD : shift + (h + 1) * HEAD, :]
            at = slice(h * HEAD, (h + 1) * HEAD)
            ot[at, :] = ot[at, :] * scale + dot_nn(own, weights.astype(jnp.bfloat16))

    for_blocks(meta, rows, causal, query_base, key_base, step)
    for h in range(heads):
        at = slice(h * HEAD, (h + 1) * HEAD)
        out_ref[at, :] = (ot[at, :] / total[h : h + 1, :]).astype(jnp.bfloat16)
    lse_ref[...] = top[...] + jnp.log(total[...])


def attend(causal, heads, meta, u, queries, parts):
    rows, inner = queries.shape
    part_rows, lanes = parts[0].shape
    count = len(parts)
    length = part_rows * count
    smem = pl.BlockSpec(memory_space=pltpu.SMEM)
    vmem = pl.BlockSpec(memory_space=pltpu.VMEM)
    given = ([u] if causal else []) + [queries] + list(parts)
    scratch = [
        pltpu.VMEM((length, lanes), jnp.bfloat16),
        pltpu.VMEM((length, inner + HEAD), jnp.bfloat16),
        pltpu.VMEM((length // KEYS, WIDE, KEYS), jnp.bfloat16),
        pltpu.VMEM((rows, inner + HEAD), jnp.bfloat16),
        pltpu.VMEM((heads, rows, inner + HEAD), jnp.bfloat16),
        pltpu.VMEM((inner, rows), jnp.float32),
        pltpu.VMEM((8, rows), jnp.float32),
        pltpu.VMEM((8, rows), jnp.float32),
    ]
    if causal:
        scratch.append(pltpu.VMEM((heads, KEYS, 4 * KEYS), jnp.float32))
    return pl.pallas_call(
        functools.partial(forward_kernel, causal, heads, count),
        out_shape=(
            jax.ShapeDtypeStruct((inner, rows), jnp.bfloat16),
            jax.ShapeDtypeStruct((8, rows), jnp.float32),
        ),
        in_specs=[smem] + [vmem] * len(given),
        out_specs=(vmem, vmem),
        scratch_shapes=scratch,
        compiler_params=pltpu.CompilerParams(vmem_limit_bytes=30 * 1024 * 1024),
        cost_estimate=taking(13),
        name="self_forward" if causal else "cross_forward",
    )(meta, *given)


def fold_diagonals(values):
    half = values.shape[0] // 2
    while half >= 1:
        values = values[:half] + pltpu.roll(values[half : 2 * half], SPAN - half, 1)
        half = half // 2
    return values


def backward_kernel(causal, heads, count, branch_count, meta, *refs):
    if causal:
        u_ref = refs[0]
        refs = refs[1:]
    q_ref, out_weight, mixed_ref, lse_ref = refs[:4]
    parts, refs = refs[4 : 4 + count], refs[4 + count :]
    branches, refs = refs[:branch_count], refs[branch_count:]
    dq_ref = refs[0]
    keep_ref, send_ref, refs = refs[1], refs[2], refs[3:]
    if causal:
        dbias_ref = refs[0]
        refs = refs[1:]
    branch_ref = branches[0]
    kvs, kext, kt, qx, qm, dom, ra, rb, dqt, row, dkv, do_ref = refs[:12]
    query_base = 2
    key_base = 2 if causal else 2 + DOCS + 1
    rows, inner = q_ref.shape
    lanes = kvs.shape[1]
    do_ref[:, 0:inner] = jnp.zeros((rows, inner), jnp.bfloat16)
    do_ref[:, inner:] = dot_nt(branch_ref[...], out_weight[...]).astype(jnp.bfloat16)
    gather_blocks(meta, parts, kvs, kext, key_base)
    query_heads(meta, q_ref, qx, qm, heads, query_base)
    for kb in range(kvs.shape[0] // KEYS):
        kt[kb] = kvs[kb * KEYS : (kb + 1) * KEYS, 0:WIDE].T
    shift = WIDE - inner
    for h in range(heads):
        dom[h] = do_ref[:, lanes - WIDE :] * head_mask(WIDE, shift, h, None)
        ra[h * rows : (h + 1) * rows, :] = q_ext_only(qx, h, inner)
    ra[heads * rows :, :] = do_ref[:, 0:WIDE] * head_mask(WIDE, inner, 0, None)
    for h in range(1, heads):
        rb[(h - 1) * rows : h * rows, :] = do_ref[:, WIDE:] * head_mask(lanes - WIDE, inner - WIDE, h, None)
    turned = do_ref[:, lanes - WIDE :].astype(jnp.float32).T
    inner_sum = turned[shift:, :] * mixed_ref[...].astype(jnp.float32)
    for h in range(heads):
        row[h : h + 1, :] = jnp.sum(inner_sum[h * HEAD : (h + 1) * HEAD, :], axis=0, keepdims=True)
    dqt[...] = jnp.zeros_like(dqt)
    dkv[...] = jnp.zeros_like(dkv)
    if causal:
        tile, dtile, dfar = refs[12:15]
        bias_tiles(u_ref, tile, heads)
        dtile[...] = jnp.zeros_like(dtile)
        dfar[...] = jnp.zeros_like(dfar)

    def step(kb, place):
        at_keys = pl.ds(pl.multiple_of(kb * KEYS, KEYS), KEYS)
        kx = kext[at_keys, :]
        vx = kvs[at_keys, lanes - WIDE :]
        weights_low = []
        grads_low = []
        for h in range(heads):
            scores = dot_nt(kx, qm[h])
            lse = lse_ref[h : h + 1, :]
            if place is not None:
                scores = scores + tile[h, :, place : place + rows]
            elif causal:
                lse = lse - u_ref[h : h + 1, 4 * KEYS - 1 : 4 * KEYS]
            weights = jnp.exp(scores - lse)
            grad_weights = dot_nt(vx, dom[h])
            grads = weights * (grad_weights - row[h : h + 1, :])
            low = grads.astype(jnp.bfloat16)
            weights_low.append(weights.astype(jnp.bfloat16))
            grads_low.append(low)
            if causal:
                if place is not None:
                    dtile[h, :, place : place + rows] += low.astype(jnp.float32)
                else:
                    dfar[h : h + 1, :] += jnp.sum(low.astype(jnp.float32), axis=0, keepdims=True)
            at = slice(h * HEAD, (h + 1) * HEAD)
            dqt[at, :] += dot_nn(kt[kb, at, :], low)
        dkv[at_keys, 0:WIDE] = dot_nn(jnp.concatenate(grads_low + weights_low[:1], axis=1), ra[...]).astype(jnp.bfloat16)
        dkv[at_keys, WIDE:] = dot_nn(jnp.concatenate(weights_low[1:], axis=1), rb[...]).astype(jnp.bfloat16)

    for_blocks(meta, rows, causal, query_base, key_base, step)
    dq_ref[...] = dqt[...].astype(jnp.bfloat16)
    me = meta[1]
    part_rows = parts[0].shape[0]
    for r in range(count):
        at = pl.multiple_of(jnp.bitwise_xor(me, r) * part_rows, part_rows)
        to = (r // 2) * part_rows
        (send_ref if r % 2 else keep_ref)[to : to + part_rows, :] = dkv[pl.ds(at, part_rows), :]
    if causal:
        lane = lax.broadcasted_iota(jnp.int32, (1, SPAN), 1)
        dbias_ref[...] = jnp.zeros_like(dbias_ref)
        for h in range(heads):
            padded = jnp.concatenate([dtile[h], jnp.zeros((KEYS, SPAN - 4 * KEYS), jnp.float32)], axis=1)
            far = jnp.sum(dfar[h : h + 1, :], axis=1, keepdims=True)
            dbias_ref[h : h + 1, :] = fold_diagonals(padded) + jnp.where(lane == 4 * KEYS - 1, far, 0.0)


def q_ext_only(qx, head, inner):
    return qx[...] * head_mask(qx.shape[1], 0, head, None)


def attend_back(causal, heads, meta, u, queries, out_weight, mixed, lse, parts, branches):
    rows, inner = queries.shape
    part_rows, lanes = parts[0].shape
    count = len(parts)
    length = part_rows * count
    smem = pl.BlockSpec(memory_space=pltpu.SMEM)
    vmem = pl.BlockSpec(memory_space=pltpu.VMEM)
    given = ([u] if causal else []) + [queries, out_weight, mixed, lse] + list(parts) + list(branches)
    out_shape = [jax.ShapeDtypeStruct((inner, rows), jnp.bfloat16)]
    out_shape += [jax.ShapeDtypeStruct((length // 2, lanes), jnp.bfloat16)] * 2
    if causal:
        out_shape.append(jax.ShapeDtypeStruct((8, SPAN), jnp.float32))
    scratch = [
        pltpu.VMEM((length, lanes), jnp.bfloat16),
        pltpu.VMEM((length, inner + HEAD), jnp.bfloat16),
        pltpu.VMEM((length // KEYS, WIDE, KEYS), jnp.bfloat16),
        pltpu.VMEM((rows, inner + HEAD), jnp.bfloat16),
        pltpu.VMEM((heads, rows, inner + HEAD), jnp.bfloat16),
        pltpu.VMEM((heads, rows, WIDE), jnp.bfloat16),
        pltpu.VMEM(((heads + 1) * rows, WIDE), jnp.bfloat16),
        pltpu.VMEM(((heads - 1) * rows, lanes - WIDE), jnp.bfloat16),
        pltpu.VMEM((inner, rows), jnp.float32),
        pltpu.VMEM((8, rows), jnp.float32),
        pltpu.VMEM((length, lanes), jnp.bfloat16),
        pltpu.VMEM((rows, lanes), jnp.bfloat16),
    ]
    if causal:
        scratch += [
            pltpu.VMEM((heads, KEYS, 4 * KEYS), jnp.float32),
            pltpu.VMEM((heads, KEYS, 4 * KEYS), jnp.float32),
            pltpu.VMEM((8, rows), jnp.float32),
        ]
    return pl.pallas_call(
        functools.partial(backward_kernel, causal, heads, count, len(branches)),
        out_shape=tuple(out_shape),
        in_specs=[smem] + [vmem] * len(given),
        out_specs=tuple([vmem] * len(out_shape)),
        scratch_shapes=scratch,
        compiler_params=pltpu.CompilerParams(vmem_limit_bytes=30 * 1024 * 1024),
        cost_estimate=taking(19),
        name="self_backward" if causal else "cross_backward",
    )(meta, *given)


def position_rows(bias_table, heads):
    table = span_onehot()
    rows = jnp.dot(bias_table.astype(jnp.bfloat16).T, jnp.asarray(table.T, jnp.bfloat16), preferred_element_type=jnp.float32)
    rows = rows + jnp.asarray(np.where(table.sum(1) > 0, 0.0, MASKED)[None, :], jnp.float32)
    return jnp.concatenate([rows, jnp.zeros((8 - heads, SPAN), jnp.float32)], axis=0)


def make_meta(dec_row, enc_row, offset, place, rest):
    docs = jnp.arange(DOCS + 1, dtype=jnp.int32)
    dec = jnp.sum((dec_row[None, :] < docs[:, None]).astype(jnp.int32), axis=1)
    enc = jnp.sum((enc_row[None, :] < docs[:, None]).astype(jnp.int32), axis=1)
    first = jnp.stack([offset, place]).astype(jnp.int32)
    return jnp.concatenate([first, dec, enc, jnp.stack(rest).astype(jnp.int32)])


def room(*groups):
    total = 0
    for group in groups:
        for x in group:
            rows = int(np.prod(x.shape[:-1])) if x.shape else 1
            lanes = -(-x.shape[-1] // 128) * 128 if x.shape else 128
            total += max(rows, 8) * lanes * jnp.dtype(x.dtype).itemsize
    return 2 * total + 4 * 1024 * 1024


def onchip(kernel, name, out_shape, given, scratch=(), specs=None, cost=2):
    vmem = pl.BlockSpec(memory_space=pltpu.VMEM)
    in_specs = [pl.BlockSpec(memory_space=pltpu.SMEM)] + [vmem] * (len(given) - 1)
    for at, spec in (specs or {}).items():
        in_specs[at] = spec
    return pl.pallas_call(
        kernel,
        grid=(1,) if specs else (),
        out_shape=tuple(out_shape),
        in_specs=in_specs,
        out_specs=tuple([vmem] * len(out_shape)),
        scratch_shapes=list(scratch),
        compiler_params=pltpu.CompilerParams(vmem_limit_bytes=room(out_shape, given, scratch)),
        cost_estimate=taking(cost),
        name=name,
    )(*given)


def shape_of(rows, columns, kind):
    return jax.ShapeDtypeStruct((rows, columns), kind)


F32 = jnp.float32
LOW = jnp.bfloat16
AT_SLOT = 2 + 2 * (DOCS + 1)
AT_ODD = AT_SLOT + 1
AT_HALF = AT_SLOT + 2
AT_QUARTER = AT_SLOT + 3
AT_DP = AT_SLOT + 4
AT_FAR = AT_SLOT + 5


def plain_of(values):
    scale = lax.rsqrt(jnp.mean(values * values, axis=-1, keepdims=True) + EPSILON)
    return values * scale, scale


def input_gradient(grad_normed, plain, scale, gain):
    grad_plain = grad_normed * gain
    inner = jnp.mean(grad_plain * plain, axis=-1, keepdims=True)
    return scale * (grad_plain - plain * inner)


def sides_kernel(meta, x_ref, gain_ref, k_ref, v_ref, normed_ref, out_ref):
    plain, _ = plain_of(x_ref[...].astype(F32))
    normed = (plain * gain_ref[...].astype(F32)).astype(LOW)
    normed_ref[...] = normed
    out_ref[...] = dot_nt(normed, jnp.concatenate([k_ref[...], v_ref[...]], axis=0)).astype(LOW)


def others_kernel(meta, normed_ref, q_ref, enc_ref, k_ref, v_ref, out_ref, sides_ref):
    out_ref[...] = dot_nt(normed_ref[...], q_ref[...]).astype(LOW)
    sides_ref[...] = dot_nt(enc_ref[...], jnp.concatenate([k_ref[...], v_ref[...]], axis=0)).astype(LOW)


def weights_kernel(count, meta, own_ref, other_ref, *outs):
    parts = 4
    rows = outs[0].shape[0] // (count * parts)
    for side, ref in enumerate((own_ref, other_ref)):
        for b in range(2):
            part = 2 * jnp.bitwise_xor(meta[AT_ODD], side) + jnp.bitwise_xor(meta[AT_DP], b)
            for r in range(count):
                shard = jnp.bitwise_xor(meta[AT_SLOT], r)
                to = pl.multiple_of((shard * parts + part) * rows, rows)
                for w, out in enumerate(outs):
                    at = ((b * count + r) * len(outs) + w) * rows
                    out[pl.ds(to, rows), :] = ref[at : at + rows, :]


def pieces_kernel(meta, *refs):
    half = len(refs) // 2
    for weight, out in zip(refs[:half], refs[half:]):
        rows = out.shape[0]
        at = pl.multiple_of((2 * meta[AT_ODD] + meta[AT_DP]) * rows, rows)
        out[...] = weight[pl.ds(at, rows), :]


def lay_blocks(meta, blocks, whole):
    rows = blocks[0].shape[0]
    for r, block in enumerate(blocks):
        at = pl.multiple_of(jnp.bitwise_xor(meta[AT_SLOT], r) * rows, rows)
        whole[pl.ds(at, rows), :] = block[...]


def deal_blocks(meta, whole, blocks):
    rows = blocks[0].shape[0]
    for r, block in enumerate(blocks):
        at = pl.multiple_of(jnp.bitwise_xor(meta[AT_SLOT], r) * rows, rows)
        block[...] = whole[pl.ds(at, rows), :].astype(block.dtype)


def cross_entry_kernel(count, meta, x_ref, *refs):
    mixed, weight, gain_ref, q_ref, after_ref, normed_ref, out_ref = refs
    after = x_ref[...].astype(F32) + dot_nn(mixed[...].T, weight[...])
    after_ref[...] = after
    plain, _ = plain_of(after)
    normed = (plain * gain_ref[...].astype(F32)).astype(LOW)
    normed_ref[...] = normed
    out_ref[...] = dot_nt(normed, q_ref[...]).astype(LOW)


def feed_kernel(count, meta, after_ref, mixed, weight, gain_ref, up_ref, down_ref, grad_ref, *refs):
    rows_ref, normed_ref, active_ref, pre_ref, gain_grad_ref = refs[:5]
    dealt = refs[5 : 5 + count]
    part, total = refs[5 + count :]
    total[...] = after_ref[...] + dot_nn(mixed[...].T, weight[...])
    deal_blocks(meta, total, [rows_ref])
    plain, _ = plain_of(total[...])
    normed = (plain * gain_ref[...].astype(F32)).astype(LOW)
    normed_ref[...] = normed
    pre = dot_nn(normed, up_ref[...])
    squared = pre * pre
    bent = jnp.tanh(CURVE_SCALE * pre * (1.0 + CUBIC_TERM * squared))
    active_ref[...] = (0.5 * pre * (1.0 + bent)).astype(LOW)
    slope = 0.5 * (1.0 + bent) + 0.5 * pre * (1.0 - bent * bent) * CURVE_SCALE * (
        1.0 + 3.0 * CUBIC_TERM * squared
    )
    grad_pre = (dot_nt(grad_ref[...], down_ref[...]) * slope).astype(LOW)
    pre_ref[...] = grad_pre
    part[...] = dot_nt(grad_pre, up_ref[...])
    deal_blocks(meta, part, dealt)
    gain_grad_ref[...] = jnp.broadcast_to(
        jnp.sum(part[...] * plain, axis=0, keepdims=True), gain_grad_ref.shape
    )


def feed_back_kernel(count, meta, rows_ref, grad_ref, gain_ref, *refs):
    blocks, out_ref = refs[:count], refs[count]
    grad = blocks[0][...].astype(F32)
    for block in blocks[1:]:
        grad = grad + block[...].astype(F32)
    plain, scale = plain_of(rows_ref[...])
    rows = rows_ref.shape[0]
    own = grad_ref[pl.ds(pl.multiple_of(meta[AT_SLOT] * rows, rows), rows), :].astype(F32)
    out_ref[...] = (own + input_gradient(grad, plain, scale, gain_ref[...].astype(F32))).astype(LOW)


def layer_kernel(count, meta, active_ref, down_ref, *refs):
    dealt, part = refs[:count], refs[count]
    part[...] = dot_nn(active_ref[...], down_ref[...])
    deal_blocks(meta, part, dealt)


def far_kernel(meta, keep_ref, add_ref, out_ref):
    rows = out_ref.shape[0]
    out_ref[...] = (keep_ref[rows:, :].astype(F32) + add_ref[rows:, :].astype(F32)).astype(LOW)


def encoder_kernel(count, meta, keep_ref, add_ref, recv_ref, k_ref, v_ref, rows_ref, *refs):
    blocks, sides_ref, layer_ref = refs[:count], refs[count], refs[count + 1]
    dealt, part = refs[count + 2 : 2 * count + 2], refs[2 * count + 2]
    near = keep_ref.shape[0] // 2
    sides = (
        keep_ref[0:near, :].astype(F32) + add_ref[0:near, :].astype(F32) + recv_ref[...].astype(F32)
    ).astype(LOW)
    sides_ref[...] = sides
    part[...] = dot_nn(sides, jnp.concatenate([k_ref[...], v_ref[...]], axis=0))
    deal_blocks(meta, part, dealt)
    rows = rows_ref[...]
    for block in blocks:
        rows = rows + block[...].astype(F32)
    layer_ref[...] = rows.astype(LOW)


def self_entry_kernel(count, meta, after_ref, *refs):
    blocks, refs = refs[:count], refs[count:]
    weight, gain_ref, branch_ref, rows_ref, out_ref, gain_grad_ref, turned, total = refs
    lay_blocks(meta, blocks, turned)
    part = dot_nn(turned[...].T, weight[...])
    plain, scale = plain_of(after_ref[...])
    grad = branch_ref[...].astype(F32) + input_gradient(part, plain, scale, gain_ref[...].astype(F32))
    total[...] = grad
    out_ref[...] = grad.astype(LOW)
    deal_blocks(meta, total, [rows_ref])
    share = 1.0 / count
    gain_grad_ref[...] = jnp.broadcast_to(
        share * jnp.sum(part * plain, axis=0, keepdims=True), gain_grad_ref.shape
    )


def exit_kernel(count, meta, keep_ref, add_ref, recv_ref, dq_ref, q_ref, k_ref, v_ref, x_ref, g2_ref, g3_ref, *refs):
    sides_ref, dealt, part = refs[0], refs[1 : 1 + count], refs[1 + count]
    rows = keep_ref.shape[0] // 2
    sides = (
        keep_ref[0:rows, :].astype(F32) + add_ref[0:rows, :].astype(F32) + recv_ref[...].astype(F32)
    ).astype(LOW)
    sides_ref[...] = sides
    part[...] = dot_nn(dq_ref[...].T, q_ref[...]) + dot_nn(
        sides, jnp.concatenate([k_ref[...], v_ref[...]], axis=0)
    )
    plain, _ = plain_of(x_ref[...].astype(F32))
    first = jnp.sum(part[...] * plain, axis=0, keepdims=True)
    row = lax.broadcasted_iota(jnp.int32, (8, first.shape[1]), 0)
    gains = jnp.where(row == 0, first, jnp.where(row == 1, g2_ref[...], g3_ref[...]))
    high = gains.astype(LOW)
    rest = (gains - high.astype(F32)).astype(LOW)
    share = dealt[0].shape[0] - 16
    for r, out in enumerate(dealt):
        at = pl.multiple_of(jnp.bitwise_xor(meta[AT_SLOT], r) * share, share)
        out[0:share, :] = part[pl.ds(at, share), :].astype(LOW)
        out[share:, :] = jnp.concatenate([high, rest], axis=0)


def last_rows_kernel(count, meta, rows_ref, x_ref, gain_ref, *refs):
    blocks, pairs, out_ref, gains_ref = refs[:count], refs[count : 2 * count], refs[2 * count], refs[2 * count + 1]
    rows = rows_ref.shape[0]
    grad = blocks[0][...].astype(F32)
    for block in blocks[1:]:
        grad = grad + block[...].astype(F32)
    gains_ref[...] = grad[rows : rows + 8, :] + grad[rows + 8 :, :]
    own = x_ref[pl.ds(pl.multiple_of(meta[AT_SLOT] * rows, rows), rows), :].astype(F32)
    plain, scale = plain_of(own)
    out_ref[0:rows, :] = (
        rows_ref[...] + input_gradient(grad[0:rows, :], plain, scale, gain_ref[...].astype(F32))
    ).astype(LOW)
    total = pairs[0][...].astype(F32)
    for pair in pairs[1:]:
        total = total + pair[...].astype(F32)
    out_ref[rows:, :] = total.astype(LOW)


def layer_rows_kernel(count, meta, *refs):
    lay_blocks(meta, refs[:count], refs[count])


def pair_rows_kernel(count, meta, *refs):
    blocks, first_ref, second_ref = refs[:count], refs[count], refs[count + 1]
    rows = blocks[0].shape[0] // 2
    for r, block in enumerate(blocks):
        at = pl.multiple_of(jnp.bitwise_xor(meta[AT_SLOT], r) * rows, rows)
        first_ref[pl.ds(at, rows), :] = block[0:rows, :]
        second_ref[pl.ds(at, rows), :] = block[rows:, :]


def feed_weights_kernel(split, meta, normed_ref, pre_ref, active_ref, grad_ref, first_ref, second_ref):
    up = dot_nn(normed_ref[...].T, pre_ref[...]).astype(LOW)
    down = dot_nn(active_ref[...].T, grad_ref[...]).astype(LOW)
    if not split:
        first_ref[...] = up
        second_ref[...] = down
        return
    half = meta[AT_HALF]

    @pl.when(half == 0)
    def _():
        first_ref[...] = up
        second_ref[...] = down

    @pl.when(half == 1)
    def _():
        first_ref[...] = down
        second_ref[...] = up


def cross_weights_kernel(meta, dq_ref, normed_ref, sides_ref, enc_ref, mixed_cross_ref, branch_cross_ref, mixed_self_ref, branch_self_ref, out_ref):
    inner = dq_ref.shape[0]
    out_ref[0:inner, :] = dot_nn(dq_ref[...], normed_ref[...]).astype(LOW)
    out_ref[inner : 3 * inner, :] = dot_nn(sides_ref[...].T, enc_ref[...]).astype(LOW)
    out_ref[3 * inner : 4 * inner, :] = dot_nn(mixed_cross_ref[...], branch_cross_ref[...]).astype(LOW)
    out_ref[4 * inner :, :] = dot_nn(mixed_self_ref[...], branch_self_ref[...]).astype(LOW)


def payload_kernel(split, meta, cross_ref, normed_ref, dq_ref, sides_ref, bias_ref, hot_ref, *refs):
    outs, whole = refs[:-1], refs[-1]
    inner = dq_ref.shape[0]
    width = normed_ref.shape[1]
    at = 5 * inner
    whole[0:at, :] = cross_ref[...]
    whole[at : at + inner, :] = dot_nn(dq_ref[...], normed_ref[...]).astype(LOW)
    whole[at + inner : at + 3 * inner, :] = dot_nn(sides_ref[...].T, normed_ref[...]).astype(LOW)
    diagonal = bias_ref[...]
    high = diagonal.astype(LOW)
    rest = (diagonal - high.astype(F32)).astype(LOW)
    bias = dot_nn(high, hot_ref[...]) + dot_nn(rest, hot_ref[...])
    bias = jnp.concatenate([bias, jnp.zeros((8, width - bias.shape[1]), F32)], axis=1)
    at = at + 3 * inner
    whole[at : at + 16, :] = jnp.concatenate([bias, jnp.zeros_like(bias)], axis=0).astype(LOW)
    whole[at + 16 :, :] = jnp.zeros((whole.shape[0] - at - 16, width), LOW)
    if not split:
        outs[0][...] = whole[...]
        return
    rows = whole.shape[0] // 2
    half = meta[AT_HALF]
    outs[0][...] = whole[pl.ds(pl.multiple_of(half * rows, rows), rows), :]
    outs[1][...] = whole[pl.ds(pl.multiple_of((1 - half) * rows, rows), rows), :]


def quarter_kernel(meta, keep_ref, recv_ref, *refs):
    blocks, total = refs[:4], refs[4]
    total[...] = keep_ref[...].astype(F32) + recv_ref[...].astype(F32)
    rows = blocks[0].shape[0]
    for f in range(4):
        at = pl.multiple_of(jnp.bitwise_xor(meta[AT_QUARTER], f) * rows, rows)
        blocks[f][...] = total[pl.ds(at, rows), :].astype(LOW)


def halves_kernel(at_bit, meta, keep_ref, recv_ref, first_ref, second_ref, total):
    total[...] = keep_ref[...].astype(F32) + recv_ref[...].astype(F32)
    rows = first_ref.shape[0]
    bit = meta[at_bit]
    first_ref[...] = total[pl.ds(pl.multiple_of(bit * rows, rows), rows), :].astype(LOW)
    second_ref[...] = total[pl.ds(pl.multiple_of((1 - bit) * rows, rows), rows), :].astype(LOW)


def join_kernel(at_bit, meta, own_ref, other_ref, out_ref):
    rows = own_ref.shape[0]
    bit = meta[at_bit]
    out_ref[pl.ds(pl.multiple_of(bit * rows, rows), rows), :] = own_ref[...]
    out_ref[pl.ds(pl.multiple_of((1 - bit) * rows, rows), rows), :] = other_ref[...]


def feed_finish_kernel(split, meta, own_ref, other_ref, up_ref, down_ref):
    if not split:
        up_ref[...] = own_ref[...].astype(F32)
        down_ref[...] = other_ref[...].astype(F32)
        return

    @pl.when(meta[AT_HALF] == 0)
    def _():
        up_ref[...] = own_ref[...].astype(F32)
        down_ref[...] = other_ref[...].astype(F32)

    @pl.when(meta[AT_HALF] == 1)
    def _():
        up_ref[...] = other_ref[...].astype(F32)
        down_ref[...] = own_ref[...].astype(F32)


def own_kernel(meta, *refs):
    blocks, gains_ref, out_ref = refs[:4], refs[4], refs[5]
    rows = blocks[0].shape[0]
    total = blocks[0][...].astype(F32)
    for block in blocks[1:]:
        total = total + block[...].astype(F32)
    out_ref[0:rows, :] = total.astype(LOW)
    high = gains_ref[...].astype(LOW)
    rest = (gains_ref[...] - high.astype(F32)).astype(LOW)
    out_ref[rows:, :] = jnp.concatenate([high, rest], axis=0)


def finish_kernel(split, meta, *refs):
    count = 8 if split else 1
    parts, outs, whole = refs[:count], refs[count:-1], refs[-1]
    if split:
        outs, gains_ref = outs[:-1], outs[-1]
        rows = parts[0].shape[0] - 16
        gains = parts[0][rows:, :].astype(F32)
        for part in parts[1:]:
            gains = gains + part[rows:, :].astype(F32)
        gains_ref[...] = gains[0:8, :] + gains[8:, :]
        half = meta[AT_HALF]
        for i, part in enumerate(parts):
            side = half if i < 4 else 1 - half
            at = side * 4 * rows + jnp.bitwise_xor(meta[AT_QUARTER], i % 4) * rows
            whole[pl.ds(pl.multiple_of(at, rows), rows), :] = part[0:rows, :].astype(F32)
    else:
        whole[...] = parts[0][...].astype(F32)
    at = 0
    for out in outs:
        out[...] = whole[at : at + out.shape[0], :]
        at += out.shape[0]


def swap(values, axis, flip):
    count = lax.axis_size(axis)
    return lax.ppermute(values, axis, [(i, i ^ flip) for i in range(count)])


def swaps(values, axis):
    return [values] + [swap(values, axis, flip) for flip in range(1, lax.axis_size(axis))]


def trades(blocks, axis):
    return [blocks[0]] + [swap(block, axis, flip) for flip, block in enumerate(blocks) if flip]


def gather_rows(values, axis):
    return lax.all_gather(values, axis, axis=0, tiled=True)


def after(values, *others):
    return lax.optimization_barrier((values,) + others)[0]


def body(
    hidden_in,
    encoder_out,
    dec_segments,
    enc_segments,
    gain_self,
    gain_cross,
    gain_feed,
    self_query,
    self_key,
    self_value,
    self_output,
    bias_table,
    cross_query,
    cross_key,
    cross_value,
    cross_output,
    hidden_up,
    hidden_down,
    out_grad,
):
    tok_len, width = hidden_in.shape[1:]
    heads = bias_table.shape[1]
    inner = self_query.shape[1]
    place = lax.axis_index("ctx")
    slot = lax.axis_index("tensor")
    slots = lax.axis_size("tensor")
    split = lax.axis_size("dp") == 2 and lax.axis_size("ctx") == 4
    both = ("dp", "ctx")
    share = tok_len // slots
    lanes = 2 * inner
    odd = place & 1
    line = lax.axis_index("dp")
    combined = line * 4 + place
    meta = make_meta(
        dec_segments[0],
        enc_segments[0],
        place * tok_len,
        place,
        [slot, odd, combined & 1, (combined >> 1) & 3, line & 1, (place >> 1) & 1],
    )
    bias_rows = position_rows(bias_table, heads)
    tokens = hidden_in[0]
    encoded = encoder_out[0]
    cotangent = out_grad[0]
    gain_one = gain_self[None]
    gain_two = gain_cross[None]
    gain_three = gain_feed[None]
    rows_low = shape_of(tok_len, width, LOW)
    rows_full = shape_of(tok_len, width, F32)
    part_low = shape_of(share, width, LOW)
    part_full = shape_of(share, width, F32)
    sum_row = shape_of(8, width, F32)
    weight_low = shape_of(slots * inner, width, LOW)
    sides_low = shape_of(tok_len, lanes, LOW)
    mixed_room = pltpu.VMEM((slots * inner, tok_len), LOW)
    total_room = pltpu.VMEM((tok_len, width), F32)

    def send(block, flip):
        return lax.ppermute(block, both, [(i, i ^ flip) for i in range(8)])

    def add_halves(at_bit, keep, recv, name):
        rows, columns = keep.shape
        half = shape_of(rows // 2, columns, LOW)
        return onchip(
            functools.partial(halves_kernel, at_bit),
            name,
            [half, half],
            [meta, keep, recv],
            [pltpu.VMEM((rows, columns), F32)],
            cost=1,
        )

    def join(at_bit, own, other, name):
        rows, columns = own.shape
        return onchip(
            functools.partial(join_kernel, at_bit),
            name,
            [shape_of(2 * rows, columns, LOW)],
            [meta, own, other],
            cost=1,
        )[0]

    def far_sum(keep, add, name):
        return onchip(far_kernel, name, [sides_low], [meta, keep, add], cost=1)[0]

    self_query, self_key, self_value = self_query.T, self_key.T, self_value.T
    cross_query, cross_key, cross_value = cross_query.T, cross_key.T, cross_value.T

    def gather_plane(column):
        return jnp.concatenate([column, swap(column, "dp", 1)], axis=0)

    def lay_weights(plane, count, name):
        return onchip(
            functools.partial(weights_kernel, slots),
            name,
            [weight_low] * count,
            [meta, plane, swap(plane, "ctx", 1)],
            cost=1,
        )

    normed_self, own_sides = onchip(
        sides_kernel, "self_sides", [rows_low, sides_low], [meta, tokens, gain_one, self_key, self_value]
    )
    far_sides = swap(own_sides, "ctx", 2)
    pieces = onchip(
        pieces_kernel,
        "pieces",
        [shape_of(inner // 4, width, LOW)] * 3,
        [meta, self_output, cross_output, after(cross_query, own_sides)],
        cost=1,
    )
    self_pieces = swaps(pieces[0], "tensor")
    queries, own_cross = onchip(
        others_kernel,
        "query_and_cross_sides",
        [shape_of(tok_len, inner, LOW), sides_low],
        [meta, normed_self, self_query, encoded, cross_key, cross_value],
    )
    self_pieces, far_sides, own_cross = after((tuple(self_pieces), far_sides, own_cross), queries)
    cross_pieces = swaps(after(jnp.concatenate(pieces[1:], axis=0), *self_pieces), "tensor")
    column = jnp.concatenate(self_pieces, axis=0)
    far_column = swap(column, "dp", 1)
    sides = [own_sides, swap(own_sides, "ctx", 1), far_sides, swap(far_sides, "ctx", 1)]
    far_cross = swap(own_cross, "ctx", 2)
    mixed_self, lse_self = attend(True, heads, meta, bias_rows, queries, sides)
    mixed_self_in, far_column, far_cross, cross_pieces = after(
        (mixed_self, far_column, far_cross, tuple(cross_pieces)), lse_self
    )
    cross_sides = [own_cross, swap(own_cross, "ctx", 1), far_cross, swap(far_cross, "ctx", 1)]
    (self_output_all,) = lay_weights(jnp.concatenate([column, far_column], axis=0), 1, "self_weight")
    mixed_self_all = gather_rows(mixed_self_in, "tensor")
    after_self, normed_cross, cross_queries = onchip(
        functools.partial(cross_entry_kernel, slots),
        "cross_entry",
        [rows_full, rows_low, shape_of(tok_len, inner, LOW)],
        [meta, tokens, mixed_self_all, self_output_all, gain_two, cross_query],
        cost=2,
    )
    cross_column = jnp.concatenate(after(cross_pieces, cross_queries), axis=0)
    far_column = swap(cross_column, "dp", 1)
    mixed_cross, lse_cross = attend(False, heads, meta, None, cross_queries, cross_sides)
    mixed_cross_in, far_column = after((mixed_cross, far_column), lse_cross)
    cross_output_all, cross_query_all = lay_weights(
        jnp.concatenate([cross_column, far_column], axis=0), 2, "cross_weights_all"
    )
    fed = onchip(
        functools.partial(feed_kernel, slots),
        "feed",
        [part_full, rows_low, rows_low, rows_low, sum_row] + [part_low] * slots,
        [meta, after_self, gather_rows(mixed_cross_in, "tensor"), cross_output_all]
        + [gain_three, hidden_up, hidden_down, cotangent],
        [total_room, total_room],
        cost=4,
    )
    after_rows, normed_feed, active, grad_pre, gain_grad_feed = fed[:5]
    feed_blocks = trades(fed[5:], "tensor")
    feed_weights = onchip(
        functools.partial(feed_weights_kernel, split),
        "feed_weights",
        [shape_of(width, hidden_up.shape[1], LOW)] * 2,
        [meta, normed_feed, grad_pre, active, cotangent],
        cost=2,
    )
    layer_parts = onchip(
        functools.partial(layer_kernel, slots),
        "layer_parts",
        [part_low] * slots,
        [meta, active, hidden_down],
        [total_room],
        cost=1,
    )
    if split:
        by_line = add_halves(AT_DP, feed_weights[0], send(feed_weights[1], 1), "feed_line")
        feed_blocks, by_line = after((feed_blocks, tuple(by_line)), *layer_parts)
    (branch_rows,) = onchip(
        functools.partial(feed_back_kernel, slots),
        "feed_back",
        [part_low],
        [meta, after_rows, cotangent, gain_three] + list(feed_blocks),
        cost=1,
    )
    branch_cross = gather_rows(branch_rows, "tensor")
    if split:
        by_far = add_halves(AT_FAR, by_line[0], send(by_line[1], 4), "feed_far")
        branch_cross, by_far, layer_parts = after(
            (branch_cross, tuple(by_far), tuple(layer_parts)), branch_rows
        )
        far_recv = send(by_far[1], 2)
    layer_blocks = trades(after(tuple(layer_parts), branch_cross), "tensor")

    back = attend_back(
        False, heads, meta, None, cross_queries, cross_output, mixed_cross, lse_cross, cross_sides, [branch_cross]
    )
    grad_cross_q, keep, near = back
    if split:
        grad_cross_q, keep, near = after((grad_cross_q, keep, near), far_recv, *layer_blocks)
        feed_own = (by_far[0].astype(F32) + far_recv.astype(F32)).astype(LOW)
    else:
        grad_cross_q, keep, near = after((grad_cross_q, keep, near), *layer_blocks)
    near = swap(near, "ctx", 1)
    far = swap(far_sum(keep, near, "cross_far"), "ctx", 2)
    after_self_rows, branch_self, gain_grad_cross = onchip(
        functools.partial(self_entry_kernel, slots),
        "self_entry",
        [part_full, rows_low, sum_row],
        [meta, after_self]
        + swaps(grad_cross_q, "tensor")
        + [cross_query_all, gain_two, branch_cross],
        [mixed_room, total_room],
        cost=2,
    )
    encoded_out = onchip(
        functools.partial(encoder_kernel, slots),
        "encoder_parts",
        [sides_low, part_low] + [part_low] * slots,
        [meta, keep, near, far, cross_key, cross_value, after_rows] + layer_blocks,
        [total_room],
        cost=1,
    )
    grad_cross_sides, layer_rows = encoded_out[:2]
    branch_self = after(branch_self, encoded_out)
    encoder_blocks = trades(after(tuple(encoded_out[2:]), branch_self), "tensor")
    back = attend_back(
        True, heads, meta, bias_rows, queries, self_output, mixed_self, lse_self, sides, [branch_self]
    )
    grad_queries, keep, near, diagonals = back
    if split:
        feed_half = join(AT_FAR, feed_own, send(after(feed_own, branch_self), 2), "feed_half")
        grad_queries, keep, near, feed_half = after((grad_queries, keep, near, feed_half), *encoder_blocks)
        feed_most = join(AT_DP, feed_half, send(feed_half, 4), "feed_most")
    else:
        grad_queries, keep, near = after((grad_queries, keep, near), *encoder_blocks)
    near = swap(near, "ctx", 1)
    far = swap(far_sum(keep, near, "self_far"), "ctx", 2)
    layer_pieces = swaps(after(layer_rows, *encoder_blocks), "tensor")
    (cross_weights,) = onchip(
        cross_weights_kernel,
        "cross_weights",
        [shape_of(5 * inner, width, LOW)],
        [meta, grad_cross_q, normed_cross, grad_cross_sides, encoded, mixed_cross, branch_cross]
        + [mixed_self, branch_self],
        cost=2,
    )
    far, cross_weights = after((far, cross_weights), *layer_pieces, *([feed_most] if split else []))
    left = onchip(
        functools.partial(exit_kernel, slots),
        "self_exit",
        [sides_low] + [shape_of(share + 16, width, LOW)] * slots,
        [meta, keep, near, far, grad_queries, self_query, self_key, self_value, tokens]
        + [gain_grad_cross, gain_grad_feed],
        [total_room],
        cost=1,
    )
    grad_sides = left[0]
    last_rows, gains = onchip(
        functools.partial(last_rows_kernel, slots),
        "last_rows",
        [shape_of(2 * share, width, LOW), sum_row],
        [meta, after_self_rows, tokens, gain_one] + trades(left[1:], "tensor") + encoder_blocks,
        cost=1,
    )
    (layer_out,) = onchip(
        functools.partial(layer_rows_kernel, slots), "layer_rows", [rows_low], [meta] + layer_pieces
    )
    weight_rows = -(-(8 * inner + 16) // 128) * 128
    hot = jnp.asarray(np.pad(span_onehot(), ((0, 0), (0, 128 - BUCKETS))), LOW)
    payload = onchip(
        functools.partial(payload_kernel, split),
        "last_weights",
        [shape_of(weight_rows // 2, width, LOW)] * 2 if split else [shape_of(weight_rows, width, LOW)],
        [meta, cross_weights, normed_self, grad_queries, grad_sides, diagonals, hot],
        [pltpu.VMEM((weight_rows, width), LOW)],
        cost=2,
    )
    if split:
        rows = weight_rows // 8
        quarters = onchip(
            quarter_kernel,
            "quarters",
            [shape_of(rows, width, LOW)] * 4,
            [meta, payload[0], send(payload[1], 1)],
            [pltpu.VMEM((4 * rows, width), F32)],
            cost=1,
        )
        (own,) = onchip(
            own_kernel,
            "own_eighth",
            [shape_of(rows + 16, width, LOW)],
            [meta, quarters[0]] + [send(quarters[flip], 2 * flip) for flip in (1, 2, 3)] + [gains],
            cost=1,
        )
        summed = [own] + [send(own, 2 * flip) for flip in (1, 2, 3)]
        summed = summed + [send(block, 1) for block in summed]
        feed_summed = [feed_most, send(feed_most, 1)]
    else:
        summed = [lax.psum(payload[0], both)]
        feed_summed = list(lax.psum(tuple(feed_weights), both))
        gains = lax.psum(gains, both)
    grad_up, grad_down = onchip(
        functools.partial(feed_finish_kernel, split),
        "feed_finish",
        [shape_of(width, hidden_up.shape[1], F32)] * 2,
        [meta] + feed_summed,
        cost=3,
    )
    grad_hidden, grad_encoder = onchip(
        functools.partial(pair_rows_kernel, slots),
        "gathered_rows",
        [rows_low, rows_low],
        [meta] + swaps(last_rows, "tensor"),
        cost=2,
    )
    weights = onchip(
        functools.partial(finish_kernel, split),
        "finish",
        [shape_of(inner, width, F32)] * 8 + [shape_of(16, width, F32)] + [sum_row] * split,
        [meta] + summed,
        [pltpu.VMEM((weight_rows, width), F32)],
        cost=3,
    )
    if split:
        gains = weights[9]
    return (
        layer_out[None],
        grad_hidden[None],
        grad_encoder[None],
        gains[0],
        gains[1],
        gains[2],
        weights[5].T,
        weights[6].T,
        weights[7].T,
        weights[4],
        weights[8][:heads, :BUCKETS].T,
        weights[0].T,
        weights[1].T,
        weights[2].T,
        weights[3],
        grad_up,
        grad_down,
    )


def solution(mesh):
    rows = P("dp", "ctx", None)
    ids = P("dp", None)
    columns = P(None, "tensor")
    shards = P("tensor", None)
    placed = (
        (rows, rows, ids, ids, P(), P(), P())
        + (columns, columns, columns, shards, columns, columns, columns, columns, shards)
        + (columns, shards, rows)
    )
    given = (
        (rows, rows, rows, P(), P(), P())
        + (columns, columns, columns, shards, columns, columns, columns, columns, shards)
        + (columns, shards)
    )
    return jax.shard_map(body, mesh=mesh, in_specs=placed, out_specs=given, check_vma=False)
```

```python
import math
import functools
import numpy as np
import jax
import jax.numpy as jnp
from jax import lax
from jax.sharding import PartitionSpec as P
from jax.experimental import pallas as pl
from jax.experimental.pallas import tpu as pltpu

BUCKETS = 32
MAXDIST = 128
DOCS = 8
EPSILON = 1e-06
MASKED = -1000000000.0
MASK_WEIGHT = -float(2**30)
CURVE_SCALE = math.sqrt(2.0 / math.pi)
CUBIC_TERM = 0.044715
HIGHEST = lax.Precision.HIGHEST

HEAD = 64
KEYS = 256
WIDE = 256
SPAN = 1280
VMEM_BYTES = 60 * 1024 * 1024


def position_bucket(distance):
    exact_cut = BUCKETS // 2
    if distance < exact_cut:
        return distance
    scaled = math.log(distance / exact_cut) / math.log(MAXDIST / exact_cut) * (BUCKETS - exact_cut)
    return min(exact_cut + int(scaled), BUCKETS - 1)


def span_onehot():
    table = np.zeros((SPAN, BUCKETS), np.float32)
    for place in range(KEYS, KEYS + 3 * KEYS):
        table[place, position_bucket(place - KEYS)] = 1.0
    return table


def taking(microseconds):
    return pl.CostEstimate(flops=int(microseconds * 1e9), transcendentals=0, bytes_accessed=int(microseconds * 3.5e6))


def dot_nt(left, right):
    return lax.dot_general(left, right, (((1,), (1,)), ((), ())), preferred_element_type=jnp.float32)


def dot_nn(left, right):
    return lax.dot_general(left, right, (((1,), (0,)), ((), ())), preferred_element_type=jnp.float32)


def onehot_rows(count, first, meta, base):
    lane = lax.broadcasted_iota(jnp.int32, (1, HEAD), 1)
    low = jnp.zeros((1, HEAD), jnp.int32)
    high = jnp.zeros((1, HEAD), jnp.int32)
    for d in range(DOCS):
        low = jnp.where(lane == d, meta[base + d], low)
        high = jnp.where(lane == d, meta[base + d + 1], high)
    place = lax.broadcasted_iota(jnp.int32, (count, HEAD), 0) + first
    return (place >= low) & (place < high)


def head_mask(width, first, head, feature_from):
    lane = lax.broadcasted_iota(jnp.int32, (1, width), 1)
    start = first + head * HEAD
    keep = (lane >= start) & (lane < start + HEAD)
    if feature_from is not None:
        keep = keep | (lane >= feature_from)
    return keep.astype(jnp.float32).astype(jnp.bfloat16)


def gather_blocks(meta, parts, kvs, kext, key_base):
    rows = parts[0].shape[0]
    me = meta[1]
    inner = kext.shape[1] - HEAD
    for r, part in enumerate(parts):
        at = pl.multiple_of(jnp.bitwise_xor(me, r) * rows, rows)
        kvs[pl.ds(at, rows), :] = part[...]
        kext[pl.ds(at, rows), 0:inner] = part[:, 0:inner]
        kext[pl.ds(at, rows), inner:] = onehot_rows(rows, at, meta, key_base).astype(jnp.float32).astype(jnp.bfloat16)


def query_heads(meta, q_ref, qx, qm, heads, query_base):
    rows, inner = q_ref.shape
    own = onehot_rows(rows, meta[0], meta, query_base)
    qx[:, 0:inner] = q_ref[...]
    qx[:, inner:] = jnp.where(own, 0.0, MASK_WEIGHT).astype(jnp.bfloat16)
    for h in range(heads):
        qm[h] = qx[...] * head_mask(qx.shape[1], 0, h, inner)


def bias_tiles(u_ref, tile, heads):
    for h in range(heads):
        row = jnp.broadcast_to(u_ref[h : h + 1, :], (KEYS, SPAN))
        tile[h] = pltpu.roll(row, 0, 1, stride=1, stride_axis=0)[:, 0 : 4 * KEYS]


def key_range(meta, rows, query_base, key_base):
    first = meta[0]
    last = first + rows - 1
    low = meta[key_base]
    high = meta[key_base + 1]
    for d in range(1, DOCS):
        low = jnp.where(meta[query_base + d] <= first, meta[key_base + d], low)
        high = jnp.where(meta[query_base + d] <= last, meta[key_base + d + 1], high)
    return lax.div(low, KEYS), lax.div(high + KEYS - 1, KEYS)


def for_blocks(meta, rows, causal, query_base, key_base, step, carry):
    low, high = key_range(meta, rows, query_base, key_base)
    if not causal:
        return lax.fori_loop(
            lax.div(low, 2), lax.div(high + 1, 2), lambda kb, c: step(2 * kb + 1, None, step(2 * kb, None, c)), carry
        )
    near = lax.div(meta[0], KEYS)
    carry = lax.fori_loop(
        lax.div(low, 2), lax.div(near, 2) - 1, lambda kb, c: step(2 * kb + 1, None, step(2 * kb, None, c)), carry
    )
    carry = lax.cond(
        near > 0, lambda c: step(near - 1, 2 * KEYS, step(near - 2, None, c)), lambda c: c, carry
    )
    carry = step(near, KEYS, carry)
    return step(near + 1, 0, carry)


def forward_kernel(causal, heads, count, meta, *refs):
    if causal:
        u_ref, q_ref = refs[0], refs[1]
        refs = refs[2:]
    else:
        q_ref = refs[0]
        refs = refs[1:]
    parts, refs = refs[:count], refs[count:]
    out_ref, lse_ref = refs[:2]
    refs = refs[2:]
    if causal:
        tile = refs[0]
        refs = refs[1:]
        bias_tiles(u_ref, tile, heads)
    kvs, kext, vt, qx, qm, ot = refs
    query_base = 2
    key_base = 2 if causal else 2 + DOCS + 1
    rows = q_ref.shape[0]
    gather_blocks(meta, parts, kvs, kext, key_base)
    query_heads(meta, q_ref, qx, qm, heads, query_base)
    lanes = kvs.shape[1]
    for kb in range(kvs.shape[0] // KEYS):
        vt[kb] = kvs[kb * KEYS : (kb + 1) * KEYS, lanes - WIDE :].T
    ot[...] = jnp.zeros_like(ot)
    shift = WIDE - heads * HEAD

    def step(kb, place, carry):
        kx = kext[pl.ds(pl.multiple_of(kb * KEYS, KEYS), KEYS), :]
        scores = [dot_nt(kx, qm[h]) for h in range(heads)]
        tops, sums = carry
        new_tops, new_sums = [], []
        for h in range(heads):
            far = 0.0
            if place is not None:
                scores[h] = scores[h] + tile[h, :, place : place + rows]
            elif causal:
                far = u_ref[h : h + 1, 4 * KEYS - 1 : 4 * KEYS]
            after = jnp.maximum(tops[h], jnp.max(scores[h], axis=0, keepdims=True) + far)
            scale = jnp.exp(tops[h] - after)
            weights = jnp.exp(scores[h] - (after - far))
            new_tops.append(after)
            new_sums.append(sums[h] * scale + jnp.sum(weights.reshape(KEYS // 8, 8, rows), axis=0))
            own = vt[kb, shift + h * HEAD : shift + (h + 1) * HEAD, :]
            at = slice(h * HEAD, (h + 1) * HEAD)
            ot[at, :] = ot[at, :] * scale + dot_nn(own, weights.astype(jnp.bfloat16))
        return new_tops, new_sums

    carry = (
        [jnp.full((1, rows), -3e38, jnp.float32)] * heads,
        [jnp.zeros((8, rows), jnp.float32)] * heads,
    )
    tops, sums = for_blocks(meta, rows, causal, query_base, key_base, step, carry)
    lse_ref[...] = jnp.zeros_like(lse_ref)
    for h in range(heads):
        at = slice(h * HEAD, (h + 1) * HEAD)
        total = jnp.sum(sums[h], axis=0, keepdims=True)
        out_ref[at, :] = (ot[at, :] / total).astype(jnp.bfloat16)
        lse_ref[h : h + 1, :] = tops[h] + jnp.log(total)


def attend(causal, heads, meta, u, queries, parts):
    rows, inner = queries.shape
    part_rows, lanes = parts[0].shape
    count = len(parts)
    length = part_rows * count
    smem = pl.BlockSpec(memory_space=pltpu.SMEM)
    vmem = pl.BlockSpec(memory_space=pltpu.VMEM)
    given = ([u] if causal else []) + [queries] + list(parts)
    scratch = [
        pltpu.VMEM((length, lanes), jnp.bfloat16),
        pltpu.VMEM((length, inner + HEAD), jnp.bfloat16),
        pltpu.VMEM((length // KEYS, WIDE, KEYS), jnp.bfloat16),
        pltpu.VMEM((rows, inner + HEAD), jnp.bfloat16),
        pltpu.VMEM((heads, rows, inner + HEAD), jnp.bfloat16),
        pltpu.VMEM((inner, rows), jnp.float32),
    ]
    out_shape = [
        jax.ShapeDtypeStruct((inner, rows), jnp.bfloat16),
        jax.ShapeDtypeStruct((8, rows), jnp.float32),
    ]
    if causal:
        out_shape.append(jax.ShapeDtypeStruct((heads, KEYS, 4 * KEYS), jnp.float32))
    return pl.pallas_call(
        functools.partial(forward_kernel, causal, heads, count),
        out_shape=tuple(out_shape),
        in_specs=[smem] + [vmem] * len(given),
        out_specs=tuple([vmem] * len(out_shape)),
        scratch_shapes=scratch,
        compiler_params=pltpu.CompilerParams(vmem_limit_bytes=30 * 1024 * 1024),
        cost_estimate=taking(9),
        name="self_forward" if causal else "cross_forward",
    )(meta, *given)


def fold_diagonals(values):
    half = values.shape[0] // 2
    while half >= 1:
        values = values[:half] + pltpu.roll(values[half : 2 * half], SPAN - half, 1)
        half = half // 2
    return values


def backward_kernel(causal, heads, count, branch_count, meta, *refs):
    if causal:
        u_ref, tile = refs[:2]
        refs = refs[2:]
    q_ref, out_weight, mixed_ref, lse_ref = refs[:4]
    parts, refs = refs[4 : 4 + count], refs[4 + count :]
    branches, refs = refs[:branch_count], refs[branch_count:]
    dq_ref = refs[0]
    keep_ref, send_ref, refs = refs[1], refs[2], refs[3:]
    if causal:
        dbias_ref = refs[0]
        refs = refs[1:]
    branch_ref = branches[0]
    kvs, kext, kt, qx, qm, dom, ra, rb, dqt, row, dkv, do_ref = refs[:12]
    query_base = 2
    key_base = 2 if causal else 2 + DOCS + 1
    rows, inner = q_ref.shape
    lanes = kvs.shape[1]
    do_ref[:, 0:inner] = jnp.zeros((rows, inner), jnp.bfloat16)
    do_ref[:, inner:] = dot_nt(branch_ref[...], out_weight[...]).astype(jnp.bfloat16)
    gather_blocks(meta, parts, kvs, kext, key_base)
    query_heads(meta, q_ref, qx, qm, heads, query_base)
    for kb in range(kvs.shape[0] // KEYS):
        kt[kb] = kvs[kb * KEYS : (kb + 1) * KEYS, 0:WIDE].T
    shift = WIDE - inner
    for h in range(heads):
        dom[h] = do_ref[:, lanes - WIDE :] * head_mask(WIDE, shift, h, None)
        ra[h * rows : (h + 1) * rows, :] = q_ext_only(qx, h, inner)
    ra[heads * rows :, :] = do_ref[:, 0:WIDE] * head_mask(WIDE, inner, 0, None)
    for h in range(1, heads):
        rb[(h - 1) * rows : h * rows, :] = do_ref[:, WIDE:] * head_mask(lanes - WIDE, inner - WIDE, h, None)
    turned = do_ref[:, lanes - WIDE :].astype(jnp.float32).T
    inner_sum = turned[shift:, :] * mixed_ref[...].astype(jnp.float32)
    for h in range(heads):
        row[h : h + 1, :] = jnp.sum(inner_sum[h * HEAD : (h + 1) * HEAD, :], axis=0, keepdims=True)
    dqt[...] = jnp.zeros_like(dqt)
    dkv[...] = jnp.zeros_like(dkv)
    if causal:
        dtile, dfar = refs[12:14]
        dtile[...] = jnp.zeros_like(dtile)
        dfar[...] = jnp.zeros_like(dfar)

    def step(kb, place):
        at_keys = pl.ds(pl.multiple_of(kb * KEYS, KEYS), KEYS)
        kx = kext[at_keys, :]
        vx = kvs[at_keys, lanes - WIDE :]
        weights_low = []
        grads_low = []
        all_scores = [dot_nt(kx, qm[h]) for h in range(heads)]
        all_grads = [dot_nt(vx, dom[h]) for h in range(heads)]
        for h in range(heads):
            scores = all_scores[h]
            lse = lse_ref[h : h + 1, :]
            if place is not None:
                scores = scores + tile[h, :, place : place + rows]
            elif causal:
                lse = lse - u_ref[h : h + 1, 4 * KEYS - 1 : 4 * KEYS]
            weights = jnp.exp(scores - lse)
            grads = weights * (all_grads[h] - row[h : h + 1, :])
            low = grads.astype(jnp.bfloat16)
            weights_low.append(weights.astype(jnp.bfloat16))
            grads_low.append(low)
            if causal:
                if place is not None:
                    dtile[h, :, place : place + rows] += grads
                else:
                    dfar[8 * h : 8 * h + 8, :] += jnp.sum(grads.reshape(KEYS // 8, 8, rows), axis=0)
        for h in range(heads):
            at = slice(h * HEAD, (h + 1) * HEAD)
            dqt[at, :] += dot_nn(kt[kb, at, :], grads_low[h])
        dkv[at_keys, 0:WIDE] = dot_nn(jnp.concatenate(grads_low + weights_low[:1], axis=1), ra[...]).astype(jnp.bfloat16)
        dkv[at_keys, WIDE:] = dot_nn(jnp.concatenate(weights_low[1:], axis=1), rb[...]).astype(jnp.bfloat16)

    for_blocks(meta, rows, causal, query_base, key_base, lambda kb, place, c: (step(kb, place), c)[1], 0)
    dq_ref[...] = dqt[...].astype(jnp.bfloat16)
    me = meta[1]
    part_rows = parts[0].shape[0]
    for r in range(count):
        at = pl.multiple_of(jnp.bitwise_xor(me, r) * part_rows, part_rows)
        to = (r // 2) * part_rows
        (send_ref if r % 2 else keep_ref)[to : to + part_rows, :] = dkv[pl.ds(at, part_rows), :]
    if causal:
        lane = lax.broadcasted_iota(jnp.int32, (1, SPAN), 1)
        dbias_ref[...] = jnp.zeros_like(dbias_ref)
        for h in range(heads):
            padded = jnp.concatenate([dtile[h], jnp.zeros((KEYS, SPAN - 4 * KEYS), jnp.float32)], axis=1)
            far = jnp.sum(jnp.sum(dfar[8 * h : 8 * h + 8, :], axis=0, keepdims=True), axis=1, keepdims=True)
            dbias_ref[h : h + 1, :] = fold_diagonals(padded) + jnp.where(lane == 4 * KEYS - 1, far, 0.0)


def q_ext_only(qx, head, inner):
    return qx[...] * head_mask(qx.shape[1], 0, head, None)


def attend_back(causal, heads, meta, u, queries, out_weight, mixed, lse, parts, branches):
    rows, inner = queries.shape
    part_rows, lanes = parts[0].shape
    count = len(parts)
    length = part_rows * count
    smem = pl.BlockSpec(memory_space=pltpu.SMEM)
    vmem = pl.BlockSpec(memory_space=pltpu.VMEM)
    given = list(u) + [queries, out_weight, mixed, lse] + list(parts) + list(branches)
    out_shape = [jax.ShapeDtypeStruct((inner, rows), jnp.bfloat16)]
    out_shape += [jax.ShapeDtypeStruct((length // 2, lanes), jnp.bfloat16)] * 2
    if causal:
        out_shape.append(jax.ShapeDtypeStruct((8, SPAN), jnp.float32))
    scratch = [
        pltpu.VMEM((length, lanes), jnp.bfloat16),
        pltpu.VMEM((length, inner + HEAD), jnp.bfloat16),
        pltpu.VMEM((length // KEYS, WIDE, KEYS), jnp.bfloat16),
        pltpu.VMEM((rows, inner + HEAD), jnp.bfloat16),
        pltpu.VMEM((heads, rows, inner + HEAD), jnp.bfloat16),
        pltpu.VMEM((heads, rows, WIDE), jnp.bfloat16),
        pltpu.VMEM(((heads + 1) * rows, WIDE), jnp.bfloat16),
        pltpu.VMEM(((heads - 1) * rows, lanes - WIDE), jnp.bfloat16),
        pltpu.VMEM((inner, rows), jnp.float32),
        pltpu.VMEM((8, rows), jnp.float32),
        pltpu.VMEM((length, lanes), jnp.bfloat16),
        pltpu.VMEM((rows, lanes), jnp.bfloat16),
    ]
    if causal:
        scratch += [
            pltpu.VMEM((heads, KEYS, 4 * KEYS), jnp.float32),
            pltpu.VMEM((8 * heads, rows), jnp.float32),
        ]
    return pl.pallas_call(
        functools.partial(backward_kernel, causal, heads, count, len(branches)),
        out_shape=tuple(out_shape),
        in_specs=[smem] + [vmem] * len(given),
        out_specs=tuple([vmem] * len(out_shape)),
        scratch_shapes=scratch,
        compiler_params=pltpu.CompilerParams(vmem_limit_bytes=30 * 1024 * 1024),
        cost_estimate=taking(13),
        name="self_backward" if causal else "cross_backward",
    )(meta, *given)


def position_rows(bias_table, heads):
    table = span_onehot()
    rows = jnp.dot(bias_table.astype(jnp.bfloat16).T, jnp.asarray(table.T, jnp.bfloat16), preferred_element_type=jnp.float32)
    rows = rows + jnp.asarray(np.where(table.sum(1) > 0, 0.0, MASKED)[None, :], jnp.float32)
    return jnp.concatenate([rows, jnp.zeros((8 - heads, SPAN), jnp.float32)], axis=0)


def make_meta(dec_row, enc_row, offset, place, rest):
    docs = jnp.arange(DOCS + 1, dtype=jnp.int32)
    dec = jnp.sum((dec_row[None, :] < docs[:, None]).astype(jnp.int32), axis=1)
    enc = jnp.sum((enc_row[None, :] < docs[:, None]).astype(jnp.int32), axis=1)
    first = jnp.stack([offset, place]).astype(jnp.int32)
    return jnp.concatenate([first, dec, enc, jnp.stack(rest).astype(jnp.int32)])


def room(*groups):
    total = 0
    for group in groups:
        for x in group:
            rows = int(np.prod(x.shape[:-1])) if x.shape else 1
            lanes = -(-x.shape[-1] // 128) * 128 if x.shape else 128
            total += max(rows, 8) * lanes * jnp.dtype(x.dtype).itemsize
    return 2 * total + 4 * 1024 * 1024


def onchip(kernel, name, out_shape, given, scratch=(), cost=2, table=True):
    vmem = pl.BlockSpec(memory_space=pltpu.VMEM)
    in_specs = [pl.BlockSpec(memory_space=pltpu.SMEM)] + [vmem] * (len(given) - 1)
    if not table:
        in_specs = [vmem] * len(given)
    return pl.pallas_call(
        kernel,
        out_shape=tuple(out_shape),
        in_specs=in_specs,
        out_specs=tuple([vmem] * len(out_shape)),
        scratch_shapes=list(scratch),
        compiler_params=pltpu.CompilerParams(vmem_limit_bytes=room(out_shape, given, scratch)),
        cost_estimate=taking(cost),
        name=name,
    )(*given)


def shape_of(rows, columns, kind):
    return jax.ShapeDtypeStruct((rows, columns), kind)


F32 = jnp.float32
LOW = jnp.bfloat16
AT_SLOT = 2 + 2 * (DOCS + 1)
AT_ODD = AT_SLOT + 1
AT_HALF = AT_SLOT + 2
AT_QUARTER = AT_SLOT + 3
AT_DP = AT_SLOT + 4
AT_FAR = AT_SLOT + 5


def plain_of(values):
    scale = lax.rsqrt(jnp.mean(values * values, axis=-1, keepdims=True) + EPSILON)
    return values * scale, scale


def input_gradient(grad_normed, plain, scale, gain):
    grad_plain = grad_normed * gain
    inner = jnp.mean(grad_plain * plain, axis=-1, keepdims=True)
    return scale * (grad_plain - plain * inner)


def sides_kernel(x_ref, gain_ref, k_ref, v_ref, normed_ref, out_ref):
    plain, _ = plain_of(x_ref[...].astype(F32))
    normed = (plain * gain_ref[...].astype(F32)).astype(LOW)
    normed_ref[...] = normed
    out_ref[...] = dot_nt(normed, jnp.concatenate([k_ref[...], v_ref[...]], axis=0)).astype(LOW)


def others_kernel(normed_ref, q_ref, enc_ref, k_ref, v_ref, out_ref, sides_ref):
    out_ref[...] = dot_nt(normed_ref[...], q_ref[...]).astype(LOW)
    sides_ref[...] = dot_nt(enc_ref[...], jnp.concatenate([k_ref[...], v_ref[...]], axis=0)).astype(LOW)


def weights_kernel(count, meta, own_ref, other_ref, *outs):
    parts = 4
    rows = outs[0].shape[0] // (count * parts)
    for side, ref in enumerate((own_ref, other_ref)):
        for b in range(2):
            part = 2 * jnp.bitwise_xor(meta[AT_ODD], side) + jnp.bitwise_xor(meta[AT_DP], b)
            for r in range(count):
                shard = jnp.bitwise_xor(meta[AT_SLOT], r)
                to = pl.multiple_of((shard * parts + part) * rows, rows)
                for w, out in enumerate(outs):
                    at = ((b * count + r) * len(outs) + w) * rows
                    out[pl.ds(to, rows), :] = ref[at : at + rows, :]


def pieces_kernel(meta, *refs):
    half = len(refs) // 2
    for weight, out in zip(refs[:half], refs[half:]):
        rows = out.shape[0]
        at = pl.multiple_of((2 * meta[AT_ODD] + meta[AT_DP]) * rows, rows)
        out[...] = weight[pl.ds(at, rows), :]


def lay_blocks(meta, blocks, whole):
    rows = blocks[0].shape[0]
    for r, block in enumerate(blocks):
        at = pl.multiple_of(jnp.bitwise_xor(meta[AT_SLOT], r) * rows, rows)
        whole[pl.ds(at, rows), :] = block[...]


def deal_blocks(meta, whole, blocks):
    rows = blocks[0].shape[0]
    for r, block in enumerate(blocks):
        at = pl.multiple_of(jnp.bitwise_xor(meta[AT_SLOT], r) * rows, rows)
        block[...] = whole[pl.ds(at, rows), :].astype(block.dtype)


def cross_entry_kernel(count, meta, x_ref, *refs):
    mixed, weight, gain_ref, q_ref, after_ref, normed_ref, out_ref = refs
    after = x_ref[...].astype(F32) + dot_nn(mixed[...].T, weight[...])
    after_ref[...] = after
    plain, _ = plain_of(after)
    normed = (plain * gain_ref[...].astype(F32)).astype(LOW)
    normed_ref[...] = normed
    out_ref[...] = dot_nt(normed, q_ref[...]).astype(LOW)


def feed_kernel(count, meta, after_ref, mixed, weight, gain_ref, up_ref, down_ref, grad_ref, *refs):
    rows_ref, normed_ref, active_ref, pre_ref, gain_grad_ref = refs[:5]
    dealt = refs[5 : 5 + count]
    part, total = refs[5 + count :]
    total[...] = after_ref[...] + dot_nn(mixed[...].T, weight[...])
    deal_blocks(meta, total, [rows_ref])
    plain, _ = plain_of(total[...])
    normed = (plain * gain_ref[...].astype(F32)).astype(LOW)
    normed_ref[...] = normed
    pre = dot_nn(normed, up_ref[...])
    squared = pre * pre
    bent = jnp.tanh(CURVE_SCALE * pre * (1.0 + CUBIC_TERM * squared))
    active_ref[...] = (0.5 * pre * (1.0 + bent)).astype(LOW)
    slope = 0.5 * (1.0 + bent) + 0.5 * pre * (1.0 - bent * bent) * CURVE_SCALE * (
        1.0 + 3.0 * CUBIC_TERM * squared
    )
    grad_pre = (dot_nt(grad_ref[...], down_ref[...]) * slope).astype(LOW)
    pre_ref[...] = grad_pre
    part[...] = dot_nt(grad_pre, up_ref[...])
    deal_blocks(meta, part, dealt)
    gain_grad_ref[...] = jnp.broadcast_to(
        jnp.sum(part[...] * plain, axis=0, keepdims=True), gain_grad_ref.shape
    )


def feed_back_kernel(count, meta, rows_ref, grad_ref, gain_ref, *refs):
    blocks, out_ref = refs[:count], refs[count]
    grad = blocks[0][...].astype(F32)
    for block in blocks[1:]:
        grad = grad + block[...].astype(F32)
    plain, scale = plain_of(rows_ref[...])
    rows = rows_ref.shape[0]
    own = grad_ref[pl.ds(pl.multiple_of(meta[AT_SLOT] * rows, rows), rows), :].astype(F32)
    out_ref[...] = (own + input_gradient(grad, plain, scale, gain_ref[...].astype(F32))).astype(LOW)


def layer_kernel(count, meta, active_ref, down_ref, *refs):
    dealt, part = refs[:count], refs[count]
    part[...] = dot_nn(active_ref[...], down_ref[...])
    deal_blocks(meta, part, dealt)


def far_kernel(meta, keep_ref, add_ref, out_ref):
    rows = out_ref.shape[0]
    out_ref[...] = (keep_ref[rows:, :].astype(F32) + add_ref[rows:, :].astype(F32)).astype(LOW)


def encoder_kernel(count, meta, keep_ref, add_ref, recv_ref, k_ref, v_ref, *refs):
    sides_ref, dealt, part = refs[0], refs[1 : count + 1], refs[count + 1]
    near = keep_ref.shape[0] // 2
    sides = (
        keep_ref[0:near, :].astype(F32) + add_ref[0:near, :].astype(F32) + recv_ref[...].astype(F32)
    ).astype(LOW)
    sides_ref[...] = sides
    part[...] = dot_nn(sides, jnp.concatenate([k_ref[...], v_ref[...]], axis=0))
    deal_blocks(meta, part, dealt)


def layer_sum_kernel(count, meta, rows_ref, *refs):
    blocks, out_ref = refs[:count], refs[count]
    rows = rows_ref[...]
    for block in blocks:
        rows = rows + block[...].astype(F32)
    out_ref[...] = rows.astype(LOW)


def self_entry_kernel(count, meta, after_ref, *refs):
    turned, weight, gain_ref, branch_ref, rows_ref, out_ref, gain_grad_ref, total = refs
    part = dot_nn(turned[...].T, weight[...])
    plain, scale = plain_of(after_ref[...])
    grad = branch_ref[...].astype(F32) + input_gradient(part, plain, scale, gain_ref[...].astype(F32))
    total[...] = grad
    out_ref[...] = grad.astype(LOW)
    deal_blocks(meta, total, [rows_ref])
    share = 1.0 / count
    gain_grad_ref[...] = jnp.broadcast_to(
        share * jnp.sum(part * plain, axis=0, keepdims=True), gain_grad_ref.shape
    )


def exit_kernel(count, meta, keep_ref, add_ref, recv_ref, dq_ref, q_ref, k_ref, v_ref, x_ref, g2_ref, g3_ref, *refs):
    sides_ref, dealt, part = refs[0], refs[1 : 1 + count], refs[1 + count]
    rows = keep_ref.shape[0] // 2
    sides = (
        keep_ref[0:rows, :].astype(F32) + add_ref[0:rows, :].astype(F32) + recv_ref[...].astype(F32)
    ).astype(LOW)
    sides_ref[...] = sides
    part[...] = dot_nn(dq_ref[...].T, q_ref[...]) + dot_nn(
        sides, jnp.concatenate([k_ref[...], v_ref[...]], axis=0)
    )
    plain, _ = plain_of(x_ref[...].astype(F32))
    first = jnp.sum(part[...] * plain, axis=0, keepdims=True)
    row = lax.broadcasted_iota(jnp.int32, (8, first.shape[1]), 0)
    gains = jnp.where(row == 0, first, jnp.where(row == 1, g2_ref[...], g3_ref[...]))
    high = gains.astype(LOW)
    rest = (gains - high.astype(F32)).astype(LOW)
    share = dealt[0].shape[0] - 16
    for r, out in enumerate(dealt):
        at = pl.multiple_of(jnp.bitwise_xor(meta[AT_SLOT], r) * share, share)
        out[0:share, :] = part[pl.ds(at, share), :].astype(LOW)
        out[share:, :] = jnp.concatenate([high, rest], axis=0)


def last_rows_kernel(count, meta, rows_ref, x_ref, gain_ref, *refs):
    blocks, pairs = refs[:count], refs[count : 2 * count]
    out_ref, second_ref, gains_ref = refs[2 * count :]
    rows = rows_ref.shape[0]
    grad = blocks[0][...].astype(F32)
    for block in blocks[1:]:
        grad = grad + block[...].astype(F32)
    gains_ref[...] = grad[rows : rows + 8, :] + grad[rows + 8 :, :]
    own = x_ref[pl.ds(pl.multiple_of(meta[AT_SLOT] * rows, rows), rows), :].astype(F32)
    plain, scale = plain_of(own)
    out_ref[...] = (
        rows_ref[...] + input_gradient(grad[0:rows, :], plain, scale, gain_ref[...].astype(F32))
    ).astype(LOW)
    total = pairs[0][...].astype(F32)
    for pair in pairs[1:]:
        total = total + pair[...].astype(F32)
    second_ref[...] = total.astype(LOW)


def layer_rows_kernel(count, meta, *refs):
    lay_blocks(meta, refs[:count], refs[count])


def pair_rows_kernel(count, meta, *refs):
    blocks, first_ref, second_ref = refs[:count], refs[count], refs[count + 1]
    rows = blocks[0].shape[0] // 2
    for r, block in enumerate(blocks):
        at = pl.multiple_of(jnp.bitwise_xor(meta[AT_SLOT], r) * rows, rows)
        first_ref[pl.ds(at, rows), :] = block[0:rows, :]
        second_ref[pl.ds(at, rows), :] = block[rows:, :]


def feed_weights_kernel(split, meta, normed_ref, pre_ref, active_ref, grad_ref, first_ref, second_ref):
    up = dot_nn(normed_ref[...].T, pre_ref[...]).astype(LOW)
    down = dot_nn(active_ref[...].T, grad_ref[...]).astype(LOW)
    if not split:
        first_ref[...] = up
        second_ref[...] = down
        return
    half = meta[AT_HALF]

    @pl.when(half == 0)
    def _():
        first_ref[...] = up
        second_ref[...] = down

    @pl.when(half == 1)
    def _():
        first_ref[...] = down
        second_ref[...] = up


def cross_weights_kernel(count, meta, dq_ref, normed_ref, sides_ref, enc_ref, mixed_cross_ref, branch_cross_ref, *refs):
    mixed_self_ref, branch_self_ref = refs[:2]
    blocks, out_ref, layer_ref = refs[2 : 2 + count], refs[2 + count], refs[3 + count]
    inner = dq_ref.shape[0]
    out_ref[0:inner, :] = dot_nn(dq_ref[...], normed_ref[...]).astype(LOW)
    out_ref[inner : 3 * inner, :] = dot_nn(sides_ref[...].T, enc_ref[...]).astype(LOW)
    out_ref[3 * inner : 4 * inner, :] = dot_nn(mixed_cross_ref[...], branch_cross_ref[...]).astype(LOW)
    out_ref[4 * inner :, :] = dot_nn(mixed_self_ref[...], branch_self_ref[...]).astype(LOW)
    lay_blocks(meta, blocks, layer_ref)


def payload_kernel(split, meta, cross_ref, normed_ref, dq_ref, sides_ref, bias_ref, hot_ref, *refs):
    outs, whole = refs[:-1], refs[-1]
    inner = dq_ref.shape[0]
    width = normed_ref.shape[1]
    at = 5 * inner
    whole[0:at, :] = cross_ref[...]
    whole[at : at + inner, :] = dot_nn(dq_ref[...], normed_ref[...]).astype(LOW)
    whole[at + inner : at + 3 * inner, :] = dot_nn(sides_ref[...].T, normed_ref[...]).astype(LOW)
    diagonal = bias_ref[...]
    high = diagonal.astype(LOW)
    rest = (diagonal - high.astype(F32)).astype(LOW)
    bias = dot_nn(high, hot_ref[...]) + dot_nn(rest, hot_ref[...])
    bias = jnp.concatenate([bias, jnp.zeros((8, width - bias.shape[1]), F32)], axis=1)
    at = at + 3 * inner
    whole[at : at + 16, :] = jnp.concatenate([bias, jnp.zeros_like(bias)], axis=0).astype(LOW)
    whole[at + 16 :, :] = jnp.zeros((whole.shape[0] - at - 16, width), LOW)
    if not split:
        outs[0][...] = whole[...]
        return
    rows = whole.shape[0] // 2
    half = meta[AT_HALF]
    outs[0][...] = whole[pl.ds(pl.multiple_of(half * rows, rows), rows), :]
    outs[1][...] = whole[pl.ds(pl.multiple_of((1 - half) * rows, rows), rows), :]


def quarter_kernel(meta, keep_ref, recv_ref, *refs):
    blocks, total = refs[:4], refs[4]
    total[...] = keep_ref[...].astype(F32) + recv_ref[...].astype(F32)
    rows = blocks[0].shape[0]
    for f in range(4):
        at = pl.multiple_of(jnp.bitwise_xor(meta[AT_QUARTER], f) * rows, rows)
        blocks[f][...] = total[pl.ds(at, rows), :].astype(LOW)


def halves_kernel(at_bit, meta, keep_ref, recv_ref, first_ref, second_ref, total):
    total[...] = keep_ref[...].astype(F32) + recv_ref[...].astype(F32)
    rows = first_ref.shape[0]
    bit = meta[at_bit]
    first_ref[...] = total[pl.ds(pl.multiple_of(bit * rows, rows), rows), :].astype(LOW)
    second_ref[...] = total[pl.ds(pl.multiple_of((1 - bit) * rows, rows), rows), :].astype(LOW)


def join_kernel(at_bit, meta, own_ref, other_ref, out_ref):
    rows = own_ref.shape[0]
    bit = meta[at_bit]
    out_ref[pl.ds(pl.multiple_of(bit * rows, rows), rows), :] = own_ref[...]
    out_ref[pl.ds(pl.multiple_of((1 - bit) * rows, rows), rows), :] = other_ref[...]


def feed_finish_kernel(split, meta, own_ref, other_ref, up_ref, down_ref):
    if not split:
        up_ref[...] = own_ref[...].astype(F32)
        down_ref[...] = other_ref[...].astype(F32)
        return

    @pl.when(meta[AT_HALF] == 0)
    def _():
        up_ref[...] = own_ref[...].astype(F32)
        down_ref[...] = other_ref[...].astype(F32)

    @pl.when(meta[AT_HALF] == 1)
    def _():
        up_ref[...] = other_ref[...].astype(F32)
        down_ref[...] = own_ref[...].astype(F32)


def own_kernel(meta, *refs):
    blocks, gains_ref, out_ref = refs[:4], refs[4], refs[5]
    rows = blocks[0].shape[0]
    total = blocks[0][...].astype(F32)
    for block in blocks[1:]:
        total = total + block[...].astype(F32)
    out_ref[0:rows, :] = total.astype(LOW)
    high = gains_ref[...].astype(LOW)
    rest = (gains_ref[...] - high.astype(F32)).astype(LOW)
    out_ref[rows:, :] = jnp.concatenate([high, rest], axis=0)


def finish_kernel(split, meta, *refs):
    count = 8 if split else 1
    parts, outs, whole = refs[:count], refs[count:-1], refs[-1]
    if split:
        outs, gains_ref = outs[:-1], outs[-1]
        rows = parts[0].shape[0] - 16
        gains = parts[0][rows:, :].astype(F32)
        for part in parts[1:]:
            gains = gains + part[rows:, :].astype(F32)
        gains_ref[...] = gains[0:8, :] + gains[8:, :]
        half = meta[AT_HALF]
        for i, part in enumerate(parts):
            side = half if i < 4 else 1 - half
            at = side * 4 * rows + jnp.bitwise_xor(meta[AT_QUARTER], i % 4) * rows
            whole[pl.ds(pl.multiple_of(at, rows), rows), :] = part[0:rows, :].astype(F32)
    else:
        whole[...] = parts[0][...].astype(F32)
    at = 0
    for out in outs:
        out[...] = whole[at : at + out.shape[0], :]
        at += out.shape[0]


def swap(values, axis, flip):
    count = lax.axis_size(axis)
    return lax.ppermute(values, axis, [(i, i ^ flip) for i in range(count)])


def swaps(values, axis):
    return [values] + [swap(values, axis, flip) for flip in range(1, lax.axis_size(axis))]


def trades(blocks, axis):
    return [blocks[0]] + [swap(block, axis, flip) for flip, block in enumerate(blocks) if flip]


def gather_rows(values, axis):
    return lax.all_gather(values, axis, axis=0, tiled=True)


def after(values, *others):
    return lax.optimization_barrier((values,) + others)[0]


def body(
    hidden_in,
    encoder_out,
    dec_segments,
    enc_segments,
    gain_self,
    gain_cross,
    gain_feed,
    self_query,
    self_key,
    self_value,
    self_output,
    bias_table,
    cross_query,
    cross_key,
    cross_value,
    cross_output,
    hidden_up,
    hidden_down,
    out_grad,
):
    tok_len, width = hidden_in.shape[1:]
    heads = bias_table.shape[1]
    inner = self_query.shape[1]
    place = lax.axis_index("ctx")
    slot = lax.axis_index("tensor")
    slots = lax.axis_size("tensor")
    split = lax.axis_size("dp") == 2 and lax.axis_size("ctx") == 4
    both = ("dp", "ctx")
    share = tok_len // slots
    lanes = 2 * inner
    odd = place & 1
    line = lax.axis_index("dp")
    combined = line * 4 + place
    meta = make_meta(
        dec_segments[0],
        enc_segments[0],
        place * tok_len,
        place,
        [slot, odd, combined & 1, (combined >> 1) & 3, line & 1, (place >> 1) & 1],
    )
    bias_rows = position_rows(bias_table, heads)
    tokens = hidden_in[0]
    encoded = encoder_out[0]
    cotangent = out_grad[0]
    gain_one = gain_self[None]
    gain_two = gain_cross[None]
    gain_three = gain_feed[None]
    rows_low = shape_of(tok_len, width, LOW)
    rows_full = shape_of(tok_len, width, F32)
    part_low = shape_of(share, width, LOW)
    part_full = shape_of(share, width, F32)
    sum_row = shape_of(8, width, F32)
    weight_low = shape_of(slots * inner, width, LOW)
    sides_low = shape_of(tok_len, lanes, LOW)
    mixed_room = pltpu.VMEM((slots * inner, tok_len), LOW)
    total_room = pltpu.VMEM((tok_len, width), F32)

    def send(block, flip):
        return lax.ppermute(block, both, [(i, i ^ flip) for i in range(8)])

    def add_halves(at_bit, keep, recv, name):
        rows, columns = keep.shape
        half = shape_of(rows // 2, columns, LOW)
        return onchip(
            functools.partial(halves_kernel, at_bit),
            name,
            [half, half],
            [meta, keep, recv],
            [pltpu.VMEM((rows, columns), F32)],
            cost=1,
        )

    def join(at_bit, own, other, name):
        rows, columns = own.shape
        return onchip(
            functools.partial(join_kernel, at_bit),
            name,
            [shape_of(2 * rows, columns, LOW)],
            [meta, own, other],
            cost=1,
        )[0]

    def far_sum(keep, add, name):
        return onchip(far_kernel, name, [sides_low], [meta, keep, add], cost=1)[0]

    self_query, self_key, self_value = self_query.T, self_key.T, self_value.T
    cross_query, cross_key, cross_value = cross_query.T, cross_key.T, cross_value.T

    def lay_weights(plane, other, count, name):
        return onchip(
            functools.partial(weights_kernel, slots),
            name,
            [weight_low] * count,
            [meta, plane, other],
            cost=1,
        )

    normed_self, own_sides = onchip(
        sides_kernel, "self_sides", [rows_low, sides_low], [tokens, gain_one, self_key, self_value], table=False
    )
    far_sides = swap(own_sides, "ctx", 2)
    queries, own_cross = onchip(
        others_kernel,
        "query_and_cross_sides",
        [shape_of(tok_len, inner, LOW), sides_low],
        [normed_self, self_query, encoded, cross_key, cross_value],
        table=False,
    )
    pieces = onchip(
        pieces_kernel,
        "pieces",
        [shape_of(inner // 4, width, LOW)] * 3,
        [meta, self_output, cross_output, after(cross_query, queries)],
        cost=1,
    )
    self_pieces = swaps(pieces[0], "tensor")
    cross_piece = after(jnp.concatenate(pieces[1:], axis=0), *self_pieces)
    cross_pieces = swaps(cross_piece, "tensor")
    column = jnp.concatenate(self_pieces, axis=0)
    far_column = swap(column, "dp", 1)
    sides = [own_sides, swap(own_sides, "ctx", 1), far_sides, swap(far_sides, "ctx", 1)]
    mixed_self, lse_self, tile_self = attend(True, heads, meta, bias_rows, queries, sides)
    mixed_self_in, far_column, cross_pieces, own_cross = after(
        (mixed_self, far_column, tuple(cross_pieces), own_cross), lse_self
    )
    far_cross = swap(own_cross, "ctx", 2)
    cross_column = jnp.concatenate(cross_pieces, axis=0)
    far_cross_column = swap(cross_column, "dp", 1)
    plane = jnp.concatenate([column, far_column], axis=0)
    (self_output_all,) = lay_weights(plane, swap(plane, "ctx", 1), 1, "self_weight")
    mixed_self_all = gather_rows(mixed_self_in, "tensor")
    mixed_self_all, far_cross_column, far_cross = after(
        (mixed_self_all, far_cross_column, far_cross), mixed_self_in
    )
    cross_sides = [own_cross, swap(own_cross, "ctx", 1), far_cross, swap(far_cross, "ctx", 1)]
    after_self, normed_cross, cross_queries = onchip(
        functools.partial(cross_entry_kernel, slots),
        "cross_entry",
        [rows_full, rows_low, shape_of(tok_len, inner, LOW)],
        [meta, tokens, mixed_self_all, self_output_all, gain_two, cross_query],
        cost=2,
    )
    cross_plane = jnp.concatenate([cross_column, far_cross_column], axis=0)
    other_plane = swap(cross_plane, "ctx", 1)
    mixed_cross, lse_cross = attend(False, heads, meta, None, cross_queries, cross_sides)
    mixed_cross_in, other_plane = after((mixed_cross, other_plane), lse_cross)
    cross_output_all, cross_query_all = lay_weights(cross_plane, other_plane, 2, "cross_weights_all")
    fed = onchip(
        functools.partial(feed_kernel, slots),
        "feed",
        [part_full, rows_low, rows_low, rows_low, sum_row] + [part_low] * slots,
        [meta, after_self, gather_rows(mixed_cross_in, "tensor"), cross_output_all]
        + [gain_three, hidden_up, hidden_down, cotangent],
        [total_room, total_room],
        cost=4,
    )
    after_rows, normed_feed, active, grad_pre, gain_grad_feed = fed[:5]
    feed_blocks = trades(fed[5:], "tensor")
    feed_weights = onchip(
        functools.partial(feed_weights_kernel, split),
        "feed_weights",
        [shape_of(width, hidden_up.shape[1], LOW)] * 2,
        [meta, normed_feed, grad_pre, active, cotangent],
        cost=2,
    )
    layer_parts = onchip(
        functools.partial(layer_kernel, slots),
        "layer_parts",
        [part_low] * slots,
        [meta, active, hidden_down],
        [total_room],
        cost=1,
    )
    feed_blocks, feed_weights = after((tuple(feed_blocks), tuple(feed_weights)), *layer_parts)
    (branch_rows,) = onchip(
        functools.partial(feed_back_kernel, slots),
        "feed_back",
        [part_low],
        [meta, after_rows, cotangent, gain_three] + list(feed_blocks),
        cost=1,
    )
    branch_cross = gather_rows(branch_rows, "tensor")
    if split:
        feed_keep, feed_send = after(feed_weights, branch_rows)
        feed_add = send(feed_send, 1)
        branch_cross, layer_parts, feed_add = after((branch_cross, tuple(layer_parts), feed_add), branch_rows)
        by_line = add_halves(AT_DP, feed_keep, feed_add, "feed_line")
        line_recv = send(by_line[1], 4)
    else:
        branch_cross, layer_parts = after((branch_cross, tuple(layer_parts)), branch_rows)
    layer_blocks = trades(after(tuple(layer_parts), branch_cross), "tensor")

    back = attend_back(
        False, heads, meta, (), cross_queries, cross_output, mixed_cross, lse_cross, cross_sides, [branch_cross]
    )
    grad_cross_q, keep, near = back
    if split:
        grad_cross_q, keep, near, line_recv = after((grad_cross_q, keep, near, line_recv), *layer_blocks)
        by_far = add_halves(AT_FAR, by_line[0], line_recv, "feed_far")
        far_recv = send(by_far[1], 2)
    else:
        grad_cross_q, keep, near = after((grad_cross_q, keep, near), *layer_blocks)
    near = swap(near, "ctx", 1)
    queries_all = gather_rows(grad_cross_q, "tensor")
    if split:
        queries_all, near, far_recv = after((queries_all, near, far_recv), grad_cross_q)
        feed_far_sum = (by_far[0].astype(F32) + far_recv.astype(F32)).astype(LOW)
        far_recv = send(feed_far_sum, 2)
    else:
        queries_all, near = after((queries_all, near), grad_cross_q)
    far = swap(far_sum(keep, near, "cross_far"), "ctx", 2)
    cross_keep = keep
    after_self_rows, branch_self, gain_grad_cross = onchip(
        functools.partial(self_entry_kernel, slots),
        "self_entry",
        [part_full, rows_low, sum_row],
        [meta, after_self, queries_all, cross_query_all, gain_two, branch_cross],
        [total_room],
        cost=2,
    )
    (layer_rows,) = onchip(
        functools.partial(layer_sum_kernel, slots),
        "layer_sum",
        [part_low],
        [meta, after_rows] + layer_blocks,
    )
    layer_pieces = swaps(after(layer_rows, queries_all), "tensor")
    back = attend_back(
        True, heads, meta, (bias_rows, tile_self), queries, self_output, mixed_self, lse_self, sides, [branch_self]
    )
    grad_queries, keep, own_near, diagonals = back
    gate = list(layer_pieces[1:]) + ([far, far_recv] if split else [far])
    grad_queries, keep, own_near = after((grad_queries, keep, own_near), *gate)
    encoded_out = onchip(
        functools.partial(encoder_kernel, slots),
        "encoder_parts",
        [sides_low] + [part_low] * slots,
        [meta, cross_keep, near, after(far, grad_queries), cross_key, cross_value],
        [total_room],
        cost=1,
    )
    grad_cross_sides = encoded_out[0]
    encoder_blocks = trades(encoded_out[1:], "tensor")
    near = swap(after(own_near, encoded_out[0]), "ctx", 1)
    far = swap(far_sum(keep, near, "self_far"), "ctx", 2)
    if split:
        feed_half = join(AT_FAR, feed_far_sum, after(far_recv, grad_queries), "feed_half")
        feed_most = join(AT_DP, feed_half, send(feed_half, 4), "feed_most")
    cross_weights, layer_out = onchip(
        functools.partial(cross_weights_kernel, slots),
        "cross_weights",
        [shape_of(5 * inner, width, LOW), rows_low],
        [meta, grad_cross_q, normed_cross, grad_cross_sides, encoded, mixed_cross, branch_cross]
        + [mixed_self, branch_self]
        + layer_pieces,
        cost=2,
    )
    far, cross_weights = after((far, cross_weights), layer_out, *encoder_blocks, *([feed_most] if split else []))
    left = onchip(
        functools.partial(exit_kernel, slots),
        "self_exit",
        [sides_low] + [shape_of(share + 16, width, LOW)] * slots,
        [meta, keep, near, far, grad_queries, self_query, self_key, self_value, tokens]
        + [gain_grad_cross, gain_grad_feed],
        [total_room],
        cost=1,
    )
    grad_sides = left[0]
    left_blocks = trades(left[1:], "tensor")
    if split:
        feed_summed = [feed_most, send(after(feed_most, grad_sides), 1)]
    else:
        feed_summed = list(lax.psum(tuple(feed_weights), both))
    grad_up, grad_down = onchip(
        functools.partial(feed_finish_kernel, split),
        "feed_finish",
        [shape_of(width, hidden_up.shape[1], F32)] * 2,
        [meta] + feed_summed,
        cost=3,
    )
    left_blocks = after(tuple(left_blocks), grad_up)
    hidden_rows, encoder_rows, gains = onchip(
        functools.partial(last_rows_kernel, slots),
        "last_rows",
        [part_low, part_low, sum_row],
        [meta, after_self_rows, tokens, gain_one] + list(left_blocks) + encoder_blocks,
        cost=1,
    )
    weight_rows = -(-(8 * inner + 16) // 128) * 128
    hot = jnp.asarray(np.pad(span_onehot(), ((0, 0), (0, 128 - BUCKETS))), LOW)
    payload = onchip(
        functools.partial(payload_kernel, split),
        "last_weights",
        [shape_of(weight_rows // 2, width, LOW)] * 2 if split else [shape_of(weight_rows, width, LOW)],
        [meta, cross_weights, normed_self, grad_queries, grad_sides, diagonals, hot],
        [pltpu.VMEM((weight_rows, width), LOW)],
        cost=2,
    )
    if split:
        rows = weight_rows // 8
        quarters = onchip(
            quarter_kernel,
            "quarters",
            [shape_of(rows, width, LOW)] * 4,
            [meta, payload[0], send(payload[1], 1)],
            [pltpu.VMEM((4 * rows, width), F32)],
            cost=1,
        )
        (own,) = onchip(
            own_kernel,
            "own_eighth",
            [shape_of(rows + 16, width, LOW)],
            [meta, quarters[0]] + [send(quarters[flip], 2 * flip) for flip in (1, 2, 3)] + [gains],
            cost=1,
        )
        summed = [own] + [send(own, 2 * flip) for flip in (1, 2, 3)]
    else:
        summed = [lax.psum(payload[0], both)]
        gains = lax.psum(gains, both)
    grad_hidden = gather_rows(hidden_rows, "tensor")
    if split:
        grad_hidden, near_blocks = after((grad_hidden, tuple(summed)), hidden_rows)
        summed = list(near_blocks) + [send(block, 1) for block in near_blocks]
    grad_encoder = gather_rows(after(encoder_rows, grad_hidden), "tensor")
    weights = onchip(
        functools.partial(finish_kernel, split),
        "finish",
        [shape_of(inner, width, F32)] * 8 + [shape_of(16, width, F32)] + [sum_row] * split,
        [meta] + summed,
        [pltpu.VMEM((weight_rows, width), F32)],
        cost=3,
    )
    if split:
        gains = weights[9]
    return (
        layer_out[None],
        grad_hidden[None],
        grad_encoder[None],
        gains[0],
        gains[1],
        gains[2],
        weights[5].T,
        weights[6].T,
        weights[7].T,
        weights[4],
        weights[8][:heads, :BUCKETS].T,
        weights[0].T,
        weights[1].T,
        weights[2].T,
        weights[3],
        grad_up,
        grad_down,
    )


def solution(mesh):
    rows = P("dp", "ctx", None)
    ids = P("dp", None)
    columns = P(None, "tensor")
    shards = P("tensor", None)
    placed = (
        (rows, rows, ids, ids, P(), P(), P())
        + (columns, columns, columns, shards, columns, columns, columns, columns, shards)
        + (columns, shards, rows)
    )
    given = (
        (rows, rows, rows, P(), P(), P())
        + (columns, columns, columns, shards, columns, columns, columns, columns, shards)
        + (columns, shards)
    )
    return jax.shard_map(body, mesh=mesh, in_specs=placed, out_specs=given, check_vma=False)
```

```python
import math
import functools
import numpy as np
import jax
import jax.numpy as jnp
from jax import lax
from jax.sharding import PartitionSpec as P
from jax.experimental import pallas as pl
from jax.experimental.pallas import tpu as pltpu

BUCKETS = 32
MAXDIST = 128
DOCS = 8
EPSILON = 1e-06
MASKED = -1000000000.0
MASK_WEIGHT = -float(2**30)
CURVE_SCALE = math.sqrt(2.0 / math.pi)
CUBIC_TERM = 0.044715
HIGHEST = lax.Precision.HIGHEST

HEAD = 64
KEYS = 256
WIDE = 256
SPAN = 1280
VMEM_BYTES = 60 * 1024 * 1024


def position_bucket(distance):
    exact_cut = BUCKETS // 2
    if distance < exact_cut:
        return distance
    scaled = math.log(distance / exact_cut) / math.log(MAXDIST / exact_cut) * (BUCKETS - exact_cut)
    return min(exact_cut + int(scaled), BUCKETS - 1)


def span_onehot():
    table = np.zeros((SPAN, BUCKETS), np.float32)
    for place in range(KEYS, KEYS + 3 * KEYS):
        table[place, position_bucket(place - KEYS)] = 1.0
    return table


def taking(microseconds):
    return pl.CostEstimate(flops=int(microseconds * 1e9), transcendentals=0, bytes_accessed=int(microseconds * 3.5e6))


def dot_nt(left, right):
    return lax.dot_general(left, right, (((1,), (1,)), ((), ())), preferred_element_type=jnp.float32)


def dot_nn(left, right):
    return lax.dot_general(left, right, (((1,), (0,)), ((), ())), preferred_element_type=jnp.float32)


def onehot_rows(count, first, meta, base):
    lane = lax.broadcasted_iota(jnp.int32, (1, HEAD), 1)
    low = jnp.zeros((1, HEAD), jnp.int32)
    high = jnp.zeros((1, HEAD), jnp.int32)
    for d in range(DOCS):
        low = jnp.where(lane == d, meta[base + d], low)
        high = jnp.where(lane == d, meta[base + d + 1], high)
    place = lax.broadcasted_iota(jnp.int32, (count, HEAD), 0) + first
    return (place >= low) & (place < high)


def head_mask(width, first, head, feature_from):
    lane = lax.broadcasted_iota(jnp.int32, (1, width), 1)
    start = first + head * HEAD
    keep = (lane >= start) & (lane < start + HEAD)
    if feature_from is not None:
        keep = keep | (lane >= feature_from)
    return keep.astype(jnp.float32).astype(jnp.bfloat16)


def gather_blocks(meta, parts, kvs, kext, key_base):
    rows = parts[0].shape[0]
    me = meta[1]
    inner = kext.shape[1] - HEAD
    for r, part in enumerate(parts):
        at = pl.multiple_of(jnp.bitwise_xor(me, r) * rows, rows)
        kvs[pl.ds(at, rows), :] = part[...]
        kext[pl.ds(at, rows), 0:inner] = part[:, 0:inner]
        kext[pl.ds(at, rows), inner:] = onehot_rows(rows, at, meta, key_base).astype(jnp.float32).astype(jnp.bfloat16)


def query_heads(meta, q_ref, qx, qm, heads, query_base):
    rows, inner = q_ref.shape
    own = onehot_rows(rows, meta[0], meta, query_base)
    qx[:, 0:inner] = q_ref[...]
    qx[:, inner:] = jnp.where(own, 0.0, MASK_WEIGHT).astype(jnp.bfloat16)
    for h in range(heads):
        qm[h] = qx[...] * head_mask(qx.shape[1], 0, h, inner)


def tile_kernel(u_ref, tile):
    for h in range(tile.shape[0]):
        row = jnp.broadcast_to(u_ref[h : h + 1, :], (KEYS, SPAN))
        tile[h] = pltpu.roll(row, 0, 1, stride=1, stride_axis=0)[:, 0 : 4 * KEYS]


def key_range(meta, rows, query_base, key_base):
    first = meta[0]
    last = first + rows - 1
    low = meta[key_base]
    high = meta[key_base + 1]
    for d in range(1, DOCS):
        low = jnp.where(meta[query_base + d] <= first, meta[key_base + d], low)
        high = jnp.where(meta[query_base + d] <= last, meta[key_base + d + 1], high)
    return lax.div(low, KEYS), lax.div(high + KEYS - 1, KEYS)


def for_blocks(meta, rows, causal, query_base, key_base, step, carry):
    low, high = key_range(meta, rows, query_base, key_base)
    if not causal:
        return lax.fori_loop(
            lax.div(low, 2), lax.div(high + 1, 2), lambda kb, c: step(2 * kb + 1, None, step(2 * kb, None, c)), carry
        )
    near = lax.div(meta[0], KEYS)
    carry = lax.fori_loop(
        lax.div(low, 2), lax.div(near, 2) - 1, lambda kb, c: step(2 * kb + 1, None, step(2 * kb, None, c)), carry
    )
    carry = lax.cond(
        near > 0, lambda c: step(near - 1, 2 * KEYS, step(near - 2, None, c)), lambda c: c, carry
    )
    carry = step(near, KEYS, carry)
    return step(near + 1, 0, carry)


def forward_kernel(causal, heads, count, meta, *refs):
    if causal:
        u_ref, tile = refs[:2]
        refs = refs[2:]
    q_ref, refs = refs[0], refs[1:]
    parts, refs = refs[:count], refs[count:]
    out_ref, lse_ref = refs[:2]
    refs = refs[2:]
    kvs, kext, vt, qx, qm, ot = refs
    query_base = 2
    key_base = 2 if causal else 2 + DOCS + 1
    rows = q_ref.shape[0]
    gather_blocks(meta, parts, kvs, kext, key_base)
    query_heads(meta, q_ref, qx, qm, heads, query_base)
    lanes = kvs.shape[1]
    for kb in range(kvs.shape[0] // KEYS):
        vt[kb] = kvs[kb * KEYS : (kb + 1) * KEYS, lanes - WIDE :].T
    ot[...] = jnp.zeros_like(ot)
    shift = WIDE - heads * HEAD

    def step(kb, place, carry):
        kx = kext[pl.ds(pl.multiple_of(kb * KEYS, KEYS), KEYS), :]
        scores = [dot_nt(kx, qm[h]) for h in range(heads)]
        tops, sums = carry
        new_tops, new_sums = [], []
        for h in range(heads):
            far = 0.0
            if place is not None:
                scores[h] = scores[h] + tile[h, :, place : place + rows]
            elif causal:
                far = u_ref[h : h + 1, 4 * KEYS - 1 : 4 * KEYS]
            after = jnp.maximum(tops[h], jnp.max(scores[h], axis=0, keepdims=True) + far)
            scale = jnp.exp(tops[h] - after)
            weights = jnp.exp(scores[h] - (after - far))
            new_tops.append(after)
            new_sums.append(sums[h] * scale + jnp.sum(weights.reshape(KEYS // 8, 8, rows), axis=0))
            own = vt[kb, shift + h * HEAD : shift + (h + 1) * HEAD, :]
            at = slice(h * HEAD, (h + 1) * HEAD)
            ot[at, :] = ot[at, :] * scale + dot_nn(own, weights.astype(jnp.bfloat16))
        return new_tops, new_sums

    carry = (
        [jnp.full((1, rows), -3e38, jnp.float32)] * heads,
        [jnp.zeros((8, rows), jnp.float32)] * heads,
    )
    tops, sums = for_blocks(meta, rows, causal, query_base, key_base, step, carry)
    lse_ref[...] = jnp.zeros_like(lse_ref)
    for h in range(heads):
        at = slice(h * HEAD, (h + 1) * HEAD)
        total = jnp.sum(sums[h], axis=0, keepdims=True)
        out_ref[at, :] = (ot[at, :] / total).astype(jnp.bfloat16)
        lse_ref[h : h + 1, :] = tops[h] + jnp.log(total)


def attend(causal, heads, meta, u, queries, parts):
    rows, inner = queries.shape
    part_rows, lanes = parts[0].shape
    count = len(parts)
    length = part_rows * count
    smem = pl.BlockSpec(memory_space=pltpu.SMEM)
    vmem = pl.BlockSpec(memory_space=pltpu.VMEM)
    given = list(u) + [queries] + list(parts)
    scratch = [
        pltpu.VMEM((length, lanes), jnp.bfloat16),
        pltpu.VMEM((length, inner + HEAD), jnp.bfloat16),
        pltpu.VMEM((length // KEYS, WIDE, KEYS), jnp.bfloat16),
        pltpu.VMEM((rows, inner + HEAD), jnp.bfloat16),
        pltpu.VMEM((heads, rows, inner + HEAD), jnp.bfloat16),
        pltpu.VMEM((inner, rows), jnp.float32),
    ]
    out_shape = [
        jax.ShapeDtypeStruct((inner, rows), jnp.bfloat16),
        jax.ShapeDtypeStruct((8, rows), jnp.float32),
    ]
    return pl.pallas_call(
        functools.partial(forward_kernel, causal, heads, count),
        out_shape=tuple(out_shape),
        in_specs=[smem] + [vmem] * len(given),
        out_specs=tuple([vmem] * len(out_shape)),
        scratch_shapes=scratch,
        compiler_params=pltpu.CompilerParams(vmem_limit_bytes=30 * 1024 * 1024),
        cost_estimate=taking(9),
        name="self_forward" if causal else "cross_forward",
    )(meta, *given)


def fold_diagonals(values):
    half = values.shape[0] // 2
    while half >= 1:
        values = values[:half] + pltpu.roll(values[half : 2 * half], SPAN - half, 1)
        half = half // 2
    return values


def backward_kernel(causal, heads, count, branch_count, meta, *refs):
    if causal:
        u_ref, tile = refs[:2]
        refs = refs[2:]
    q_ref, out_weight, mixed_ref, lse_ref = refs[:4]
    parts, refs = refs[4 : 4 + count], refs[4 + count :]
    branches, refs = refs[:branch_count], refs[branch_count:]
    dq_ref = refs[0]
    keep_ref, send_ref, refs = refs[1], refs[2], refs[3:]
    if causal:
        dbias_ref = refs[0]
        refs = refs[1:]
    branch_ref = branches[0]
    kvs, kext, kt, qx, qm, dom, ra, rb, dqt, row, dkv, do_ref = refs[:12]
    query_base = 2
    key_base = 2 if causal else 2 + DOCS + 1
    rows, inner = q_ref.shape
    lanes = kvs.shape[1]
    do_ref[:, 0:inner] = jnp.zeros((rows, inner), jnp.bfloat16)
    do_ref[:, inner:] = dot_nt(branch_ref[...], out_weight[...]).astype(jnp.bfloat16)
    gather_blocks(meta, parts, kvs, kext, key_base)
    query_heads(meta, q_ref, qx, qm, heads, query_base)
    for kb in range(kvs.shape[0] // KEYS):
        kt[kb] = kvs[kb * KEYS : (kb + 1) * KEYS, 0:WIDE].T
    shift = WIDE - inner
    for h in range(heads):
        dom[h] = do_ref[:, lanes - WIDE :] * head_mask(WIDE, shift, h, None)
        ra[h * rows : (h + 1) * rows, :] = q_ext_only(qx, h, inner)
    ra[heads * rows :, :] = do_ref[:, 0:WIDE] * head_mask(WIDE, inner, 0, None)
    for h in range(1, heads):
        rb[(h - 1) * rows : h * rows, :] = do_ref[:, WIDE:] * head_mask(lanes - WIDE, inner - WIDE, h, None)
    turned = do_ref[:, lanes - WIDE :].astype(jnp.float32).T
    inner_sum = turned[shift:, :] * mixed_ref[...].astype(jnp.float32)
    for h in range(heads):
        row[h : h + 1, :] = jnp.sum(inner_sum[h * HEAD : (h + 1) * HEAD, :], axis=0, keepdims=True)
    dqt[...] = jnp.zeros_like(dqt)
    dkv[...] = jnp.zeros_like(dkv)
    if causal:
        dtile, dfar = refs[12:14]
        dtile[...] = jnp.zeros_like(dtile)
        dfar[...] = jnp.zeros_like(dfar)

    def step(kb, place):
        at_keys = pl.ds(pl.multiple_of(kb * KEYS, KEYS), KEYS)
        kx = kext[at_keys, :]
        vx = kvs[at_keys, lanes - WIDE :]
        weights_low = []
        grads_low = []
        all_scores = [dot_nt(kx, qm[h]) for h in range(heads)]
        all_grads = [dot_nt(vx, dom[h]) for h in range(heads)]
        for h in range(heads):
            scores = all_scores[h]
            lse = lse_ref[h : h + 1, :]
            if place is not None:
                scores = scores + tile[h, :, place : place + rows]
            elif causal:
                lse = lse - u_ref[h : h + 1, 4 * KEYS - 1 : 4 * KEYS]
            weights = jnp.exp(scores - lse)
            grads = weights * (all_grads[h] - row[h : h + 1, :])
            low = grads.astype(jnp.bfloat16)
            weights_low.append(weights.astype(jnp.bfloat16))
            grads_low.append(low)
            if causal:
                if place is not None:
                    dtile[h, :, place : place + rows] += grads
                else:
                    dfar[8 * h : 8 * h + 8, :] += jnp.sum(grads.reshape(KEYS // 8, 8, rows), axis=0)
        for h in range(heads):
            at = slice(h * HEAD, (h + 1) * HEAD)
            dqt[at, :] += dot_nn(kt[kb, at, :], grads_low[h])
        dkv[at_keys, 0:WIDE] = dot_nn(jnp.concatenate(grads_low + weights_low[:1], axis=1), ra[...]).astype(jnp.bfloat16)
        dkv[at_keys, WIDE:] = dot_nn(jnp.concatenate(weights_low[1:], axis=1), rb[...]).astype(jnp.bfloat16)

    for_blocks(meta, rows, causal, query_base, key_base, lambda kb, place, c: (step(kb, place), c)[1], 0)
    dq_ref[...] = dqt[...].astype(jnp.bfloat16)
    me = meta[1]
    part_rows = parts[0].shape[0]
    for r in range(count):
        at = pl.multiple_of(jnp.bitwise_xor(me, r) * part_rows, part_rows)
        to = (r // 2) * part_rows
        (send_ref if r % 2 else keep_ref)[to : to + part_rows, :] = dkv[pl.ds(at, part_rows), :]
    if causal:
        lane = lax.broadcasted_iota(jnp.int32, (1, SPAN), 1)
        dbias_ref[...] = jnp.zeros_like(dbias_ref)
        for h in range(heads):
            padded = jnp.concatenate([dtile[h], jnp.zeros((KEYS, SPAN - 4 * KEYS), jnp.float32)], axis=1)
            far = jnp.sum(jnp.sum(dfar[8 * h : 8 * h + 8, :], axis=0, keepdims=True), axis=1, keepdims=True)
            dbias_ref[h : h + 1, :] = fold_diagonals(padded) + jnp.where(lane == 4 * KEYS - 1, far, 0.0)


def q_ext_only(qx, head, inner):
    return qx[...] * head_mask(qx.shape[1], 0, head, None)


def attend_back(causal, heads, meta, u, queries, out_weight, mixed, lse, parts, branches):
    rows, inner = queries.shape
    part_rows, lanes = parts[0].shape
    count = len(parts)
    length = part_rows * count
    smem = pl.BlockSpec(memory_space=pltpu.SMEM)
    vmem = pl.BlockSpec(memory_space=pltpu.VMEM)
    given = list(u) + [queries, out_weight, mixed, lse] + list(parts) + list(branches)
    out_shape = [jax.ShapeDtypeStruct((inner, rows), jnp.bfloat16)]
    out_shape += [jax.ShapeDtypeStruct((length // 2, lanes), jnp.bfloat16)] * 2
    if causal:
        out_shape.append(jax.ShapeDtypeStruct((8, SPAN), jnp.float32))
    scratch = [
        pltpu.VMEM((length, lanes), jnp.bfloat16),
        pltpu.VMEM((length, inner + HEAD), jnp.bfloat16),
        pltpu.VMEM((length // KEYS, WIDE, KEYS), jnp.bfloat16),
        pltpu.VMEM((rows, inner + HEAD), jnp.bfloat16),
        pltpu.VMEM((heads, rows, inner + HEAD), jnp.bfloat16),
        pltpu.VMEM((heads, rows, WIDE), jnp.bfloat16),
        pltpu.VMEM(((heads + 1) * rows, WIDE), jnp.bfloat16),
        pltpu.VMEM(((heads - 1) * rows, lanes - WIDE), jnp.bfloat16),
        pltpu.VMEM((inner, rows), jnp.float32),
        pltpu.VMEM((8, rows), jnp.float32),
        pltpu.VMEM((length, lanes), jnp.bfloat16),
        pltpu.VMEM((rows, lanes), jnp.bfloat16),
    ]
    if causal:
        scratch += [
            pltpu.VMEM((heads, KEYS, 4 * KEYS), jnp.float32),
            pltpu.VMEM((8 * heads, rows), jnp.float32),
        ]
    return pl.pallas_call(
        functools.partial(backward_kernel, causal, heads, count, len(branches)),
        out_shape=tuple(out_shape),
        in_specs=[smem] + [vmem] * len(given),
        out_specs=tuple([vmem] * len(out_shape)),
        scratch_shapes=scratch,
        compiler_params=pltpu.CompilerParams(vmem_limit_bytes=30 * 1024 * 1024),
        cost_estimate=taking(13),
        name="self_backward" if causal else "cross_backward",
    )(meta, *given)


def position_rows(bias_table, heads):
    table = span_onehot()
    rows = jnp.dot(bias_table.astype(jnp.bfloat16).T, jnp.asarray(table.T, jnp.bfloat16), preferred_element_type=jnp.float32)
    rows = rows + jnp.asarray(np.where(table.sum(1) > 0, 0.0, MASKED)[None, :], jnp.float32)
    return jnp.concatenate([rows, jnp.zeros((8 - heads, SPAN), jnp.float32)], axis=0)


def make_meta(dec_row, enc_row, offset, place, rest):
    docs = jnp.arange(DOCS + 1, dtype=jnp.int32)
    dec = jnp.sum((dec_row[None, :] < docs[:, None]).astype(jnp.int32), axis=1)
    enc = jnp.sum((enc_row[None, :] < docs[:, None]).astype(jnp.int32), axis=1)
    first = jnp.stack([offset, place]).astype(jnp.int32)
    return jnp.concatenate([first, dec, enc, jnp.stack(rest).astype(jnp.int32)])


def room(*groups):
    total = 0
    for group in groups:
        for x in group:
            rows = int(np.prod(x.shape[:-1])) if x.shape else 1
            lanes = -(-x.shape[-1] // 128) * 128 if x.shape else 128
            total += max(rows, 8) * lanes * jnp.dtype(x.dtype).itemsize
    return 2 * total + 4 * 1024 * 1024


def onchip(kernel, name, out_shape, given, scratch=(), cost=2, table=True):
    vmem = pl.BlockSpec(memory_space=pltpu.VMEM)
    in_specs = [pl.BlockSpec(memory_space=pltpu.SMEM)] + [vmem] * (len(given) - 1)
    if not table:
        in_specs = [vmem] * len(given)
    return pl.pallas_call(
        kernel,
        out_shape=tuple(out_shape),
        in_specs=in_specs,
        out_specs=tuple([vmem] * len(out_shape)),
        scratch_shapes=list(scratch),
        compiler_params=pltpu.CompilerParams(vmem_limit_bytes=room(out_shape, given, scratch)),
        cost_estimate=taking(cost),
        name=name,
    )(*given)


def shape_of(rows, columns, kind):
    return jax.ShapeDtypeStruct((rows, columns), kind)


F32 = jnp.float32
LOW = jnp.bfloat16
AT_SLOT = 2 + 2 * (DOCS + 1)
AT_ODD = AT_SLOT + 1
AT_HALF = AT_SLOT + 2
AT_QUARTER = AT_SLOT + 3
AT_DP = AT_SLOT + 4
AT_FAR = AT_SLOT + 5


def plain_of(values):
    scale = lax.rsqrt(jnp.mean(values * values, axis=-1, keepdims=True) + EPSILON)
    return values * scale, scale


def input_gradient(grad_normed, plain, scale, gain):
    grad_plain = grad_normed * gain
    inner = jnp.mean(grad_plain * plain, axis=-1, keepdims=True)
    return scale * (grad_plain - plain * inner)


def sides_kernel(x_ref, gain_ref, k_ref, v_ref, normed_ref, out_ref):
    plain, _ = plain_of(x_ref[...].astype(F32))
    normed = (plain * gain_ref[...].astype(F32)).astype(LOW)
    normed_ref[...] = normed
    out_ref[...] = dot_nt(normed, jnp.concatenate([k_ref[...], v_ref[...]], axis=0)).astype(LOW)


def others_kernel(normed_ref, q_ref, enc_ref, k_ref, v_ref, out_ref, sides_ref):
    out_ref[...] = dot_nt(normed_ref[...], q_ref[...]).astype(LOW)
    sides_ref[...] = dot_nt(enc_ref[...], jnp.concatenate([k_ref[...], v_ref[...]], axis=0)).astype(LOW)


def weights_kernel(count, meta, own_ref, other_ref, *outs):
    parts = 4
    rows = outs[0].shape[0] // (count * parts)
    for side, ref in enumerate((own_ref, other_ref)):
        for b in range(2):
            part = 2 * jnp.bitwise_xor(meta[AT_ODD], side) + jnp.bitwise_xor(meta[AT_DP], b)
            for r in range(count):
                shard = jnp.bitwise_xor(meta[AT_SLOT], r)
                to = pl.multiple_of((shard * parts + part) * rows, rows)
                for w, out in enumerate(outs):
                    at = ((b * count + r) * len(outs) + w) * rows
                    out[pl.ds(to, rows), :] = ref[at : at + rows, :]


def pieces_kernel(meta, *refs):
    half = len(refs) // 2
    for weight, out in zip(refs[:half], refs[half:]):
        rows = out.shape[0]
        at = pl.multiple_of((2 * meta[AT_ODD] + meta[AT_DP]) * rows, rows)
        out[...] = weight[pl.ds(at, rows), :]


def lay_blocks(meta, blocks, whole):
    rows = blocks[0].shape[0]
    for r, block in enumerate(blocks):
        at = pl.multiple_of(jnp.bitwise_xor(meta[AT_SLOT], r) * rows, rows)
        whole[pl.ds(at, rows), :] = block[...]


def deal_blocks(meta, whole, blocks):
    rows = blocks[0].shape[0]
    for r, block in enumerate(blocks):
        at = pl.multiple_of(jnp.bitwise_xor(meta[AT_SLOT], r) * rows, rows)
        block[...] = whole[pl.ds(at, rows), :].astype(block.dtype)


def cross_entry_kernel(count, meta, x_ref, *refs):
    mixed, weight, gain_ref, q_ref, after_ref, normed_ref, out_ref = refs
    after = x_ref[...].astype(F32) + dot_nn(mixed[...].T, weight[...])
    after_ref[...] = after
    plain, _ = plain_of(after)
    normed = (plain * gain_ref[...].astype(F32)).astype(LOW)
    normed_ref[...] = normed
    out_ref[...] = dot_nt(normed, q_ref[...]).astype(LOW)


def feed_kernel(count, meta, after_ref, mixed, weight, gain_ref, up_ref, down_ref, grad_ref, *refs):
    rows_ref, normed_ref, active_ref, pre_ref, gain_grad_ref = refs[:5]
    dealt = refs[5 : 5 + count]
    part, total = refs[5 + count :]
    total[...] = after_ref[...] + dot_nn(mixed[...].T, weight[...])
    deal_blocks(meta, total, [rows_ref])
    plain, _ = plain_of(total[...])
    normed = (plain * gain_ref[...].astype(F32)).astype(LOW)
    normed_ref[...] = normed
    pre = dot_nn(normed, up_ref[...])
    squared = pre * pre
    bent = jnp.tanh(CURVE_SCALE * pre * (1.0 + CUBIC_TERM * squared))
    active_ref[...] = (0.5 * pre * (1.0 + bent)).astype(LOW)
    slope = 0.5 * (1.0 + bent) + 0.5 * pre * (1.0 - bent * bent) * CURVE_SCALE * (
        1.0 + 3.0 * CUBIC_TERM * squared
    )
    grad_pre = (dot_nt(grad_ref[...], down_ref[...]) * slope).astype(LOW)
    pre_ref[...] = grad_pre
    part[...] = dot_nt(grad_pre, up_ref[...])
    deal_blocks(meta, part, dealt)
    gain_grad_ref[...] = jnp.broadcast_to(
        jnp.sum(part[...] * plain, axis=0, keepdims=True), gain_grad_ref.shape
    )


def feed_back_kernel(count, meta, rows_ref, grad_ref, gain_ref, *refs):
    blocks, out_ref = refs[:count], refs[count]
    grad = blocks[0][...].astype(F32)
    for block in blocks[1:]:
        grad = grad + block[...].astype(F32)
    plain, scale = plain_of(rows_ref[...])
    rows = rows_ref.shape[0]
    own = grad_ref[pl.ds(pl.multiple_of(meta[AT_SLOT] * rows, rows), rows), :].astype(F32)
    out_ref[...] = (own + input_gradient(grad, plain, scale, gain_ref[...].astype(F32))).astype(LOW)


def layer_kernel(count, meta, active_ref, down_ref, *refs):
    dealt, part = refs[:count], refs[count]
    part[...] = dot_nn(active_ref[...], down_ref[...])
    deal_blocks(meta, part, dealt)


def far_kernel(meta, keep_ref, add_ref, out_ref):
    rows = out_ref.shape[0]
    out_ref[...] = (keep_ref[rows:, :].astype(F32) + add_ref[rows:, :].astype(F32)).astype(LOW)


def encoder_kernel(count, meta, keep_ref, add_ref, recv_ref, k_ref, v_ref, *refs):
    sides_ref, dealt, part = refs[0], refs[1 : count + 1], refs[count + 1]
    near = keep_ref.shape[0] // 2
    sides = (
        keep_ref[0:near, :].astype(F32) + add_ref[0:near, :].astype(F32) + recv_ref[...].astype(F32)
    ).astype(LOW)
    sides_ref[...] = sides
    part[...] = dot_nn(sides, jnp.concatenate([k_ref[...], v_ref[...]], axis=0))
    deal_blocks(meta, part, dealt)


def layer_sum_kernel(count, meta, rows_ref, *refs):
    blocks, out_ref = refs[:count], refs[count]
    rows = rows_ref[...]
    for block in blocks:
        rows = rows + block[...].astype(F32)
    out_ref[...] = rows.astype(LOW)


def self_entry_kernel(count, meta, after_ref, *refs):
    turned, weight, gain_ref, branch_ref, rows_ref, out_ref, gain_grad_ref, total = refs
    part = dot_nn(turned[...].T, weight[...])
    plain, scale = plain_of(after_ref[...])
    grad = branch_ref[...].astype(F32) + input_gradient(part, plain, scale, gain_ref[...].astype(F32))
    total[...] = grad
    out_ref[...] = grad.astype(LOW)
    deal_blocks(meta, total, [rows_ref])
    share = 1.0 / count
    gain_grad_ref[...] = jnp.broadcast_to(
        share * jnp.sum(part * plain, axis=0, keepdims=True), gain_grad_ref.shape
    )


def exit_kernel(count, meta, keep_ref, add_ref, recv_ref, dq_ref, q_ref, k_ref, v_ref, x_ref, g2_ref, g3_ref, *refs):
    sides_ref, dealt, part = refs[0], refs[1 : 1 + count], refs[1 + count]
    rows = keep_ref.shape[0] // 2
    sides = (
        keep_ref[0:rows, :].astype(F32) + add_ref[0:rows, :].astype(F32) + recv_ref[...].astype(F32)
    ).astype(LOW)
    sides_ref[...] = sides
    part[...] = dot_nn(dq_ref[...].T, q_ref[...]) + dot_nn(
        sides, jnp.concatenate([k_ref[...], v_ref[...]], axis=0)
    )
    plain, _ = plain_of(x_ref[...].astype(F32))
    first = jnp.sum(part[...] * plain, axis=0, keepdims=True)
    row = lax.broadcasted_iota(jnp.int32, (8, first.shape[1]), 0)
    gains = jnp.where(row == 0, first, jnp.where(row == 1, g2_ref[...], g3_ref[...]))
    high = gains.astype(LOW)
    rest = (gains - high.astype(F32)).astype(LOW)
    share = dealt[0].shape[0] - 16
    for r, out in enumerate(dealt):
        at = pl.multiple_of(jnp.bitwise_xor(meta[AT_SLOT], r) * share, share)
        out[0:share, :] = part[pl.ds(at, share), :].astype(LOW)
        out[share:, :] = jnp.concatenate([high, rest], axis=0)


def last_rows_kernel(count, meta, rows_ref, x_ref, gain_ref, *refs):
    blocks, pairs = refs[:count], refs[count : 2 * count]
    out_ref, second_ref, gains_ref = refs[2 * count :]
    rows = rows_ref.shape[0]
    grad = blocks[0][...].astype(F32)
    for block in blocks[1:]:
        grad = grad + block[...].astype(F32)
    gains_ref[...] = grad[rows : rows + 8, :] + grad[rows + 8 :, :]
    own = x_ref[pl.ds(pl.multiple_of(meta[AT_SLOT] * rows, rows), rows), :].astype(F32)
    plain, scale = plain_of(own)
    out_ref[...] = (
        rows_ref[...] + input_gradient(grad[0:rows, :], plain, scale, gain_ref[...].astype(F32))
    ).astype(LOW)
    total = pairs[0][...].astype(F32)
    for pair in pairs[1:]:
        total = total + pair[...].astype(F32)
    second_ref[...] = total.astype(LOW)


def layer_rows_kernel(count, meta, *refs):
    lay_blocks(meta, refs[:count], refs[count])


def pair_rows_kernel(count, meta, *refs):
    blocks, first_ref, second_ref = refs[:count], refs[count], refs[count + 1]
    rows = blocks[0].shape[0] // 2
    for r, block in enumerate(blocks):
        at = pl.multiple_of(jnp.bitwise_xor(meta[AT_SLOT], r) * rows, rows)
        first_ref[pl.ds(at, rows), :] = block[0:rows, :]
        second_ref[pl.ds(at, rows), :] = block[rows:, :]


def feed_weights_kernel(split, meta, normed_ref, pre_ref, active_ref, grad_ref, first_ref, second_ref):
    up = dot_nn(normed_ref[...].T, pre_ref[...]).astype(LOW)
    down = dot_nn(active_ref[...].T, grad_ref[...]).astype(LOW)
    if not split:
        first_ref[...] = up
        second_ref[...] = down
        return
    half = meta[AT_HALF]

    @pl.when(half == 0)
    def _():
        first_ref[...] = up
        second_ref[...] = down

    @pl.when(half == 1)
    def _():
        first_ref[...] = down
        second_ref[...] = up


def cross_weights_kernel(count, meta, dq_ref, normed_ref, sides_ref, enc_ref, mixed_cross_ref, branch_cross_ref, *refs):
    mixed_self_ref, branch_self_ref = refs[:2]
    blocks, out_ref, layer_ref = refs[2 : 2 + count], refs[2 + count], refs[3 + count]
    inner = dq_ref.shape[0]
    out_ref[0:inner, :] = dot_nn(dq_ref[...], normed_ref[...]).astype(LOW)
    out_ref[inner : 3 * inner, :] = dot_nn(sides_ref[...].T, enc_ref[...]).astype(LOW)
    out_ref[3 * inner : 4 * inner, :] = dot_nn(mixed_cross_ref[...], branch_cross_ref[...]).astype(LOW)
    out_ref[4 * inner :, :] = dot_nn(mixed_self_ref[...], branch_self_ref[...]).astype(LOW)
    lay_blocks(meta, blocks, layer_ref)


def payload_kernel(split, meta, cross_ref, normed_ref, dq_ref, sides_ref, bias_ref, hot_ref, *refs):
    outs, whole = refs[:-1], refs[-1]
    inner = dq_ref.shape[0]
    width = normed_ref.shape[1]
    at = 5 * inner
    whole[0:at, :] = cross_ref[...]
    whole[at : at + inner, :] = dot_nn(dq_ref[...], normed_ref[...]).astype(LOW)
    whole[at + inner : at + 3 * inner, :] = dot_nn(sides_ref[...].T, normed_ref[...]).astype(LOW)
    diagonal = bias_ref[...]
    high = diagonal.astype(LOW)
    rest = (diagonal - high.astype(F32)).astype(LOW)
    bias = dot_nn(high, hot_ref[...]) + dot_nn(rest, hot_ref[...])
    bias = jnp.concatenate([bias, jnp.zeros((8, width - bias.shape[1]), F32)], axis=1)
    at = at + 3 * inner
    whole[at : at + 16, :] = jnp.concatenate([bias, jnp.zeros_like(bias)], axis=0).astype(LOW)
    whole[at + 16 :, :] = jnp.zeros((whole.shape[0] - at - 16, width), LOW)
    if not split:
        outs[0][...] = whole[...]
        return
    rows = whole.shape[0] // 2
    half = meta[AT_HALF]
    outs[0][...] = whole[pl.ds(pl.multiple_of(half * rows, rows), rows), :]
    outs[1][...] = whole[pl.ds(pl.multiple_of((1 - half) * rows, rows), rows), :]


def quarter_kernel(meta, keep_ref, recv_ref, *refs):
    blocks, total = refs[:4], refs[4]
    total[...] = keep_ref[...].astype(F32) + recv_ref[...].astype(F32)
    rows = blocks[0].shape[0]
    for f in range(4):
        at = pl.multiple_of(jnp.bitwise_xor(meta[AT_QUARTER], f) * rows, rows)
        blocks[f][...] = total[pl.ds(at, rows), :].astype(LOW)


def gather_kernel(count, meta, *refs):
    lay_blocks(meta, refs[:count], refs[count])


def halves_kernel(at_bit, meta, keep_ref, recv_ref, first_ref, second_ref, total):
    total[...] = keep_ref[...].astype(F32) + recv_ref[...].astype(F32)
    rows = first_ref.shape[0]
    bit = meta[at_bit]
    first_ref[...] = total[pl.ds(pl.multiple_of(bit * rows, rows), rows), :].astype(LOW)
    second_ref[...] = total[pl.ds(pl.multiple_of((1 - bit) * rows, rows), rows), :].astype(LOW)


def join_kernel(at_bit, meta, own_ref, other_ref, out_ref):
    rows = own_ref.shape[0]
    bit = meta[at_bit]
    out_ref[pl.ds(pl.multiple_of(bit * rows, rows), rows), :] = own_ref[...]
    out_ref[pl.ds(pl.multiple_of((1 - bit) * rows, rows), rows), :] = other_ref[...]


def feed_finish_kernel(split, meta, own_ref, other_ref, up_ref, down_ref):
    if not split:
        up_ref[...] = own_ref[...].astype(F32)
        down_ref[...] = other_ref[...].astype(F32)
        return

    @pl.when(meta[AT_HALF] == 0)
    def _():
        up_ref[...] = own_ref[...].astype(F32)
        down_ref[...] = other_ref[...].astype(F32)

    @pl.when(meta[AT_HALF] == 1)
    def _():
        up_ref[...] = other_ref[...].astype(F32)
        down_ref[...] = own_ref[...].astype(F32)


def own_kernel(meta, *refs):
    blocks, gains_ref, out_ref = refs[:4], refs[4], refs[5]
    rows = blocks[0].shape[0]
    total = blocks[0][...].astype(F32)
    for block in blocks[1:]:
        total = total + block[...].astype(F32)
    out_ref[0:rows, :] = total.astype(LOW)
    high = gains_ref[...].astype(LOW)
    rest = (gains_ref[...] - high.astype(F32)).astype(LOW)
    out_ref[rows:, :] = jnp.concatenate([high, rest], axis=0)


def finish_kernel(split, meta, *refs):
    count = 8 if split else 1
    parts, rows_ref, outs, copy_ref, whole = refs[:count], refs[count], refs[count + 1 : -2], refs[-2], refs[-1]
    copy_ref[...] = rows_ref[...]
    if split:
        outs, gains_ref = outs[:-1], outs[-1]
        rows = parts[0].shape[0] - 16
        gains = parts[0][rows:, :].astype(F32)
        for part in parts[1:]:
            gains = gains + part[rows:, :].astype(F32)
        gains_ref[...] = gains[0:8, :] + gains[8:, :]
        half = meta[AT_HALF]
        for i, part in enumerate(parts):
            side = half if i < 4 else 1 - half
            at = side * 4 * rows + jnp.bitwise_xor(meta[AT_QUARTER], i % 4) * rows
            whole[pl.ds(pl.multiple_of(at, rows), rows), :] = part[0:rows, :].astype(F32)
    else:
        whole[...] = parts[0][...].astype(F32)
    at = 0
    for out in outs:
        out[...] = whole[at : at + out.shape[0], :]
        at += out.shape[0]


def swap(values, axis, flip):
    count = lax.axis_size(axis)
    return lax.ppermute(values, axis, [(i, i ^ flip) for i in range(count)])


def swaps(values, axis):
    return [values] + [swap(values, axis, flip) for flip in range(1, lax.axis_size(axis))]


def trades(blocks, axis):
    return [blocks[0]] + [swap(block, axis, flip) for flip, block in enumerate(blocks) if flip]


def gather_rows(values, axis):
    return lax.all_gather(values, axis, axis=0, tiled=True)


def after(values, *others):
    return lax.optimization_barrier((values,) + others)[0]


def body(
    hidden_in,
    encoder_out,
    dec_segments,
    enc_segments,
    gain_self,
    gain_cross,
    gain_feed,
    self_query,
    self_key,
    self_value,
    self_output,
    bias_table,
    cross_query,
    cross_key,
    cross_value,
    cross_output,
    hidden_up,
    hidden_down,
    out_grad,
):
    tok_len, width = hidden_in.shape[1:]
    heads = bias_table.shape[1]
    inner = self_query.shape[1]
    place = lax.axis_index("ctx")
    slot = lax.axis_index("tensor")
    slots = lax.axis_size("tensor")
    split = lax.axis_size("dp") == 2 and lax.axis_size("ctx") == 4
    both = ("dp", "ctx")
    share = tok_len // slots
    lanes = 2 * inner
    odd = place & 1
    line = lax.axis_index("dp")
    combined = line * 4 + place
    meta = make_meta(
        dec_segments[0],
        enc_segments[0],
        place * tok_len,
        place,
        [slot, odd, combined & 1, (combined >> 1) & 3, line & 1, (place >> 1) & 1],
    )
    bias_rows = position_rows(bias_table, heads)
    tokens = hidden_in[0]
    encoded = encoder_out[0]
    cotangent = out_grad[0]
    gain_one = gain_self[None]
    gain_two = gain_cross[None]
    gain_three = gain_feed[None]
    rows_low = shape_of(tok_len, width, LOW)
    rows_full = shape_of(tok_len, width, F32)
    part_low = shape_of(share, width, LOW)
    part_full = shape_of(share, width, F32)
    sum_row = shape_of(8, width, F32)
    weight_low = shape_of(slots * inner, width, LOW)
    sides_low = shape_of(tok_len, lanes, LOW)
    mixed_room = pltpu.VMEM((slots * inner, tok_len), LOW)
    total_room = pltpu.VMEM((tok_len, width), F32)

    def send(block, flip):
        return lax.ppermute(block, both, [(i, i ^ flip) for i in range(8)])

    def add_halves(at_bit, keep, recv, name):
        rows, columns = keep.shape
        half = shape_of(rows // 2, columns, LOW)
        return onchip(
            functools.partial(halves_kernel, at_bit),
            name,
            [half, half],
            [meta, keep, recv],
            [pltpu.VMEM((rows, columns), F32)],
            cost=1,
        )

    def join(at_bit, own, other, name):
        rows, columns = own.shape
        return onchip(
            functools.partial(join_kernel, at_bit),
            name,
            [shape_of(2 * rows, columns, LOW)],
            [meta, own, other],
            cost=1,
        )[0]

    def far_sum(keep, add, name):
        return onchip(far_kernel, name, [sides_low], [meta, keep, add], cost=1)[0]

    self_query, self_key, self_value = self_query.T, self_key.T, self_value.T
    cross_query, cross_key, cross_value = cross_query.T, cross_key.T, cross_value.T

    def lay_weights(plane, other, count, name):
        return onchip(
            functools.partial(weights_kernel, slots),
            name,
            [weight_low] * count,
            [meta, plane, other],
            cost=1,
        )

    normed_self, own_sides = onchip(
        sides_kernel, "self_sides", [rows_low, sides_low], [tokens, gain_one, self_key, self_value], table=False
    )
    far_sides = swap(own_sides, "ctx", 2)
    queries, own_cross = onchip(
        others_kernel,
        "query_and_cross_sides",
        [shape_of(tok_len, inner, LOW), sides_low],
        [normed_self, self_query, encoded, cross_key, cross_value],
        table=False,
    )
    pieces = onchip(
        pieces_kernel,
        "pieces",
        [shape_of(inner // 4, width, LOW)] * 3,
        [meta, self_output, cross_output, after(cross_query, queries)],
        cost=1,
    )
    self_pieces = swaps(pieces[0], "tensor")
    cross_piece = after(jnp.concatenate(pieces[1:], axis=0), *self_pieces)
    cross_pieces = swaps(cross_piece, "tensor")
    column = jnp.concatenate(self_pieces, axis=0)
    far_column = swap(column, "dp", 1)
    sides = [own_sides, swap(own_sides, "ctx", 1), far_sides, swap(far_sides, "ctx", 1)]
    (tile_self,) = onchip(
        tile_kernel,
        "bias_tile",
        [jax.ShapeDtypeStruct((heads, KEYS, 4 * KEYS), F32)],
        [after(bias_rows, queries)],
        table=False,
    )
    mixed_self, lse_self = attend(True, heads, meta, (bias_rows, tile_self), queries, sides)
    mixed_self_in, far_column, cross_pieces, own_cross = after(
        (mixed_self, far_column, tuple(cross_pieces), own_cross), lse_self
    )
    far_cross = swap(own_cross, "ctx", 2)
    cross_column = jnp.concatenate(cross_pieces, axis=0)
    far_cross_column = swap(cross_column, "dp", 1)
    plane = jnp.concatenate([column, far_column], axis=0)
    (self_output_all,) = lay_weights(plane, swap(plane, "ctx", 1), 1, "self_weight")
    mixed_self_all = gather_rows(mixed_self_in, "tensor")
    mixed_self_all, far_cross_column, far_cross = after(
        (mixed_self_all, far_cross_column, far_cross), mixed_self_in
    )
    cross_sides = [own_cross, swap(own_cross, "ctx", 1), far_cross, swap(far_cross, "ctx", 1)]
    after_self, normed_cross, cross_queries = onchip(
        functools.partial(cross_entry_kernel, slots),
        "cross_entry",
        [rows_full, rows_low, shape_of(tok_len, inner, LOW)],
        [meta, tokens, mixed_self_all, self_output_all, gain_two, cross_query],
        cost=2,
    )
    cross_plane = jnp.concatenate([cross_column, far_cross_column], axis=0)
    other_plane = swap(cross_plane, "ctx", 1)
    mixed_cross, lse_cross = attend(False, heads, meta, (), cross_queries, cross_sides)
    mixed_cross_in, other_plane = after((mixed_cross, other_plane), lse_cross)
    cross_output_all, cross_query_all = lay_weights(cross_plane, other_plane, 2, "cross_weights_all")
    fed = onchip(
        functools.partial(feed_kernel, slots),
        "feed",
        [part_full, rows_low, rows_low, rows_low, sum_row] + [part_low] * slots,
        [meta, after_self, gather_rows(mixed_cross_in, "tensor"), cross_output_all]
        + [gain_three, hidden_up, hidden_down, cotangent],
        [total_room, total_room],
        cost=4,
    )
    after_rows, normed_feed, active, grad_pre, gain_grad_feed = fed[:5]
    feed_blocks = trades(fed[5:], "tensor")
    feed_weights = onchip(
        functools.partial(feed_weights_kernel, split),
        "feed_weights",
        [shape_of(width, hidden_up.shape[1], LOW)] * 2,
        [meta, normed_feed, grad_pre, active, cotangent],
        cost=2,
    )
    layer_parts = onchip(
        functools.partial(layer_kernel, slots),
        "layer_parts",
        [part_low] * slots,
        [meta, active, hidden_down],
        [total_room],
        cost=1,
    )
    feed_blocks, feed_weights = after((tuple(feed_blocks), tuple(feed_weights)), *layer_parts)
    (branch_rows,) = onchip(
        functools.partial(feed_back_kernel, slots),
        "feed_back",
        [part_low],
        [meta, after_rows, cotangent, gain_three] + list(feed_blocks),
        cost=1,
    )
    branch_cross = gather_rows(branch_rows, "tensor")
    if split:
        feed_keep, feed_send = after(feed_weights, branch_rows)
        feed_add = send(feed_send, 1)
        branch_cross, layer_parts, feed_add = after((branch_cross, tuple(layer_parts), feed_add), branch_rows)
        by_line = add_halves(AT_DP, feed_keep, feed_add, "feed_line")
        line_recv = send(by_line[1], 4)
    else:
        branch_cross, layer_parts = after((branch_cross, tuple(layer_parts)), branch_rows)
    layer_blocks = trades(after(tuple(layer_parts), branch_cross), "tensor")

    back = attend_back(
        False, heads, meta, (), cross_queries, cross_output, mixed_cross, lse_cross, cross_sides, [branch_cross]
    )
    grad_cross_q, keep, near = back
    if split:
        grad_cross_q, keep, near, line_recv = after((grad_cross_q, keep, near, line_recv), *layer_blocks)
        by_far = add_halves(AT_FAR, by_line[0], line_recv, "feed_far")
        far_recv = send(by_far[1], 2)
    else:
        grad_cross_q, keep, near = after((grad_cross_q, keep, near), *layer_blocks)
    near = swap(near, "ctx", 1)
    queries_all = gather_rows(grad_cross_q, "tensor")
    if split:
        queries_all, near, far_recv = after((queries_all, near, far_recv), grad_cross_q)
        feed_far_sum = (by_far[0].astype(F32) + far_recv.astype(F32)).astype(LOW)
        far_recv = send(feed_far_sum, 2)
    else:
        queries_all, near = after((queries_all, near), grad_cross_q)
    far = swap(far_sum(keep, near, "cross_far"), "ctx", 2)
    cross_keep = keep
    after_self_rows, branch_self, gain_grad_cross = onchip(
        functools.partial(self_entry_kernel, slots),
        "self_entry",
        [part_full, rows_low, sum_row],
        [meta, after_self, queries_all, cross_query_all, gain_two, branch_cross],
        [total_room],
        cost=2,
    )
    (layer_rows,) = onchip(
        functools.partial(layer_sum_kernel, slots),
        "layer_sum",
        [part_low],
        [meta, after_rows] + layer_blocks,
    )
    layer_pieces = swaps(after(layer_rows, queries_all), "tensor")
    back = attend_back(
        True, heads, meta, (bias_rows, tile_self), queries, self_output, mixed_self, lse_self, sides, [branch_self]
    )
    grad_queries, keep, own_near, diagonals = back
    gate = list(layer_pieces[1:]) + ([far, far_recv] if split else [far])
    grad_queries, keep, own_near = after((grad_queries, keep, own_near), *gate)
    encoded_out = onchip(
        functools.partial(encoder_kernel, slots),
        "encoder_parts",
        [sides_low] + [part_low] * slots,
        [meta, cross_keep, near, after(far, grad_queries), cross_key, cross_value],
        [total_room],
        cost=1,
    )
    grad_cross_sides = encoded_out[0]
    encoder_blocks = trades(encoded_out[1:], "tensor")
    near = swap(after(own_near, encoded_out[0]), "ctx", 1)
    far = swap(far_sum(keep, near, "self_far"), "ctx", 2)
    if split:
        feed_half = join(AT_FAR, feed_far_sum, after(far_recv, grad_queries), "feed_half")
        feed_most = join(AT_DP, feed_half, send(feed_half, 4), "feed_most")
    cross_weights, layer_out = onchip(
        functools.partial(cross_weights_kernel, slots),
        "cross_weights",
        [shape_of(5 * inner, width, LOW), rows_low],
        [meta, grad_cross_q, normed_cross, grad_cross_sides, encoded, mixed_cross, branch_cross]
        + [mixed_self, branch_self]
        + layer_pieces,
        cost=2,
    )
    far, cross_weights = after((far, cross_weights), layer_out, *encoder_blocks, *([feed_most] if split else []))
    left = onchip(
        functools.partial(exit_kernel, slots),
        "self_exit",
        [sides_low] + [shape_of(share + 16, width, LOW)] * slots,
        [meta, keep, near, far, grad_queries, self_query, self_key, self_value, tokens]
        + [gain_grad_cross, gain_grad_feed],
        [total_room],
        cost=1,
    )
    grad_sides = left[0]
    left_blocks = trades(left[1:], "tensor")
    if split:
        feed_summed = [feed_most, send(after(feed_most, grad_sides), 1)]
    else:
        feed_summed = list(lax.psum(tuple(feed_weights), both))
    grad_up, grad_down = onchip(
        functools.partial(feed_finish_kernel, split),
        "feed_finish",
        [shape_of(width, hidden_up.shape[1], F32)] * 2,
        [meta] + feed_summed,
        cost=3,
    )
    left_blocks = after(tuple(left_blocks), grad_up)
    hidden_rows, encoder_rows, gains = onchip(
        functools.partial(last_rows_kernel, slots),
        "last_rows",
        [part_low, part_low, sum_row],
        [meta, after_self_rows, tokens, gain_one] + list(left_blocks) + encoder_blocks,
        cost=1,
    )
    weight_rows = -(-(8 * inner + 16) // 128) * 128
    hot = jnp.asarray(np.pad(span_onehot(), ((0, 0), (0, 128 - BUCKETS))), LOW)
    payload = onchip(
        functools.partial(payload_kernel, split),
        "last_weights",
        [shape_of(weight_rows // 2, width, LOW)] * 2 if split else [shape_of(weight_rows, width, LOW)],
        [meta, cross_weights, normed_self, grad_queries, grad_sides, diagonals, hot],
        [pltpu.VMEM((weight_rows, width), LOW)],
        cost=2,
    )
    if split:
        rows = weight_rows // 8
        quarters = onchip(
            quarter_kernel,
            "quarters",
            [shape_of(rows, width, LOW)] * 4,
            [meta, payload[0], send(payload[1], 1)],
            [pltpu.VMEM((4 * rows, width), F32)],
            cost=1,
        )
        (own,) = onchip(
            own_kernel,
            "own_eighth",
            [shape_of(rows + 16, width, LOW)],
            [meta, quarters[0]] + [send(quarters[flip], 2 * flip) for flip in (1, 2, 3)] + [gains],
            cost=1,
        )
        summed = [own] + [send(own, 2 * flip) for flip in (1, 2, 3)]
    else:
        summed = [lax.psum(payload[0], both)]
        gains = lax.psum(gains, both)
    grad_hidden = gather_rows(hidden_rows, "tensor")
    grad_hidden, gathered_encoder, *near_blocks = after((grad_hidden, encoder_rows) + tuple(summed if split else ()), hidden_rows)
    encoder_pieces = swaps(gathered_encoder, "tensor")
    if split:
        summed = list(near_blocks) + [send(block, 1) for block in near_blocks]
    weights = onchip(
        functools.partial(finish_kernel, split),
        "finish",
        [shape_of(inner, width, F32)] * 8 + [shape_of(16, width, F32)] + [sum_row] * split + [rows_low],
        [meta] + summed + [grad_hidden],
        [pltpu.VMEM((weight_rows, width), F32)],
        cost=3,
    )
    if split:
        gains = weights[9]
    (grad_encoder,) = onchip(
        functools.partial(gather_kernel, slots), "encoder_rows", [rows_low], [meta] + list(after(tuple(encoder_pieces), weights[0])), cost=1
    )
    return (
        layer_out[None],
        weights[-1][None],
        grad_encoder[None],
        gains[0],
        gains[1],
        gains[2],
        weights[5].T,
        weights[6].T,
        weights[7].T,
        weights[4],
        weights[8][:heads, :BUCKETS].T,
        weights[0].T,
        weights[1].T,
        weights[2].T,
        weights[3],
        grad_up,
        grad_down,
    )


def solution(mesh):
    rows = P("dp", "ctx", None)
    ids = P("dp", None)
    columns = P(None, "tensor")
    shards = P("tensor", None)
    placed = (
        (rows, rows, ids, ids, P(), P(), P())
        + (columns, columns, columns, shards, columns, columns, columns, columns, shards)
        + (columns, shards, rows)
    )
    given = (
        (rows, rows, rows, P(), P(), P())
        + (columns, columns, columns, shards, columns, columns, columns, columns, shards)
        + (columns, shards)
    )
    return jax.shard_map(body, mesh=mesh, in_specs=placed, out_specs=given, check_vma=False)
```

```python
import math
import functools
import numpy as np
import jax
import jax.numpy as jnp
from jax import lax
from jax.sharding import PartitionSpec as P
from jax.experimental import pallas as pl
from jax.experimental.pallas import tpu as pltpu

BUCKETS = 32
MAXDIST = 128
DOCS = 8
EPSILON = 1e-06
MASKED = -1000000000.0
MASK_WEIGHT = -float(2**30)
CURVE_SCALE = math.sqrt(2.0 / math.pi)
CUBIC_TERM = 0.044715
HIGHEST = lax.Precision.HIGHEST

HEAD = 64
KEYS = 256
WIDE = 256
SPAN = 1280
VMEM_BYTES = 60 * 1024 * 1024


def position_bucket(distance):
    exact_cut = BUCKETS // 2
    if distance < exact_cut:
        return distance
    scaled = math.log(distance / exact_cut) / math.log(MAXDIST / exact_cut) * (BUCKETS - exact_cut)
    return min(exact_cut + int(scaled), BUCKETS - 1)


def span_onehot():
    table = np.zeros((SPAN, BUCKETS), np.float32)
    for place in range(KEYS, KEYS + 3 * KEYS):
        table[place, position_bucket(place - KEYS)] = 1.0
    return table


def taking(microseconds):
    return pl.CostEstimate(flops=int(microseconds * 1e9), transcendentals=0, bytes_accessed=int(microseconds * 3.5e6))


def dot_nt(left, right):
    return lax.dot_general(left, right, (((1,), (1,)), ((), ())), preferred_element_type=jnp.float32)


def dot_nn(left, right):
    return lax.dot_general(left, right, (((1,), (0,)), ((), ())), preferred_element_type=jnp.float32)


def onehot_rows(count, first, meta, base):
    lane = lax.broadcasted_iota(jnp.int32, (1, HEAD), 1)
    low = jnp.zeros((1, HEAD), jnp.int32)
    high = jnp.zeros((1, HEAD), jnp.int32)
    for d in range(DOCS):
        low = jnp.where(lane == d, meta[base + d], low)
        high = jnp.where(lane == d, meta[base + d + 1], high)
    place = lax.broadcasted_iota(jnp.int32, (count, HEAD), 0) + first
    return (place >= low) & (place < high)


def head_mask(width, first, head, feature_from):
    lane = lax.broadcasted_iota(jnp.int32, (1, width), 1)
    start = first + head * HEAD
    keep = (lane >= start) & (lane < start + HEAD)
    if feature_from is not None:
        keep = keep | (lane >= feature_from)
    return keep.astype(jnp.float32).astype(jnp.bfloat16)


def gather_blocks(meta, parts, kvs, kext, key_base):
    rows = parts[0].shape[0]
    me = meta[1]
    inner = kext.shape[1] - HEAD
    for r, part in enumerate(parts):
        at = pl.multiple_of(jnp.bitwise_xor(me, r) * rows, rows)
        kvs[pl.ds(at, rows), :] = part[...]
        kext[pl.ds(at, rows), 0:inner] = part[:, 0:inner]
        kext[pl.ds(at, rows), inner:] = onehot_rows(rows, at, meta, key_base).astype(jnp.float32).astype(jnp.bfloat16)


def query_heads(meta, q_ref, qx, qm, heads, query_base):
    rows, inner = q_ref.shape
    own = onehot_rows(rows, meta[0], meta, query_base)
    qx[:, 0:inner] = q_ref[...]
    qx[:, inner:] = jnp.where(own, 0.0, MASK_WEIGHT).astype(jnp.bfloat16)
    for h in range(heads):
        qm[h] = qx[...] * head_mask(qx.shape[1], 0, h, inner)


def tile_kernel(u_ref, tile):
    for h in range(tile.shape[0]):
        row = jnp.broadcast_to(u_ref[h : h + 1, :], (KEYS, SPAN))
        tile[h] = pltpu.roll(row, 0, 1, stride=1, stride_axis=0)[:, 0 : 4 * KEYS]


def key_range(meta, rows, query_base, key_base):
    first = meta[0]
    last = first + rows - 1
    low = meta[key_base]
    high = meta[key_base + 1]
    for d in range(1, DOCS):
        low = jnp.where(meta[query_base + d] <= first, meta[key_base + d], low)
        high = jnp.where(meta[query_base + d] <= last, meta[key_base + d + 1], high)
    return lax.div(low, KEYS), lax.div(high + KEYS - 1, KEYS)


def for_blocks(meta, rows, causal, query_base, key_base, step, carry):
    low, high = key_range(meta, rows, query_base, key_base)
    if not causal:
        return lax.fori_loop(
            lax.div(low, 2), lax.div(high + 1, 2), lambda kb, c: step(2 * kb + 1, None, step(2 * kb, None, c)), carry
        )
    near = lax.div(meta[0], KEYS)
    carry = lax.fori_loop(
        lax.div(low, 2), lax.div(near, 2) - 1, lambda kb, c: step(2 * kb + 1, None, step(2 * kb, None, c)), carry
    )
    carry = lax.cond(
        near > 0, lambda c: step(near - 1, 2 * KEYS, step(near - 2, None, c)), lambda c: c, carry
    )
    carry = step(near, KEYS, carry)
    return step(near + 1, 0, carry)


def forward_kernel(causal, heads, count, meta, *refs):
    if causal:
        u_ref, tile = refs[:2]
        refs = refs[2:]
    q_ref, refs = refs[0], refs[1:]
    parts, refs = refs[:count], refs[count:]
    out_ref, lse_ref = refs[:2]
    refs = refs[2:]
    kvs, kext, vt, qx, qm, ot = refs
    query_base = 2
    key_base = 2 if causal else 2 + DOCS + 1
    rows = q_ref.shape[0]
    gather_blocks(meta, parts, kvs, kext, key_base)
    query_heads(meta, q_ref, qx, qm, heads, query_base)
    lanes = kvs.shape[1]
    for kb in range(kvs.shape[0] // KEYS):
        vt[kb] = kvs[kb * KEYS : (kb + 1) * KEYS, lanes - WIDE :].T
    ot[...] = jnp.zeros_like(ot)
    shift = WIDE - heads * HEAD

    def step(kb, place, carry):
        kx = kext[pl.ds(pl.multiple_of(kb * KEYS, KEYS), KEYS), :]
        scores = [dot_nt(kx, qm[h]) for h in range(heads)]
        tops, sums = carry
        new_tops, new_sums = [], []
        for h in range(heads):
            far = 0.0
            if place is not None:
                scores[h] = scores[h] + tile[h, :, place : place + rows]
            elif causal:
                far = u_ref[h : h + 1, 4 * KEYS - 1 : 4 * KEYS]
            after = jnp.maximum(tops[h], jnp.max(scores[h], axis=0, keepdims=True) + far)
            scale = jnp.exp(tops[h] - after)
            weights = jnp.exp(scores[h] - (after - far))
            new_tops.append(after)
            new_sums.append(sums[h] * scale + jnp.sum(weights.reshape(KEYS // 8, 8, rows), axis=0))
            own = vt[kb, shift + h * HEAD : shift + (h + 1) * HEAD, :]
            at = slice(h * HEAD, (h + 1) * HEAD)
            ot[at, :] = ot[at, :] * scale + dot_nn(own, weights.astype(jnp.bfloat16))
        return new_tops, new_sums

    carry = (
        [jnp.full((1, rows), -3e38, jnp.float32)] * heads,
        [jnp.zeros((8, rows), jnp.float32)] * heads,
    )
    tops, sums = for_blocks(meta, rows, causal, query_base, key_base, step, carry)
    lse_ref[...] = jnp.zeros_like(lse_ref)
    for h in range(heads):
        at = slice(h * HEAD, (h + 1) * HEAD)
        total = jnp.sum(sums[h], axis=0, keepdims=True)
        out_ref[at, :] = (ot[at, :] / total).astype(jnp.bfloat16)
        lse_ref[h : h + 1, :] = tops[h] + jnp.log(total)


def attend(causal, heads, meta, u, queries, parts):
    rows, inner = queries.shape
    part_rows, lanes = parts[0].shape
    count = len(parts)
    length = part_rows * count
    smem = pl.BlockSpec(memory_space=pltpu.SMEM)
    vmem = pl.BlockSpec(memory_space=pltpu.VMEM)
    given = list(u) + [queries] + list(parts)
    scratch = [
        pltpu.VMEM((length, lanes), jnp.bfloat16),
        pltpu.VMEM((length, inner + HEAD), jnp.bfloat16),
        pltpu.VMEM((length // KEYS, WIDE, KEYS), jnp.bfloat16),
        pltpu.VMEM((rows, inner + HEAD), jnp.bfloat16),
        pltpu.VMEM((heads, rows, inner + HEAD), jnp.bfloat16),
        pltpu.VMEM((inner, rows), jnp.float32),
    ]
    out_shape = [
        jax.ShapeDtypeStruct((inner, rows), jnp.bfloat16),
        jax.ShapeDtypeStruct((8, rows), jnp.float32),
    ]
    return pl.pallas_call(
        functools.partial(forward_kernel, causal, heads, count),
        out_shape=tuple(out_shape),
        in_specs=[smem] + [vmem] * len(given),
        out_specs=tuple([vmem] * len(out_shape)),
        scratch_shapes=scratch,
        compiler_params=pltpu.CompilerParams(vmem_limit_bytes=22 * 1024 * 1024),
        cost_estimate=taking(9),
        name="self_forward" if causal else "cross_forward",
    )(meta, *given)


def fold_diagonals(values):
    half = values.shape[0] // 2
    while half >= 1:
        values = values[:half] + pltpu.roll(values[half : 2 * half], SPAN - half, 1)
        half = half // 2
    return values


def backward_kernel(causal, heads, count, branch_count, meta, *refs):
    if causal:
        u_ref, tile = refs[:2]
        refs = refs[2:]
    q_ref, out_weight, mixed_ref, lse_ref = refs[:4]
    parts, refs = refs[4 : 4 + count], refs[4 + count :]
    branches, refs = refs[:branch_count], refs[branch_count:]
    dq_ref = refs[0]
    keep_ref, send_ref, refs = refs[1], refs[2], refs[3:]
    if causal:
        dbias_ref = refs[0]
        refs = refs[1:]
    branch_ref = branches[0]
    kvs, kext, kt, qx, qm, dom, ra, rb, dqt, row, dkv, do_ref = refs[:12]
    query_base = 2
    key_base = 2 if causal else 2 + DOCS + 1
    rows, inner = q_ref.shape
    lanes = kvs.shape[1]
    do_ref[:, 0:inner] = jnp.zeros((rows, inner), jnp.bfloat16)
    do_ref[:, inner:] = dot_nt(branch_ref[...], out_weight[...]).astype(jnp.bfloat16)
    gather_blocks(meta, parts, kvs, kext, key_base)
    query_heads(meta, q_ref, qx, qm, heads, query_base)
    for kb in range(kvs.shape[0] // KEYS):
        kt[kb] = kvs[kb * KEYS : (kb + 1) * KEYS, 0:WIDE].T
    shift = WIDE - inner
    for h in range(heads):
        dom[h] = do_ref[:, lanes - WIDE :] * head_mask(WIDE, shift, h, None)
        ra[h * rows : (h + 1) * rows, :] = q_ext_only(qx, h, inner)
    ra[heads * rows :, :] = do_ref[:, 0:WIDE] * head_mask(WIDE, inner, 0, None)
    for h in range(1, heads):
        rb[(h - 1) * rows : h * rows, :] = do_ref[:, WIDE:] * head_mask(lanes - WIDE, inner - WIDE, h, None)
    turned = do_ref[:, lanes - WIDE :].astype(jnp.float32).T
    inner_sum = turned[shift:, :] * mixed_ref[...].astype(jnp.float32)
    for h in range(heads):
        row[h : h + 1, :] = jnp.sum(inner_sum[h * HEAD : (h + 1) * HEAD, :], axis=0, keepdims=True)
    dqt[...] = jnp.zeros_like(dqt)
    dkv[...] = jnp.zeros_like(dkv)
    if causal:
        dtile, dfar = refs[12:14]
        dtile[...] = jnp.zeros_like(dtile)
        dfar[...] = jnp.zeros_like(dfar)

    def step(kb, place):
        at_keys = pl.ds(pl.multiple_of(kb * KEYS, KEYS), KEYS)
        kx = kext[at_keys, :]
        vx = kvs[at_keys, lanes - WIDE :]
        weights_low = []
        grads_low = []
        all_scores = [dot_nt(kx, qm[h]) for h in range(heads)]
        all_grads = [dot_nt(vx, dom[h]) for h in range(heads)]
        for h in range(heads):
            scores = all_scores[h]
            lse = lse_ref[h : h + 1, :]
            if place is not None:
                scores = scores + tile[h, :, place : place + rows]
            elif causal:
                lse = lse - u_ref[h : h + 1, 4 * KEYS - 1 : 4 * KEYS]
            weights = jnp.exp(scores - lse)
            grads = weights * (all_grads[h] - row[h : h + 1, :])
            low = grads.astype(jnp.bfloat16)
            weights_low.append(weights.astype(jnp.bfloat16))
            grads_low.append(low)
            if causal:
                if place is not None:
                    dtile[h, :, place : place + rows] += grads
                else:
                    dfar[8 * h : 8 * h + 8, :] += jnp.sum(grads.reshape(KEYS // 8, 8, rows), axis=0)
        for h in range(heads):
            at = slice(h * HEAD, (h + 1) * HEAD)
            dqt[at, :] += dot_nn(kt[kb, at, :], grads_low[h])
        dkv[at_keys, 0:WIDE] = dot_nn(jnp.concatenate(grads_low + weights_low[:1], axis=1), ra[...]).astype(jnp.bfloat16)
        dkv[at_keys, WIDE:] = dot_nn(jnp.concatenate(weights_low[1:], axis=1), rb[...]).astype(jnp.bfloat16)

    for_blocks(meta, rows, causal, query_base, key_base, lambda kb, place, c: (step(kb, place), c)[1], 0)
    dq_ref[...] = dqt[...].astype(jnp.bfloat16)
    me = meta[1]
    part_rows = parts[0].shape[0]
    for r in range(count):
        at = pl.multiple_of(jnp.bitwise_xor(me, r) * part_rows, part_rows)
        to = (r // 2) * part_rows
        (send_ref if r % 2 else keep_ref)[to : to + part_rows, :] = dkv[pl.ds(at, part_rows), :]
    if causal:
        lane = lax.broadcasted_iota(jnp.int32, (1, SPAN), 1)
        dbias_ref[...] = jnp.zeros_like(dbias_ref)
        for h in range(heads):
            padded = jnp.concatenate([dtile[h], jnp.zeros((KEYS, SPAN - 4 * KEYS), jnp.float32)], axis=1)
            far = jnp.sum(jnp.sum(dfar[8 * h : 8 * h + 8, :], axis=0, keepdims=True), axis=1, keepdims=True)
            dbias_ref[h : h + 1, :] = fold_diagonals(padded) + jnp.where(lane == 4 * KEYS - 1, far, 0.0)


def q_ext_only(qx, head, inner):
    return qx[...] * head_mask(qx.shape[1], 0, head, None)


def attend_back(causal, heads, meta, u, queries, out_weight, mixed, lse, parts, branches):
    rows, inner = queries.shape
    part_rows, lanes = parts[0].shape
    count = len(parts)
    length = part_rows * count
    smem = pl.BlockSpec(memory_space=pltpu.SMEM)
    vmem = pl.BlockSpec(memory_space=pltpu.VMEM)
    given = list(u) + [queries, out_weight, mixed, lse] + list(parts) + list(branches)
    out_shape = [jax.ShapeDtypeStruct((inner, rows), jnp.bfloat16)]
    out_shape += [jax.ShapeDtypeStruct((length // 2, lanes), jnp.bfloat16)] * 2
    if causal:
        out_shape.append(jax.ShapeDtypeStruct((8, SPAN), jnp.float32))
    scratch = [
        pltpu.VMEM((length, lanes), jnp.bfloat16),
        pltpu.VMEM((length, inner + HEAD), jnp.bfloat16),
        pltpu.VMEM((length // KEYS, WIDE, KEYS), jnp.bfloat16),
        pltpu.VMEM((rows, inner + HEAD), jnp.bfloat16),
        pltpu.VMEM((heads, rows, inner + HEAD), jnp.bfloat16),
        pltpu.VMEM((heads, rows, WIDE), jnp.bfloat16),
        pltpu.VMEM(((heads + 1) * rows, WIDE), jnp.bfloat16),
        pltpu.VMEM(((heads - 1) * rows, lanes - WIDE), jnp.bfloat16),
        pltpu.VMEM((inner, rows), jnp.float32),
        pltpu.VMEM((8, rows), jnp.float32),
        pltpu.VMEM((length, lanes), jnp.bfloat16),
        pltpu.VMEM((rows, lanes), jnp.bfloat16),
    ]
    if causal:
        scratch += [
            pltpu.VMEM((heads, KEYS, 4 * KEYS), jnp.float32),
            pltpu.VMEM((8 * heads, rows), jnp.float32),
        ]
    return pl.pallas_call(
        functools.partial(backward_kernel, causal, heads, count, len(branches)),
        out_shape=tuple(out_shape),
        in_specs=[smem] + [vmem] * len(given),
        out_specs=tuple([vmem] * len(out_shape)),
        scratch_shapes=scratch,
        compiler_params=pltpu.CompilerParams(vmem_limit_bytes=22 * 1024 * 1024),
        cost_estimate=taking(13),
        name="self_backward" if causal else "cross_backward",
    )(meta, *given)


def position_rows(bias_table, heads):
    table = span_onehot()
    rows = jnp.dot(bias_table.astype(jnp.bfloat16).T, jnp.asarray(table.T, jnp.bfloat16), preferred_element_type=jnp.float32)
    rows = rows + jnp.asarray(np.where(table.sum(1) > 0, 0.0, MASKED)[None, :], jnp.float32)
    return jnp.concatenate([rows, jnp.zeros((8 - heads, SPAN), jnp.float32)], axis=0)


def make_meta(dec_row, enc_row, offset, place, rest):
    docs = jnp.arange(DOCS + 1, dtype=jnp.int32)
    dec = jnp.sum((dec_row[None, :] < docs[:, None]).astype(jnp.int32), axis=1)
    enc = jnp.sum((enc_row[None, :] < docs[:, None]).astype(jnp.int32), axis=1)
    first = jnp.stack([offset, place]).astype(jnp.int32)
    return jnp.concatenate([first, dec, enc, jnp.stack(rest).astype(jnp.int32)])


def room(*groups):
    total = 0
    for group in groups:
        for x in group:
            rows = int(np.prod(x.shape[:-1])) if x.shape else 1
            lanes = -(-x.shape[-1] // 128) * 128 if x.shape else 128
            total += max(rows, 8) * lanes * jnp.dtype(x.dtype).itemsize
    return total + total // 2 + 3 * 1024 * 1024


def onchip(kernel, name, out_shape, given, scratch=(), cost=2, table=True):
    vmem = pl.BlockSpec(memory_space=pltpu.VMEM)
    in_specs = [pl.BlockSpec(memory_space=pltpu.SMEM)] + [vmem] * (len(given) - 1)
    if not table:
        in_specs = [vmem] * len(given)
    return pl.pallas_call(
        kernel,
        out_shape=tuple(out_shape),
        in_specs=in_specs,
        out_specs=tuple([vmem] * len(out_shape)),
        scratch_shapes=list(scratch),
        compiler_params=pltpu.CompilerParams(vmem_limit_bytes=room(out_shape, given, scratch)),
        cost_estimate=taking(cost),
        name=name,
    )(*given)


def shape_of(rows, columns, kind):
    return jax.ShapeDtypeStruct((rows, columns), kind)


F32 = jnp.float32
LOW = jnp.bfloat16
AT_SLOT = 2 + 2 * (DOCS + 1)
AT_ODD = AT_SLOT + 1
AT_HALF = AT_SLOT + 2
AT_QUARTER = AT_SLOT + 3
AT_DP = AT_SLOT + 4
AT_FAR = AT_SLOT + 5


def plain_of(values):
    scale = lax.rsqrt(jnp.mean(values * values, axis=-1, keepdims=True) + EPSILON)
    return values * scale, scale


def input_gradient(grad_normed, plain, scale, gain):
    grad_plain = grad_normed * gain
    inner = jnp.mean(grad_plain * plain, axis=-1, keepdims=True)
    return scale * (grad_plain - plain * inner)


def sides_kernel(x_ref, gain_ref, k_ref, v_ref, normed_ref, out_ref):
    plain, _ = plain_of(x_ref[...].astype(F32))
    normed = (plain * gain_ref[...].astype(F32)).astype(LOW)
    normed_ref[...] = normed
    out_ref[...] = dot_nt(normed, jnp.concatenate([k_ref[...], v_ref[...]], axis=0)).astype(LOW)


def others_kernel(normed_ref, q_ref, enc_ref, k_ref, v_ref, out_ref, sides_ref):
    out_ref[...] = dot_nt(normed_ref[...], q_ref[...]).astype(LOW)
    sides_ref[...] = dot_nt(enc_ref[...], jnp.concatenate([k_ref[...], v_ref[...]], axis=0)).astype(LOW)


def weights_kernel(count, meta, own_ref, other_ref, *outs):
    parts = 4
    rows = outs[0].shape[0] // (count * parts)
    for side, ref in enumerate((own_ref, other_ref)):
        for b in range(2):
            part = 2 * jnp.bitwise_xor(meta[AT_ODD], side) + jnp.bitwise_xor(meta[AT_DP], b)
            for r in range(count):
                shard = jnp.bitwise_xor(meta[AT_SLOT], r)
                to = pl.multiple_of((shard * parts + part) * rows, rows)
                for w, out in enumerate(outs):
                    at = ((b * count + r) * len(outs) + w) * rows
                    out[pl.ds(to, rows), :] = ref[at : at + rows, :]


def pieces_kernel(meta, *refs):
    half = len(refs) // 2
    for weight, out in zip(refs[:half], refs[half:]):
        rows = out.shape[0]
        at = pl.multiple_of((2 * meta[AT_ODD] + meta[AT_DP]) * rows, rows)
        out[...] = weight[pl.ds(at, rows), :]


def lay_blocks(meta, blocks, whole):
    rows = blocks[0].shape[0]
    for r, block in enumerate(blocks):
        at = pl.multiple_of(jnp.bitwise_xor(meta[AT_SLOT], r) * rows, rows)
        whole[pl.ds(at, rows), :] = block[...]


def deal_blocks(meta, whole, blocks):
    rows = blocks[0].shape[0]
    for r, block in enumerate(blocks):
        at = pl.multiple_of(jnp.bitwise_xor(meta[AT_SLOT], r) * rows, rows)
        block[...] = whole[pl.ds(at, rows), :].astype(block.dtype)


def cross_entry_kernel(count, meta, x_ref, *refs):
    mixed, weight, gain_ref, q_ref, after_ref, normed_ref, out_ref = refs
    after = x_ref[...].astype(F32) + dot_nn(mixed[...].T, weight[...])
    after_ref[...] = after
    plain, _ = plain_of(after)
    normed = (plain * gain_ref[...].astype(F32)).astype(LOW)
    normed_ref[...] = normed
    out_ref[...] = dot_nt(normed, q_ref[...]).astype(LOW)


def feed_kernel(count, meta, after_ref, mixed, weight, gain_ref, up_ref, down_ref, grad_ref, *refs):
    rows_ref, normed_ref, active_ref, pre_ref, gain_grad_ref = refs[:5]
    dealt = refs[5 : 5 + count]
    part, total = refs[5 + count :]
    total[...] = after_ref[...] + dot_nn(mixed[...].T, weight[...])
    deal_blocks(meta, total, [rows_ref])
    plain, _ = plain_of(total[...])
    normed = (plain * gain_ref[...].astype(F32)).astype(LOW)
    normed_ref[...] = normed
    pre = dot_nn(normed, up_ref[...])
    squared = pre * pre
    bent = jnp.tanh(CURVE_SCALE * pre * (1.0 + CUBIC_TERM * squared))
    active_ref[...] = (0.5 * pre * (1.0 + bent)).astype(LOW)
    slope = 0.5 * (1.0 + bent) + 0.5 * pre * (1.0 - bent * bent) * CURVE_SCALE * (
        1.0 + 3.0 * CUBIC_TERM * squared
    )
    grad_pre = (dot_nt(grad_ref[...], down_ref[...]) * slope).astype(LOW)
    pre_ref[...] = grad_pre
    part[...] = dot_nt(grad_pre, up_ref[...])
    deal_blocks(meta, part, dealt)
    gain_grad_ref[...] = jnp.broadcast_to(
        jnp.sum(part[...] * plain, axis=0, keepdims=True), gain_grad_ref.shape
    )


def feed_back_kernel(count, meta, rows_ref, grad_ref, gain_ref, *refs):
    blocks, out_ref = refs[:count], refs[count]
    grad = blocks[0][...].astype(F32)
    for block in blocks[1:]:
        grad = grad + block[...].astype(F32)
    plain, scale = plain_of(rows_ref[...])
    rows = rows_ref.shape[0]
    own = grad_ref[pl.ds(pl.multiple_of(meta[AT_SLOT] * rows, rows), rows), :].astype(F32)
    out_ref[...] = (own + input_gradient(grad, plain, scale, gain_ref[...].astype(F32))).astype(LOW)


def layer_kernel(count, meta, active_ref, down_ref, *refs):
    dealt, part = refs[:count], refs[count]
    part[...] = dot_nn(active_ref[...], down_ref[...])
    deal_blocks(meta, part, dealt)


def far_kernel(meta, keep_ref, add_ref, out_ref):
    rows = out_ref.shape[0]
    out_ref[...] = (keep_ref[rows:, :].astype(F32) + add_ref[rows:, :].astype(F32)).astype(LOW)


def encoder_kernel(count, meta, keep_ref, add_ref, recv_ref, k_ref, v_ref, *refs):
    sides_ref, dealt, part = refs[0], refs[1 : count + 1], refs[count + 1]
    near = keep_ref.shape[0] // 2
    sides = (
        keep_ref[0:near, :].astype(F32) + add_ref[0:near, :].astype(F32) + recv_ref[...].astype(F32)
    ).astype(LOW)
    sides_ref[...] = sides
    part[...] = dot_nn(sides, jnp.concatenate([k_ref[...], v_ref[...]], axis=0))
    deal_blocks(meta, part, dealt)


def layer_sum_kernel(count, meta, rows_ref, *refs):
    blocks, out_ref = refs[:count], refs[count]
    rows = rows_ref[...]
    for block in blocks:
        rows = rows + block[...].astype(F32)
    out_ref[...] = rows.astype(LOW)


def self_entry_kernel(count, meta, after_ref, *refs):
    turned, weight, gain_ref, branch_ref, rows_ref, out_ref, gain_grad_ref, total = refs
    part = dot_nn(turned[...].T, weight[...])
    plain, scale = plain_of(after_ref[...])
    grad = branch_ref[...].astype(F32) + input_gradient(part, plain, scale, gain_ref[...].astype(F32))
    total[...] = grad
    out_ref[...] = grad.astype(LOW)
    deal_blocks(meta, total, [rows_ref])
    share = 1.0 / count
    gain_grad_ref[...] = jnp.broadcast_to(
        share * jnp.sum(part * plain, axis=0, keepdims=True), gain_grad_ref.shape
    )


def exit_kernel(count, meta, keep_ref, add_ref, recv_ref, dq_ref, q_ref, k_ref, v_ref, x_ref, g2_ref, g3_ref, *refs):
    sides_ref, dealt, part = refs[0], refs[1 : 1 + count], refs[1 + count]
    rows = keep_ref.shape[0] // 2
    sides = (
        keep_ref[0:rows, :].astype(F32) + add_ref[0:rows, :].astype(F32) + recv_ref[...].astype(F32)
    ).astype(LOW)
    sides_ref[...] = sides
    part[...] = dot_nn(dq_ref[...].T, q_ref[...]) + dot_nn(
        sides, jnp.concatenate([k_ref[...], v_ref[...]], axis=0)
    )
    plain, _ = plain_of(x_ref[...].astype(F32))
    first = jnp.sum(part[...] * plain, axis=0, keepdims=True)
    row = lax.broadcasted_iota(jnp.int32, (8, first.shape[1]), 0)
    gains = jnp.where(row == 0, first, jnp.where(row == 1, g2_ref[...], g3_ref[...]))
    high = gains.astype(LOW)
    rest = (gains - high.astype(F32)).astype(LOW)
    share = dealt[0].shape[0] - 16
    for r, out in enumerate(dealt):
        at = pl.multiple_of(jnp.bitwise_xor(meta[AT_SLOT], r) * share, share)
        out[0:share, :] = part[pl.ds(at, share), :].astype(LOW)
        out[share:, :] = jnp.concatenate([high, rest], axis=0)


def last_rows_kernel(count, meta, rows_ref, x_ref, gain_ref, *refs):
    blocks, pairs = refs[:count], refs[count : 2 * count]
    out_ref, second_ref, gains_ref = refs[2 * count :]
    rows = rows_ref.shape[0]
    grad = blocks[0][...].astype(F32)
    for block in blocks[1:]:
        grad = grad + block[...].astype(F32)
    gains_ref[...] = grad[rows : rows + 8, :] + grad[rows + 8 :, :]
    own = x_ref[pl.ds(pl.multiple_of(meta[AT_SLOT] * rows, rows), rows), :].astype(F32)
    plain, scale = plain_of(own)
    out_ref[...] = (
        rows_ref[...] + input_gradient(grad[0:rows, :], plain, scale, gain_ref[...].astype(F32))
    ).astype(LOW)
    total = pairs[0][...].astype(F32)
    for pair in pairs[1:]:
        total = total + pair[...].astype(F32)
    second_ref[...] = total.astype(LOW)


def layer_rows_kernel(count, meta, *refs):
    lay_blocks(meta, refs[:count], refs[count])


def pair_rows_kernel(count, meta, *refs):
    blocks, first_ref, second_ref = refs[:count], refs[count], refs[count + 1]
    rows = blocks[0].shape[0] // 2
    for r, block in enumerate(blocks):
        at = pl.multiple_of(jnp.bitwise_xor(meta[AT_SLOT], r) * rows, rows)
        first_ref[pl.ds(at, rows), :] = block[0:rows, :]
        second_ref[pl.ds(at, rows), :] = block[rows:, :]


def feed_weights_kernel(split, meta, normed_ref, pre_ref, active_ref, grad_ref, first_ref, second_ref):
    up = dot_nn(normed_ref[...].T, pre_ref[...]).astype(LOW)
    down = dot_nn(active_ref[...].T, grad_ref[...]).astype(LOW)
    if not split:
        first_ref[...] = up
        second_ref[...] = down
        return
    half = meta[AT_HALF]

    @pl.when(half == 0)
    def _():
        first_ref[...] = up
        second_ref[...] = down

    @pl.when(half == 1)
    def _():
        first_ref[...] = down
        second_ref[...] = up


def cross_weights_kernel(count, meta, dq_ref, normed_ref, sides_ref, enc_ref, mixed_cross_ref, branch_cross_ref, *refs):
    mixed_self_ref, branch_self_ref = refs[:2]
    blocks, out_ref, layer_ref = refs[2 : 2 + count], refs[2 + count], refs[3 + count]
    inner = dq_ref.shape[0]
    out_ref[0:inner, :] = dot_nn(dq_ref[...], normed_ref[...]).astype(LOW)
    out_ref[inner : 3 * inner, :] = dot_nn(sides_ref[...].T, enc_ref[...]).astype(LOW)
    out_ref[3 * inner : 4 * inner, :] = dot_nn(mixed_cross_ref[...], branch_cross_ref[...]).astype(LOW)
    out_ref[4 * inner :, :] = dot_nn(mixed_self_ref[...], branch_self_ref[...]).astype(LOW)
    lay_blocks(meta, blocks, layer_ref)


def payload_kernel(split, meta, cross_ref, normed_ref, dq_ref, sides_ref, bias_ref, hot_ref, *refs):
    outs, whole = refs[:-1], refs[-1]
    inner = dq_ref.shape[0]
    width = normed_ref.shape[1]
    at = 5 * inner
    whole[0:at, :] = cross_ref[...]
    whole[at : at + inner, :] = dot_nn(dq_ref[...], normed_ref[...]).astype(LOW)
    whole[at + inner : at + 3 * inner, :] = dot_nn(sides_ref[...].T, normed_ref[...]).astype(LOW)
    diagonal = bias_ref[...]
    high = diagonal.astype(LOW)
    rest = (diagonal - high.astype(F32)).astype(LOW)
    bias = dot_nn(high, hot_ref[...]) + dot_nn(rest, hot_ref[...])
    bias = jnp.concatenate([bias, jnp.zeros((8, width - bias.shape[1]), F32)], axis=1)
    at = at + 3 * inner
    whole[at : at + 16, :] = jnp.concatenate([bias, jnp.zeros_like(bias)], axis=0).astype(LOW)
    whole[at + 16 :, :] = jnp.zeros((whole.shape[0] - at - 16, width), LOW)
    if not split:
        outs[0][...] = whole[...]
        return
    rows = whole.shape[0] // 2
    half = meta[AT_HALF]
    outs[0][...] = whole[pl.ds(pl.multiple_of(half * rows, rows), rows), :]
    outs[1][...] = whole[pl.ds(pl.multiple_of((1 - half) * rows, rows), rows), :]


def quarter_kernel(meta, keep_ref, recv_ref, *refs):
    blocks, total = refs[:4], refs[4]
    total[...] = keep_ref[...].astype(F32) + recv_ref[...].astype(F32)
    rows = blocks[0].shape[0]
    for f in range(4):
        at = pl.multiple_of(jnp.bitwise_xor(meta[AT_QUARTER], f) * rows, rows)
        blocks[f][...] = total[pl.ds(at, rows), :].astype(LOW)


def gather_kernel(count, meta, *refs):
    lay_blocks(meta, refs[:count], refs[count])


def halves_kernel(at_bit, meta, keep_ref, recv_ref, first_ref, second_ref, total):
    total[...] = keep_ref[...].astype(F32) + recv_ref[...].astype(F32)
    rows = first_ref.shape[0]
    bit = meta[at_bit]
    first_ref[...] = total[pl.ds(pl.multiple_of(bit * rows, rows), rows), :].astype(LOW)
    second_ref[...] = total[pl.ds(pl.multiple_of((1 - bit) * rows, rows), rows), :].astype(LOW)


def join_kernel(at_bit, meta, own_ref, other_ref, out_ref):
    rows = own_ref.shape[0]
    bit = meta[at_bit]
    out_ref[pl.ds(pl.multiple_of(bit * rows, rows), rows), :] = own_ref[...]
    out_ref[pl.ds(pl.multiple_of((1 - bit) * rows, rows), rows), :] = other_ref[...]


def feed_finish_kernel(split, meta, own_ref, other_ref, up_ref, down_ref):
    if not split:
        up_ref[...] = own_ref[...].astype(F32)
        down_ref[...] = other_ref[...].astype(F32)
        return

    @pl.when(meta[AT_HALF] == 0)
    def _():
        up_ref[...] = own_ref[...].astype(F32)
        down_ref[...] = other_ref[...].astype(F32)

    @pl.when(meta[AT_HALF] == 1)
    def _():
        up_ref[...] = other_ref[...].astype(F32)
        down_ref[...] = own_ref[...].astype(F32)


def own_kernel(meta, *refs):
    blocks, gains_ref, out_ref = refs[:4], refs[4], refs[5]
    rows = blocks[0].shape[0]
    total = blocks[0][...].astype(F32)
    for block in blocks[1:]:
        total = total + block[...].astype(F32)
    out_ref[0:rows, :] = total.astype(LOW)
    high = gains_ref[...].astype(LOW)
    rest = (gains_ref[...] - high.astype(F32)).astype(LOW)
    out_ref[rows:, :] = jnp.concatenate([high, rest], axis=0)


def finish_kernel(split, meta, *refs):
    count = 8 if split else 1
    parts, rows_ref, outs, copy_ref, whole = refs[:count], refs[count], refs[count + 1 : -2], refs[-2], refs[-1]
    copy_ref[...] = rows_ref[...]
    if split:
        outs, gains_ref = outs[:-1], outs[-1]
        rows = parts[0].shape[0] - 16
        gains = parts[0][rows:, :].astype(F32)
        for part in parts[1:]:
            gains = gains + part[rows:, :].astype(F32)
        gains_ref[...] = gains[0:8, :] + gains[8:, :]
        half = meta[AT_HALF]
        for i, part in enumerate(parts):
            side = half if i < 4 else 1 - half
            at = side * 4 * rows + jnp.bitwise_xor(meta[AT_QUARTER], i % 4) * rows
            whole[pl.ds(pl.multiple_of(at, rows), rows), :] = part[0:rows, :].astype(F32)
    else:
        whole[...] = parts[0][...].astype(F32)
    at = 0
    for out in outs:
        out[...] = whole[at : at + out.shape[0], :]
        at += out.shape[0]


def swap(values, axis, flip):
    count = lax.axis_size(axis)
    return lax.ppermute(values, axis, [(i, i ^ flip) for i in range(count)])


def swaps(values, axis):
    return [values] + [swap(values, axis, flip) for flip in range(1, lax.axis_size(axis))]


def trades(blocks, axis):
    return [blocks[0]] + [swap(block, axis, flip) for flip, block in enumerate(blocks) if flip]


def gather_rows(values, axis):
    return lax.all_gather(values, axis, axis=0, tiled=True)


def after(values, *others):
    return lax.optimization_barrier((values,) + others)[0]


def body(
    hidden_in,
    encoder_out,
    dec_segments,
    enc_segments,
    gain_self,
    gain_cross,
    gain_feed,
    self_query,
    self_key,
    self_value,
    self_output,
    bias_table,
    cross_query,
    cross_key,
    cross_value,
    cross_output,
    hidden_up,
    hidden_down,
    out_grad,
):
    tok_len, width = hidden_in.shape[1:]
    heads = bias_table.shape[1]
    inner = self_query.shape[1]
    place = lax.axis_index("ctx")
    slot = lax.axis_index("tensor")
    slots = lax.axis_size("tensor")
    split = lax.axis_size("dp") == 2 and lax.axis_size("ctx") == 4
    both = ("dp", "ctx")
    share = tok_len // slots
    lanes = 2 * inner
    odd = place & 1
    line = lax.axis_index("dp")
    combined = line * 4 + place
    meta = make_meta(
        dec_segments[0],
        enc_segments[0],
        place * tok_len,
        place,
        [slot, odd, combined & 1, (combined >> 1) & 3, line & 1, (place >> 1) & 1],
    )
    bias_rows = position_rows(bias_table, heads)
    tokens = hidden_in[0]
    encoded = encoder_out[0]
    cotangent = out_grad[0]
    gain_one = gain_self[None]
    gain_two = gain_cross[None]
    gain_three = gain_feed[None]
    rows_low = shape_of(tok_len, width, LOW)
    rows_full = shape_of(tok_len, width, F32)
    part_low = shape_of(share, width, LOW)
    part_full = shape_of(share, width, F32)
    sum_row = shape_of(8, width, F32)
    weight_low = shape_of(slots * inner, width, LOW)
    sides_low = shape_of(tok_len, lanes, LOW)
    mixed_room = pltpu.VMEM((slots * inner, tok_len), LOW)
    total_room = pltpu.VMEM((tok_len, width), F32)

    def send(block, flip):
        return lax.ppermute(block, both, [(i, i ^ flip) for i in range(8)])

    def add_halves(at_bit, keep, recv, name):
        rows, columns = keep.shape
        half = shape_of(rows // 2, columns, LOW)
        return onchip(
            functools.partial(halves_kernel, at_bit),
            name,
            [half, half],
            [meta, keep, recv],
            [pltpu.VMEM((rows, columns), F32)],
            cost=1,
        )

    def join(at_bit, own, other, name):
        rows, columns = own.shape
        return onchip(
            functools.partial(join_kernel, at_bit),
            name,
            [shape_of(2 * rows, columns, LOW)],
            [meta, own, other],
            cost=1,
        )[0]

    def far_sum(keep, add, name):
        return onchip(far_kernel, name, [sides_low], [meta, keep, add], cost=1)[0]

    self_query, self_key, self_value = self_query.T, self_key.T, self_value.T
    cross_query, cross_key, cross_value = cross_query.T, cross_key.T, cross_value.T

    def lay_weights(plane, other, count, name):
        return onchip(
            functools.partial(weights_kernel, slots),
            name,
            [weight_low] * count,
            [meta, plane, other],
            cost=1,
        )

    normed_self, own_sides = onchip(
        sides_kernel, "self_sides", [rows_low, sides_low], [tokens, gain_one, self_key, self_value], table=False
    )
    far_sides = swap(own_sides, "ctx", 2)
    queries, own_cross = onchip(
        others_kernel,
        "query_and_cross_sides",
        [shape_of(tok_len, inner, LOW), sides_low],
        [normed_self, self_query, encoded, cross_key, cross_value],
        table=False,
    )
    pieces = onchip(
        pieces_kernel,
        "pieces",
        [shape_of(inner // 4, width, LOW)] * 3,
        [meta, self_output, cross_output, after(cross_query, queries)],
        cost=1,
    )
    self_pieces = swaps(pieces[0], "tensor")
    cross_piece = after(jnp.concatenate(pieces[1:], axis=0), *self_pieces)
    cross_pieces = swaps(cross_piece, "tensor")
    column = jnp.concatenate(self_pieces, axis=0)
    far_column = swap(column, "dp", 1)
    sides = [own_sides, swap(own_sides, "ctx", 1), far_sides, swap(far_sides, "ctx", 1)]
    (tile_self,) = onchip(
        tile_kernel,
        "bias_tile",
        [jax.ShapeDtypeStruct((heads, KEYS, 4 * KEYS), F32)],
        [after(bias_rows, queries)],
        table=False,
    )
    mixed_self, lse_self = attend(True, heads, meta, (bias_rows, tile_self), queries, sides)
    mixed_self_in, far_column, cross_pieces, own_cross = after(
        (mixed_self, far_column, tuple(cross_pieces), own_cross), lse_self
    )
    far_cross = swap(own_cross, "ctx", 2)
    cross_column = jnp.concatenate(cross_pieces, axis=0)
    far_cross_column = swap(cross_column, "dp", 1)
    plane = jnp.concatenate([column, far_column], axis=0)
    (self_output_all,) = lay_weights(plane, swap(plane, "ctx", 1), 1, "self_weight")
    mixed_self_all = gather_rows(mixed_self_in, "tensor")
    mixed_self_all, far_cross_column, far_cross = after(
        (mixed_self_all, far_cross_column, far_cross), mixed_self_in
    )
    cross_sides = [own_cross, swap(own_cross, "ctx", 1), far_cross, swap(far_cross, "ctx", 1)]
    after_self, normed_cross, cross_queries = onchip(
        functools.partial(cross_entry_kernel, slots),
        "cross_entry",
        [rows_full, rows_low, shape_of(tok_len, inner, LOW)],
        [meta, tokens, mixed_self_all, self_output_all, gain_two, cross_query],
        cost=2,
    )
    cross_plane = jnp.concatenate([cross_column, far_cross_column], axis=0)
    other_plane = swap(cross_plane, "ctx", 1)
    mixed_cross, lse_cross = attend(False, heads, meta, (), cross_queries, cross_sides)
    mixed_cross_in, other_plane = after((mixed_cross, other_plane), lse_cross)
    cross_output_all, cross_query_all = lay_weights(cross_plane, other_plane, 2, "cross_weights_all")
    fed = onchip(
        functools.partial(feed_kernel, slots),
        "feed",
        [part_full, rows_low, rows_low, rows_low, sum_row] + [part_low] * slots,
        [meta, after_self, gather_rows(mixed_cross_in, "tensor"), cross_output_all]
        + [gain_three, hidden_up, hidden_down, cotangent],
        [total_room, total_room],
        cost=4,
    )
    after_rows, normed_feed, active, grad_pre, gain_grad_feed = fed[:5]
    feed_blocks = trades(fed[5:], "tensor")
    feed_weights = onchip(
        functools.partial(feed_weights_kernel, split),
        "feed_weights",
        [shape_of(width, hidden_up.shape[1], LOW)] * 2,
        [meta, normed_feed, grad_pre, active, cotangent],
        cost=2,
    )
    layer_parts = onchip(
        functools.partial(layer_kernel, slots),
        "layer_parts",
        [part_low] * slots,
        [meta, active, hidden_down],
        [total_room],
        cost=1,
    )
    feed_blocks, feed_weights = after((tuple(feed_blocks), tuple(feed_weights)), *layer_parts)
    (branch_rows,) = onchip(
        functools.partial(feed_back_kernel, slots),
        "feed_back",
        [part_low],
        [meta, after_rows, cotangent, gain_three] + list(feed_blocks),
        cost=1,
    )
    branch_cross = gather_rows(branch_rows, "tensor")
    if split:
        feed_keep, feed_send = after(feed_weights, branch_rows)
        feed_add = send(feed_send, 1)
        branch_cross, layer_parts, feed_add = after((branch_cross, tuple(layer_parts), feed_add), branch_rows)
        by_line = add_halves(AT_DP, feed_keep, feed_add, "feed_line")
        line_recv = send(by_line[1], 4)
    else:
        branch_cross, layer_parts = after((branch_cross, tuple(layer_parts)), branch_rows)
    layer_blocks = trades(after(tuple(layer_parts), branch_cross), "tensor")

    back = attend_back(
        False, heads, meta, (), cross_queries, cross_output, mixed_cross, lse_cross, cross_sides, [branch_cross]
    )
    grad_cross_q, keep, near = back
    if split:
        grad_cross_q, keep, near, line_recv = after((grad_cross_q, keep, near, line_recv), *layer_blocks)
        by_far = add_halves(AT_FAR, by_line[0], line_recv, "feed_far")
        far_recv = send(by_far[1], 2)
    else:
        grad_cross_q, keep, near = after((grad_cross_q, keep, near), *layer_blocks)
    near = swap(near, "ctx", 1)
    queries_all = gather_rows(grad_cross_q, "tensor")
    if split:
        queries_all, near, far_recv = after((queries_all, near, far_recv), grad_cross_q)
        feed_far_sum = (by_far[0].astype(F32) + far_recv.astype(F32)).astype(LOW)
        far_recv = send(feed_far_sum, 2)
    else:
        queries_all, near = after((queries_all, near), grad_cross_q)
    far = swap(far_sum(keep, near, "cross_far"), "ctx", 2)
    cross_keep = keep
    after_self_rows, branch_self, gain_grad_cross = onchip(
        functools.partial(self_entry_kernel, slots),
        "self_entry",
        [part_full, rows_low, sum_row],
        [meta, after_self, queries_all, cross_query_all, gain_two, branch_cross],
        [total_room],
        cost=2,
    )
    (layer_rows,) = onchip(
        functools.partial(layer_sum_kernel, slots),
        "layer_sum",
        [part_low],
        [meta, after_rows] + layer_blocks,
    )
    layer_pieces = swaps(after(layer_rows, queries_all), "tensor")
    back = attend_back(
        True, heads, meta, (bias_rows, tile_self), queries, self_output, mixed_self, lse_self, sides, [branch_self]
    )
    grad_queries, keep, own_near, diagonals = back
    gate = list(layer_pieces[1:]) + ([far, far_recv] if split else [far])
    grad_queries, keep, own_near = after((grad_queries, keep, own_near), *gate)
    encoded_out = onchip(
        functools.partial(encoder_kernel, slots),
        "encoder_parts",
        [sides_low] + [part_low] * slots,
        [meta, cross_keep, near, after(far, grad_queries), cross_key, cross_value],
        [total_room],
        cost=1,
    )
    grad_cross_sides = encoded_out[0]
    encoder_blocks = trades(encoded_out[1:], "tensor")
    near = swap(after(own_near, encoded_out[0]), "ctx", 1)
    far = swap(far_sum(keep, near, "self_far"), "ctx", 2)
    if split:
        feed_half = join(AT_FAR, feed_far_sum, after(far_recv, grad_queries), "feed_half")
        feed_most = join(AT_DP, feed_half, send(feed_half, 4), "feed_most")
    cross_weights, layer_out = onchip(
        functools.partial(cross_weights_kernel, slots),
        "cross_weights",
        [shape_of(5 * inner, width, LOW), rows_low],
        [meta, grad_cross_q, normed_cross, grad_cross_sides, encoded, mixed_cross, branch_cross]
        + [mixed_self, branch_self]
        + layer_pieces,
        cost=2,
    )
    far, cross_weights = after((far, cross_weights), layer_out, *encoder_blocks, *([feed_most] if split else []))
    left = onchip(
        functools.partial(exit_kernel, slots),
        "self_exit",
        [sides_low] + [shape_of(share + 16, width, LOW)] * slots,
        [meta, keep, near, far, grad_queries, self_query, self_key, self_value, tokens]
        + [gain_grad_cross, gain_grad_feed],
        [total_room],
        cost=1,
    )
    grad_sides = left[0]
    left_blocks = trades(left[1:], "tensor")
    if split:
        feed_summed = [feed_most, send(after(feed_most, grad_sides), 1)]
    else:
        feed_summed = list(lax.psum(tuple(feed_weights), both))
    grad_up, grad_down = onchip(
        functools.partial(feed_finish_kernel, split),
        "feed_finish",
        [shape_of(width, hidden_up.shape[1], F32)] * 2,
        [meta] + feed_summed,
        cost=3,
    )
    left_blocks = after(tuple(left_blocks), grad_up)
    hidden_rows, encoder_rows, gains = onchip(
        functools.partial(last_rows_kernel, slots),
        "last_rows",
        [part_low, part_low, sum_row],
        [meta, after_self_rows, tokens, gain_one] + list(left_blocks) + encoder_blocks,
        cost=1,
    )
    weight_rows = -(-(8 * inner + 16) // 128) * 128
    hot = jnp.asarray(np.pad(span_onehot(), ((0, 0), (0, 128 - BUCKETS))), LOW)
    payload = onchip(
        functools.partial(payload_kernel, split),
        "last_weights",
        [shape_of(weight_rows // 2, width, LOW)] * 2 if split else [shape_of(weight_rows, width, LOW)],
        [meta, cross_weights, normed_self, grad_queries, grad_sides, diagonals, hot],
        [pltpu.VMEM((weight_rows, width), LOW)],
        cost=2,
    )
    if split:
        rows = weight_rows // 8
        quarters = onchip(
            quarter_kernel,
            "quarters",
            [shape_of(rows, width, LOW)] * 4,
            [meta, payload[0], send(payload[1], 1)],
            [pltpu.VMEM((4 * rows, width), F32)],
            cost=1,
        )
        (own,) = onchip(
            own_kernel,
            "own_eighth",
            [shape_of(rows + 16, width, LOW)],
            [meta, quarters[0]] + [send(quarters[flip], 2 * flip) for flip in (1, 2, 3)] + [gains],
            cost=1,
        )
        summed = [own] + [send(own, 2 * flip) for flip in (1, 2, 3)]
    else:
        summed = [lax.psum(payload[0], both)]
        gains = lax.psum(gains, both)
    grad_hidden = gather_rows(hidden_rows, "tensor")
    grad_hidden, gathered_encoder, *near_blocks = after((grad_hidden, encoder_rows) + tuple(summed if split else ()), hidden_rows)
    encoder_pieces = swaps(gathered_encoder, "tensor")
    if split:
        summed = list(near_blocks) + [send(block, 1) for block in near_blocks]
    weights = onchip(
        functools.partial(finish_kernel, split),
        "finish",
        [shape_of(inner, width, F32)] * 8 + [shape_of(16, width, F32)] + [sum_row] * split + [rows_low],
        [meta] + summed + [grad_hidden],
        [pltpu.VMEM((weight_rows, width), F32)],
        cost=3,
    )
    if split:
        gains = weights[9]
    (grad_encoder,) = onchip(
        functools.partial(gather_kernel, slots), "encoder_rows", [rows_low], [meta] + list(after(tuple(encoder_pieces), weights[0])), cost=1
    )
    return (
        layer_out[None],
        weights[-1][None],
        grad_encoder[None],
        gains[0],
        gains[1],
        gains[2],
        weights[5].T,
        weights[6].T,
        weights[7].T,
        weights[4],
        weights[8][:heads, :BUCKETS].T,
        weights[0].T,
        weights[1].T,
        weights[2].T,
        weights[3],
        grad_up,
        grad_down,
    )


def solution(mesh):
    rows = P("dp", "ctx", None)
    ids = P("dp", None)
    columns = P(None, "tensor")
    shards = P("tensor", None)
    placed = (
        (rows, rows, ids, ids, P(), P(), P())
        + (columns, columns, columns, shards, columns, columns, columns, columns, shards)
        + (columns, shards, rows)
    )
    given = (
        (rows, rows, rows, P(), P(), P())
        + (columns, columns, columns, shards, columns, columns, columns, columns, shards)
        + (columns, shards)
    )
    return jax.shard_map(body, mesh=mesh, in_specs=placed, out_specs=given, check_vma=False)
```
